32 devices in a mesh: rep: 4 (over y, x), fsdp: 8 (over z, core).
Axes of the slice: x: 2, y: 2, z: 4, core: 2. Of those that a mesh axis runs over, the one named last changes fastest.
Arguments:
- tokens: bfloat16 [8192, 2048], P(('rep', 'fsdp')), may hold values from -6 to 6
- layer_input: bfloat16 [8192, 256], P(('rep', 'fsdp')), may hold values from -6 to 6
- cotangent: bfloat16 [8192, 2048], P(('rep', 'fsdp')), may hold values from -6 to 6
- norm_gains: float32 [6, 2048], P(None, 'fsdp'), may hold values from 0.1 to 1.9
- qk_gains: float32 [2, 256], P(None, 'fsdp'), may hold values from 0.25 to 0.5
- w_qkv: float32 [2048, 3072], P('fsdp'), may hold values from -0.125 to 0.125
- w_out: float32 [2048, 2048], P('fsdp'), may hold values from -0.125 to 0.125
- laurel_left: float32 [2048, 64], P('fsdp'), may hold values from -0.125 to 0.125
- laurel_right: float32 [64, 2048], P('fsdp'), may hold values from -0.75 to 0.75
- w_gate_up: float32 [8192, 2, 2048], P('fsdp'), may hold values from -0.125 to 0.125
- w_down: float32 [8192, 2048], P('fsdp'), may hold values from -0.0625 to 0.0625
- pli_gate: float32 [2048, 256], P('fsdp'), may hold values from -0.125 to 0.125
- pli_proj: float32 [256, 2048], P('fsdp'), may hold values from -0.375 to 0.375
Outputs:
- mixed: bfloat16 [8192, 2048], P(('rep', 'fsdp'))
- grad_tokens: float32 [8192, 2048], P(('rep', 'fsdp'))
- grad_layer_input: float32 [8192, 256], P(('rep', 'fsdp'))
- grad_norm_gains: float32 [6, 2048], P(None, 'fsdp')
- grad_qk_gains: float32 [2, 256], P(None, 'fsdp')
- grad_w_qkv: float32 [2048, 3072], P('fsdp')
- grad_w_out: float32 [2048, 2048], P('fsdp')
- grad_laurel_left: float32 [2048, 64], P('fsdp')
- grad_laurel_right: float32 [64, 2048], P('fsdp')
- grad_w_gate_up: float32 [8192, 2, 2048], P('fsdp')
- grad_w_down: float32 [8192, 2048], P('fsdp')
- grad_pli_gate: float32 [2048, 256], P('fsdp')
- grad_pli_proj: float32 [256, 2048], P('fsdp')
The draws below stay inside these ranges and needn't reach their ends.
All inputs are finite; a program needn't handle non-finite values.
Results may differ from the reference program's by a relative error of at most 0.028.
Values may be sent and summed in bfloat16 or wider, within the bound.
No kernel may reach another device: no remote copies, remote signals or barrier semaphores. Data moves between devices by JAX's collectives and lax.ppermute only.
A program may use at most 512 MiB of HBM per device.

```python
import math
import jax
import jax.numpy as jnp
from jax import lax

D = 2048
H = 8
KVH = 2
HD = 256
FF = 8192
LR = 64
PD = 256
CONT_LEN = 256
PLEN = 1024
FAM = 2048
TOKENS = 8192
N_REP = 4


def block_scale(rng, shape, cuts, low, top_value):
    factor_of, own = 1.0, jax.random.fold_in(rng, 6)
    for axis_at, parts in cuts:
        heights = jnp.exp(jax.random.uniform(jax.random.fold_in(own, axis_at), (parts,), jnp.float32, low / len(cuts), top_value / len(cuts)))
        factor_of = factor_of * jnp.repeat(heights, shape[axis_at] // parts).reshape([-1 if axis == axis_at else 1 for axis in range(len(shape))])
    return factor_of


def scatter_about(stream_key, extent, width, most, cuts=(), held_as=jnp.bfloat16):
    array = jax.random.normal(stream_key, extent, jnp.float32) * width
    if len(cuts) > 0:
        array = block_scale(stream_key, extent, cuts, -0.22, 0.18) * array
    return jnp.clip(array, min=-most, max=most).astype(held_as)


def setup_inputs(seed: int = 0) -> dict:
    seeds = jax.random.split(jax.random.key(seed), 14)
    return {
        "tokens": scatter_about(seeds[0], (TOKENS, D), 1.0, 6.0, ((0, 32),)),
        "layer_input": scatter_about(seeds[1], (TOKENS, PD), 1.0, 6.0, ((0, 32),)),
        "cotangent": scatter_about(seeds[2], (TOKENS, D), 1.0, 6.0, ((0, 32),)),
        "norm_gains": jnp.clip(1.0 + 0.18 * jax.random.normal(seeds[3], (6, D), jnp.float32), 0.1, 1.9),
        "qk_gains": jnp.clip(jnp.exp(math.log(0.5) - 0.6931472 * jax.random.uniform(seeds[4], (2, HD), jnp.float32) ** block_scale(seeds[4], (2, HD), ((1, 8),), -0.2, 0.2)), 0.25, 0.5),
        "w_qkv": scatter_about(seeds[5], (D, (H + 2 * KVH) * HD), D ** -0.5, 0.125, ((0, 8),), jnp.float32),
        "w_out": scatter_about(seeds[6], (H * HD, D), (H * HD) ** -0.5, 0.125, ((0, 8),), jnp.float32),
        "laurel_left": scatter_about(seeds[7], (D, LR), D ** -0.5, 0.125, ((0, 8),), jnp.float32),
        "laurel_right": scatter_about(seeds[8], (LR, D), LR ** -0.5, 0.75, ((0, 8),), jnp.float32),
        "w_gate_up": scatter_about(seeds[9], (FF, 2, D), D ** -0.5, 0.125, ((0, 8),), jnp.float32),
        "w_down": scatter_about(seeds[10], (FF, D), FF ** -0.5, 0.0625, ((0, 8),), jnp.float32),
        "pli_gate": scatter_about(seeds[11], (D, PD), D ** -0.5, 0.125, ((0, 8),), jnp.float32),
        "pli_proj": scatter_about(seeds[12], (PD, D), PD ** -0.5, 0.375, ((0, 8),), jnp.float32),
    }


@jax.custom_vjp
def low(v):
    return lax.optimization_barrier(v.astype(jnp.bfloat16)).astype(jnp.float32)

@jax.custom_vjp
def low_back(v):
    return v

def low_keep(v):
    return (low(v), None)

def low_pass(kept, grad):
    return (grad,)

def back_keep(v):
    return (v, None)

def back_low(kept, grad):
    return (low(grad),)
low.defvjp(low_keep, low_pass)
low_back.defvjp(back_keep, back_low)
EPSILON = 1e-06
THETA_BASE = 1000000.0
HALF_ROOT = 0.7071067811865476
NEG_FILL = -1e+30

def matmul_hi(left_mat, right_mat):
    return jnp.dot(left_mat, right_mat, precision=lax.Precision.HIGHEST, preferred_element_type=jnp.float32)

def rms_norm(tensor):
    return tensor * lax.rsqrt(lax.optimization_barrier(jnp.mean(tensor * tensor, axis=-1, keepdims=True)) + EPSILON)

def rotary(tensor, places):
    halfway = tensor.shape[-1] // 2
    frequency = THETA_BASE ** (-(jnp.arange(halfway, dtype=jnp.float32) * 2.0 / tensor.shape[-1]))
    angles = places.astype(jnp.float32)[:, None, None] * frequency
    cosine = jnp.cos(angles)
    sine_part = jnp.sin(angles)
    first_half = tensor[..., :halfway]
    second_half = tensor[..., halfway:]
    return jnp.concatenate([first_half * cosine - second_half * sine_part, second_half * cosine + first_half * sine_part], axis=-1)

def family_layout():
    family_rows = jnp.arange(FAM, dtype=jnp.int32)
    places = jnp.where(family_rows < PLEN, family_rows, PLEN + (family_rows - PLEN) % CONT_LEN)
    segment = jnp.where(family_rows < PLEN, -1, (family_rows - PLEN) // CONT_LEN)
    return (places, segment)

def attention(queries, keys_rot, values_norm, segment):
    block_rows = min(FAM, 512)
    blocks = FAM // block_rows
    key_index = jnp.arange(FAM, dtype=jnp.int32)

    def one_block(block_item):
        query_block, first_row = block_item
        query_index = first_row + jnp.arange(block_rows, dtype=jnp.int32)
        query_seg = lax.dynamic_slice_in_dim(segment, first_row, block_rows)
        scores = low_back(jnp.einsum('qkgd,skd->qkgs', query_block, keys_rot, precision=lax.Precision.HIGHEST))
        allowed = jnp.logical_and(key_index[None, :] <= query_index[:, None], jnp.logical_or(key_index[None, :] < PLEN, segment[None, :] == query_seg[:, None]))
        scores = jnp.where(allowed[:, None, None, :], scores, NEG_FILL)
        shares = jax.nn.softmax(scores, axis=-1)
        return jnp.einsum('qkgs,skd->qkgd', low(shares), values_norm, precision=lax.Precision.HIGHEST)
    starts = jnp.arange(blocks, dtype=jnp.int32) * block_rows
    shaped = queries.reshape(blocks, block_rows, KVH, H // KVH, HD)
    return lax.map(jax.checkpoint(one_block), (shaped, starts)).reshape(FAM, H * HD)

def family(family_item, weights):
    inputs, extra_input = family_item
    norm_rows, qk_gain, qkv_weight, out_weight, left_weight, right_weight, gu_weight, down_weight, gate_weight, proj_weight = weights
    places, segment = family_layout()
    normed = rms_norm(inputs) * norm_rows[0]
    normed_bf = low(normed)
    projected = low_back(matmul_hi(normed_bf, qkv_weight))
    query_part = projected[:, :H * HD].reshape(FAM, H, HD)
    key_part = projected[:, H * HD:(H + KVH) * HD].reshape(FAM, KVH, HD)
    value_part = projected[:, (H + KVH) * HD:].reshape(FAM, KVH, HD)
    queries = low(rotary(rms_norm(query_part) * qk_gain[0], places)).reshape(FAM, KVH, H // KVH, HD)
    keys_rot = low(rotary(rms_norm(key_part) * qk_gain[1], places))
    values_norm = low(rms_norm(value_part))
    attended = attention(queries, keys_rot, values_norm, segment)
    attended_bf = low(low_back(attended))
    attn_proj = low_back(matmul_hi(attended_bf, out_weight))
    laurel_mid = low(low_back(matmul_hi(normed_bf, left_weight)))
    laurel_out = low_back(matmul_hi(laurel_mid, right_weight))
    stream = (inputs + rms_norm(attn_proj) * norm_rows[1] + normed + rms_norm(laurel_out) * norm_rows[2]) * HALF_ROOT
    ffn_in = low(rms_norm(stream) * norm_rows[3])
    gate_up = low_back(jnp.einsum('td,fkd->tkf', ffn_in, gu_weight, precision=lax.Precision.HIGHEST))
    hidden = low(jax.nn.gelu(gate_up[:, 0], approximate=True) * gate_up[:, 1])
    ffn_out = low_back(matmul_hi(hidden, down_weight))
    after_ffn = stream + rms_norm(ffn_out) * norm_rows[4]
    pli_pre = low_back(matmul_hi(low(after_ffn), gate_weight))
    pli_mid = low(jax.nn.gelu(pli_pre, approximate=True) * extra_input)
    pli_out = low_back(matmul_hi(pli_mid, proj_weight))
    return after_ffn + rms_norm(pli_out) * norm_rows[5]

def reference(tokens, layer_input, cotangent, norm_gains, qk_gains, w_qkv, w_out, laurel_left, laurel_right, w_gate_up, w_down, pli_gate, pli_proj):
    weights = (norm_gains, qk_gains, w_qkv, w_out, laurel_left, laurel_right, w_gate_up, w_down, pli_gate, pli_proj)
    weights = tuple((weight.astype(jnp.float32) for weight in weights))
    inputs = tokens.astype(jnp.float32).reshape(N_REP, FAM, D)
    extra_input = layer_input.astype(jnp.float32).reshape(N_REP, FAM, PD)
    step_fn = jax.checkpoint(family)

    def whole_layer(inputs, extra_input, weights):
        rounded = tuple((low(weight) for weight in weights))
        return lax.map(lambda family_item: step_fn(family_item, rounded), (inputs, extra_input))
    output, pull_back = jax.vjp(whole_layer, inputs, extra_input, weights)
    grad_inputs, grad_extra, grads = pull_back(cotangent.astype(jnp.float32).reshape(N_REP, FAM, D))
    return (output.reshape(TOKENS, D).astype(jnp.bfloat16), grad_inputs.reshape(TOKENS, D), grad_extra.reshape(TOKENS, PD), grads[0], grads[1], grads[2], grads[3], grads[4], grads[5], grads[6], grads[7], grads[8], grads[9])
```

```python
import jax
import jax.numpy as jnp
from jax import lax
from jax.sharding import PartitionSpec as P

H = 8
KVH = 2
HD = 256
CONT_LEN = 256
PROMPT_DEVS = 4


EPSILON = 1e-06
THETA_BASE = 1000000.0
HALF_ROOT = 0.7071067811865476
NEG_FILL = -1e30


def rms_norm(tensor):
    return tensor * lax.rsqrt(jnp.mean(tensor * tensor, axis=-1, keepdims=True) + EPSILON)


def rotary(tensor, places):
    halfway = tensor.shape[-1] // 2
    frequency = THETA_BASE ** (-(jnp.arange(halfway, dtype=jnp.float32) * 2.0 / tensor.shape[-1]))
    angles = places.astype(jnp.float32)[:, None, None] * frequency
    cosine = jnp.cos(angles)
    sine_part = jnp.sin(angles)
    first_half = tensor[..., :halfway]
    second_half = tensor[..., halfway:]
    return jnp.concatenate(
        [
            first_half * cosine - second_half * sine_part,
            second_half * cosine + first_half * sine_part,
        ],
        axis=-1,
    )


def gelu_mix(gate_up):
    return jax.nn.gelu(gate_up[:, 0], approximate=True) * gate_up[:, 1]


def outer_sum(left_mat, right_mat):
    return lax.dot_general(
        left_mat, right_mat, (((0,), (0,)), ((), ())), preferred_element_type=jnp.float32
    )


def back_dot(gradient, weight):
    return lax.dot_general(
        gradient, weight, (((1,), (1,)), ((), ())), preferred_element_type=jnp.float32
    )


def allowed_keys(first_row, block_rows, key_count, device, rows_dev):
    prompt_len = key_count - rows_dev
    query_local = first_row + jnp.arange(block_rows, dtype=jnp.int32)
    key_index = jnp.arange(key_count, dtype=jnp.int32)
    in_prompt = device < PROMPT_DEVS
    query_global = device * rows_dev + query_local
    own_index = key_index - prompt_len
    prompt_ok = jnp.logical_or(
        jnp.logical_not(in_prompt), key_index[None, :] <= query_global[:, None]
    )
    same_piece = own_index[None, :] // CONT_LEN == query_local[:, None] // CONT_LEN
    own_ok = jnp.logical_and(
        jnp.logical_not(in_prompt),
        jnp.logical_and(same_piece, own_index[None, :] <= query_local[:, None]),
    )
    return jnp.where(key_index[None, :] < prompt_len, prompt_ok, own_ok)


def block_layout(queries):
    rows_dev = queries.shape[0]
    block_rows = min(rows_dev, 512)
    blocks = rows_dev // block_rows
    starts = jnp.arange(blocks, dtype=jnp.int32) * block_rows
    return (block_rows, blocks, starts)


def masked_scores(query_block, keys_all, first_row, block_rows, device, rows_dev):
    scores = jnp.einsum("qkgd,skd->qkgs", query_block, keys_all, preferred_element_type=jnp.float32)
    allowed = allowed_keys(first_row, block_rows, keys_all.shape[0], device, rows_dev)[
        :, None, None, :
    ]
    return jnp.where(allowed, scores, NEG_FILL)


def attention_forward(queries, keys_all, values_all, device):
    rows_dev = queries.shape[0]
    block_rows, blocks, starts = block_layout(queries)

    def one_block(block_item):
        query_block, first_row = block_item
        scores = masked_scores(query_block, keys_all, first_row, block_rows, device, rows_dev)
        row_peak = jnp.max(scores, axis=-1, keepdims=True)
        row_total = jnp.sum(jnp.exp(scores - row_peak), axis=-1, keepdims=True)
        log_total = row_peak + jnp.log(row_total)
        shares_bf = jnp.exp(scores - log_total).astype(jnp.bfloat16)
        attended = jnp.einsum(
            "qkgs,skd->qkgd", shares_bf, values_all, preferred_element_type=jnp.float32
        )
        return (attended, log_total[..., 0])

    shaped = queries.reshape((blocks, block_rows) + queries.shape[1:])
    attended, log_totals = lax.map(one_block, (shaped, starts))
    return (attended.reshape(queries.shape), log_totals.reshape(queries.shape[:3]))


def attention_backward(queries, keys_all, values_all, grad_attended, log_totals, device):
    rows_dev = queries.shape[0]
    block_rows, blocks, starts = block_layout(queries)

    def one_block(carried, block_item):
        key_grad, value_grad = carried
        query_block, grad_block, total_block, first_row = block_item
        scores = masked_scores(query_block, keys_all, first_row, block_rows, device, rows_dev)
        shares = jnp.exp(scores - total_block[..., None])
        grad_shares = jnp.einsum(
            "qkgd,skd->qkgs", grad_block, values_all, preferred_element_type=jnp.float32
        )
        inner_sum = jnp.sum(shares * grad_shares, axis=-1, keepdims=True)
        grad_scores = (shares * (grad_shares - inner_sum)).astype(jnp.bfloat16)
        grad_query = jnp.einsum(
            "qkgs,skd->qkgd", grad_scores, keys_all, preferred_element_type=jnp.float32
        )
        key_grad = key_grad + jnp.einsum(
            "qkgs,qkgd->skd", grad_scores, query_block, preferred_element_type=jnp.float32
        )
        value_grad = value_grad + jnp.einsum(
            "qkgs,qkgd->skd",
            shares.astype(jnp.bfloat16),
            grad_block,
            preferred_element_type=jnp.float32,
        )
        return ((key_grad, value_grad), grad_query)

    shaped_query = queries.reshape((blocks, block_rows) + queries.shape[1:])
    shaped_grad = grad_attended.reshape((blocks, block_rows) + queries.shape[1:])
    shaped_total = log_totals.reshape((blocks, block_rows) + queries.shape[1:3])
    zero_grad = jnp.zeros(keys_all.shape, jnp.float32)
    (key_grad, value_grad), grad_query = lax.scan(
        one_block, (zero_grad, zero_grad), (shaped_query, shaped_grad, shaped_total, starts)
    )
    return (grad_query.reshape(queries.shape), key_grad, value_grad)


def core_swap(array, count):
    return lax.ppermute(array, "fsdp", [(i, i ^ 1) for i in range(count)])


def chain_shift(array, count, step, senders):
    chips = count // 2
    pairs = [
        (2 * chip + core, 2 * (chip + step) + core)
        for chip in range(chips)
        if 0 <= chip + step < chips and senders(chip)
        for core in range(2)
    ]
    return lax.ppermute(array, "fsdp", pairs)


def chain_gather(array, count, chip):
    chips = count // 2
    right, left = [array], [array]
    for hop in range(1, chips):
        right.append(chain_shift(right[-1], count, 1, lambda i, hop=hop: i >= hop - 1))
        left.append(chain_shift(left[-1], count, -1, lambda i, hop=hop: i <= chips - hop))
    lower = chip < chips // 2
    reach = jnp.maximum(chip, chips - 1 - chip)
    slots = [array]
    for j in range(1, chips):
        far = jnp.where(lower, left[j], right[j])
        if j > chips // 2:
            near = jnp.where(lower, right[chips - j], left[chips - j])
            far = jnp.where(j <= reach, far, near)
        slots.append(far)
    return slots


def chain_reduce(slots, count, chip):
    chips = count // 2
    lower = chip < chips // 2
    going_right, going_left = None, None
    for distance in range(chips - 1, 0, -1):
        near, far = slots[distance], slots[chips - distance]
        up = near if distance * 2 == chips else jnp.where(lower, near, far)
        down = near if distance * 2 == chips else jnp.where(lower, far, near)
        if going_right is not None:
            up = up + going_right.astype(jnp.float32)
            down = down + going_left.astype(jnp.float32)
        going_right = chain_shift(
            up.astype(jnp.bfloat16), count, 1, lambda i, d=distance: i + d <= chips - 1
        )
        going_left = chain_shift(
            down.astype(jnp.bfloat16), count, -1, lambda i, d=distance: i - d >= 0
        )
    return slots[0] + going_right.astype(jnp.float32) + going_left.astype(jnp.float32)


def body(
    tokens,
    layer_input,
    cotangent,
    norm_gains,
    qk_gains,
    w_qkv,
    w_out,
    laurel_left,
    laurel_right,
    w_gate_up,
    w_down,
    pli_gate,
    pli_proj,
):
    count = lax.axis_size("fsdp")
    device = lax.axis_index("fsdp")
    chip = device // 2
    rows_dev = tokens.shape[0]
    prompt_len = PROMPT_DEVS * rows_dev
    groups = H // KVH
    bf = jnp.bfloat16

    small = jnp.concatenate(
        [
            norm_gains.astype(bf).reshape(-1),
            qk_gains.astype(bf).reshape(-1),
            laurel_left.astype(bf).reshape(-1),
            laurel_right.astype(bf).reshape(-1),
            pli_gate.astype(bf).reshape(-1),
            pli_proj.astype(bf).reshape(-1),
        ]
    )
    small_all = lax.all_gather(small, "fsdp", axis=0, tiled=False)
    qkv_all = lax.all_gather(w_qkv.astype(bf), "fsdp", axis=0, tiled=True)
    out_all = lax.all_gather(w_out.astype(bf), "fsdp", axis=0, tiled=True)
    sizes = [a.size for a in (norm_gains, qk_gains, laurel_left, laurel_right, pli_gate, pli_proj)]
    starts = [sum(sizes[:i]) for i in range(len(sizes))]
    parts = [small_all[:, s : s + z] for s, z in zip(starts, sizes)]
    gains = jnp.moveaxis(parts[0].reshape((count,) + norm_gains.shape), 0, 1).reshape(
        norm_gains.shape[0], -1
    ).astype(jnp.float32)
    qk_gain = jnp.moveaxis(parts[1].reshape((count,) + qk_gains.shape), 0, 1).reshape(
        qk_gains.shape[0], -1
    ).astype(jnp.float32)
    left_all = parts[2].reshape(-1, laurel_left.shape[1])
    right_all = parts[3].reshape(-1, laurel_right.shape[1])
    pgate_all = parts[4].reshape(-1, pli_gate.shape[1])
    pproj_all = parts[5].reshape(-1, pli_proj.shape[1])

    w_gate = w_gate_up[:, 0].astype(bf)
    w_up = w_gate_up[:, 1].astype(bf)
    w_down_bf = w_down.astype(bf)

    inputs = tokens.astype(jnp.float32)
    extra_input = layer_input.astype(jnp.float32)

    def input_norm(tensor, gain_rows):
        return rms_norm(tensor) * gain_rows[0]

    normed, input_pull = jax.vjp(input_norm, inputs, gains)
    normed_bf = normed.astype(bf)
    projected = jnp.dot(normed_bf, qkv_all, preferred_element_type=jnp.float32)
    local_rows = jnp.arange(rows_dev, dtype=jnp.int32)
    places = jnp.where(
        device < PROMPT_DEVS, device * rows_dev + local_rows, prompt_len + local_rows % CONT_LEN
    )

    def head_prep(projected, gain_pair):
        query_part = projected[:, : H * HD].reshape(rows_dev, H, HD)
        key_part = projected[:, H * HD : (H + KVH) * HD].reshape(rows_dev, KVH, HD)
        value_part = projected[:, (H + KVH) * HD :].reshape(rows_dev, KVH, HD)
        queries = rotary(rms_norm(query_part) * gain_pair[0], places).reshape(
            rows_dev, KVH, groups, HD
        )
        return (queries, rotary(rms_norm(key_part) * gain_pair[1], places), rms_norm(value_part))

    (queries, keys_own, values_own), prep_pull = jax.vjp(head_prep, projected, qk_gain)
    queries_bf = queries.astype(bf)
    keys_bf = keys_own.astype(bf)
    values_bf = values_own.astype(bf)
    kv_own = jnp.concatenate(
        [keys_bf.reshape(rows_dev, KVH * HD), values_bf.reshape(rows_dev, KVH * HD)], axis=1
    )
    kv_all = lax.all_gather(kv_own, "fsdp", axis=0, tiled=True)
    kv_seen = jnp.concatenate([kv_all[:prompt_len], kv_own], axis=0)
    keys_all = kv_seen[:, : KVH * HD].reshape(-1, KVH, HD)
    values_all = kv_seen[:, KVH * HD :].reshape(-1, KVH, HD)
    attended, log_totals = attention_forward(queries_bf, keys_all, values_all, device)
    attended_bf = attended.reshape(rows_dev, H * HD).astype(bf)
    attn_proj = jnp.dot(attended_bf, out_all, preferred_element_type=jnp.float32)
    laurel_mid = jnp.dot(normed_bf, left_all, preferred_element_type=jnp.float32).astype(bf)
    laurel_out = jnp.dot(laurel_mid, right_all, preferred_element_type=jnp.float32)

    def middle(inputs, normed, attn_proj, laurel_out, gain_rows):
        first_sum = inputs + rms_norm(attn_proj) * gain_rows[1]
        laurel_sum = normed + rms_norm(laurel_out) * gain_rows[2]
        stream = (first_sum + laurel_sum) * HALF_ROOT
        return (stream, rms_norm(stream) * gain_rows[3])

    (stream, ffn_in), middle_pull = jax.vjp(middle, inputs, normed, attn_proj, laurel_out, gains)

    def both_cores(slots):
        return [jnp.concatenate([slot, core_swap(slot, count)], axis=0) for slot in slots]

    def own_rows(partials):
        kept = []
        for partial in partials:
            other = core_swap(partial[rows_dev:].astype(bf), count)
            kept.append(partial[:rows_dev] + other.astype(jnp.float32))
        return kept

    def gelu_pair(gate, up):
        return jax.nn.gelu(gate, approximate=True) * up

    blocks_in = both_cores(chain_gather(ffn_in.astype(bf), count, chip))
    hiddens, hidden_pulls, partials = [], [], []
    for block in blocks_in:
        gate = back_dot(block, w_gate)
        up = back_dot(block, w_up)
        hidden, pull = jax.vjp(gelu_pair, gate, up)
        hidden = hidden.astype(bf)
        hiddens.append(hidden)
        hidden_pulls.append(pull)
        partials.append(jnp.dot(hidden, w_down_bf, preferred_element_type=jnp.float32))
    ffn_out = chain_reduce(own_rows(partials), count, chip)

    def tail_norm(stream, ffn_out, gain_rows):
        return stream + rms_norm(ffn_out) * gain_rows[4]

    after_ffn, tail_pull = jax.vjp(tail_norm, stream, ffn_out, gains)
    after_bf = after_ffn.astype(bf)
    pli_pre = jnp.dot(after_bf, pgate_all, preferred_element_type=jnp.float32)

    def pli_mix(pli_pre, extra_input):
        return jax.nn.gelu(pli_pre, approximate=True) * extra_input

    pli_mid, pli_pull = jax.vjp(pli_mix, pli_pre, extra_input)
    pli_mid_bf = pli_mid.astype(bf)
    pli_out = jnp.dot(pli_mid_bf, pproj_all, preferred_element_type=jnp.float32)

    def final_norm(after_ffn, pli_out, gain_rows):
        return after_ffn + rms_norm(pli_out) * gain_rows[5]

    result, final_pull = jax.vjp(final_norm, after_ffn, pli_out, gains)
    grad_after, grad_pli_out, gain_final = final_pull(cotangent.astype(jnp.float32))
    grad_pli_out_bf = grad_pli_out.astype(bf)
    grad_pproj = outer_sum(pli_mid_bf, grad_pli_out_bf)
    grad_pli_mid = back_dot(grad_pli_out_bf, pproj_all)
    grad_pli_pre, grad_extra = pli_pull(grad_pli_mid)
    grad_pli_pre_bf = grad_pli_pre.astype(bf)
    grad_pgate = outer_sum(after_bf, grad_pli_pre_bf)
    grad_after = grad_after + back_dot(grad_pli_pre_bf, pgate_all)
    grad_stream, grad_ffn_out, gain_tail = tail_pull(grad_after)

    blocks_grad = both_cores(chain_gather(grad_ffn_out.astype(bf), count, chip))
    gates, ups, partials = [], [], []
    for block, pull in zip(blocks_grad, hidden_pulls):
        gate, up = pull(back_dot(block, w_down_bf))
        gate, up = gate.astype(bf), up.astype(bf)
        gates.append(gate)
        ups.append(up)
        partials.append(
            jnp.dot(gate, w_gate, preferred_element_type=jnp.float32)
            + jnp.dot(up, w_up, preferred_element_type=jnp.float32)
        )
    grad_ffn_in = chain_reduce(own_rows(partials), count, chip)
    rows_in = jnp.concatenate(blocks_in, axis=0)
    rows_grad = jnp.concatenate(blocks_grad, axis=0)
    grad_down_w = outer_sum(jnp.concatenate(hiddens, axis=0), rows_grad).astype(bf)
    grad_gate_w = outer_sum(jnp.concatenate(gates, axis=0), rows_in).astype(bf)
    grad_up_w = outer_sum(jnp.concatenate(ups, axis=0), rows_in).astype(bf)
    down_sum = lax.psum(grad_down_w, "rep")
    gate_sum = lax.psum(grad_gate_w, "rep")
    up_sum = lax.psum(grad_up_w, "rep")

    grad_inputs, grad_normed, grad_attn_proj, grad_laurel_out, gain_middle = middle_pull(
        (grad_stream, grad_ffn_in)
    )
    grad_attn_bf = grad_attn_proj.astype(bf)
    grad_out_w = outer_sum(attended_bf, grad_attn_bf)
    grad_attended = (
        back_dot(grad_attn_bf, out_all).astype(bf).reshape(rows_dev, KVH, groups, HD)
    )
    grad_laurel_bf = grad_laurel_out.astype(bf)
    grad_right_w = outer_sum(laurel_mid, grad_laurel_bf)
    grad_mid_bf = back_dot(grad_laurel_bf, right_all).astype(bf)
    grad_left_w = outer_sum(normed_bf, grad_mid_bf)
    grad_normed = grad_normed + back_dot(grad_mid_bf, left_all)
    grad_queries, key_grad, value_grad = attention_backward(
        queries_bf, keys_all, values_all, grad_attended, log_totals, device
    )
    kv_grad = jnp.concatenate(
        [key_grad.reshape(-1, KVH * HD), value_grad.reshape(-1, KVH * HD)], axis=1
    )
    prompt_kv = lax.psum(kv_grad[:prompt_len].astype(bf), "fsdp")
    owner_start = jnp.minimum(device, PROMPT_DEVS - 1) * rows_dev
    kv_sum = jnp.where(
        device < PROMPT_DEVS,
        lax.dynamic_slice_in_dim(prompt_kv, owner_start, rows_dev, 0).astype(jnp.float32),
        kv_grad[prompt_len:],
    )
    key_sum = kv_sum[:, : KVH * HD].reshape(rows_dev, KVH, HD)
    value_sum = kv_sum[:, KVH * HD :].reshape(rows_dev, KVH, HD)
    grad_projected, grad_qk_gain = prep_pull((grad_queries, key_sum, value_sum))
    grad_proj_bf = grad_projected.astype(bf)
    grad_qkv_w = outer_sum(normed_bf, grad_proj_bf)
    grad_normed = grad_normed + back_dot(grad_proj_bf, qkv_all)
    grad_first, gain_input = input_pull(grad_normed)
    grad_tokens = grad_inputs + grad_first
    gain_total = gain_final + gain_tail + gain_middle + gain_input

    def shard_rows(array):
        return array.astype(bf).reshape(count, -1)

    def shard_columns(array):
        return jnp.moveaxis(array.astype(bf).reshape(array.shape[0], count, -1), 1, 0).reshape(
            count, -1
        )

    small_grad = jnp.concatenate(
        [
            shard_columns(gain_total),
            shard_columns(grad_qk_gain),
            shard_rows(grad_left_w),
            shard_rows(grad_right_w),
            shard_rows(grad_pgate),
            shard_rows(grad_pproj),
        ],
        axis=1,
    )
    out_sum = lax.psum(
        lax.psum_scatter(grad_out_w.astype(bf), "fsdp", scatter_dimension=0, tiled=True), "rep"
    )
    small_sum = lax.psum(
        lax.psum_scatter(small_grad, "fsdp", scatter_dimension=0, tiled=False), "rep"
    ).astype(jnp.float32)
    qkv_sum = lax.psum(
        lax.psum_scatter(grad_qkv_w.astype(bf), "fsdp", scatter_dimension=0, tiled=True), "rep"
    )
    pieces = [
        small_sum[s : s + z].reshape(a.shape)
        for s, z, a in zip(
            starts, sizes, (norm_gains, qk_gains, laurel_left, laurel_right, pli_gate, pli_proj)
        )
    ]
    return (
        result.astype(bf),
        grad_tokens,
        grad_extra,
        pieces[0],
        pieces[1],
        qkv_sum.astype(jnp.float32),
        out_sum.astype(jnp.float32),
        pieces[2],
        pieces[3],
        jnp.stack([gate_sum, up_sum], axis=1).astype(jnp.float32),
        down_sum.astype(jnp.float32),
        pieces[4],
        pieces[5],
    )


def solution(mesh):
    placed = (
        P(("rep", "fsdp"), None),
        P(("rep", "fsdp"), None),
        P(("rep", "fsdp"), None),
        P(None, "fsdp"),
        P(None, "fsdp"),
        P("fsdp", None),
        P("fsdp", None),
        P("fsdp", None),
        P("fsdp", None),
        P("fsdp", None, None),
        P("fsdp", None),
        P("fsdp", None),
        P("fsdp", None),
    )
    return jax.shard_map(
        body,
        mesh=mesh,
        in_specs=placed,
        out_specs=(
            P(("rep", "fsdp"), None),
            P(("rep", "fsdp"), None),
            P(("rep", "fsdp"), None),
            P(None, "fsdp"),
            P(None, "fsdp"),
            P("fsdp", None),
            P("fsdp", None),
            P("fsdp", None),
            P("fsdp", None),
            P("fsdp", None, None),
            P("fsdp", None),
            P("fsdp", None),
            P("fsdp", None),
        ),
        check_vma=False,
    )
```

```python
import jax
import jax.numpy as jnp
from jax import lax
from jax.experimental import pallas as pl
from jax.experimental.pallas import tpu as pltpu
from jax.sharding import PartitionSpec as P

H = 8
KVH = 2
HD = 256
CONT_LEN = 256
PROMPT_DEVS = 4
CHUNKS = 1

EPSILON = 1e-06
THETA_BASE = 1000000.0
HALF_ROOT = 0.7071067811865476
NEG_FILL = -1e30
GELU_SCALE = 0.7978845608028654
GELU_CUBIC = 0.044715
BF = jnp.bfloat16
F32 = jnp.float32


def rms_norm(tensor):
    return tensor * lax.rsqrt(jnp.mean(tensor * tensor, axis=-1, keepdims=True) + EPSILON)


def dot(left_mat, right_mat):
    return jnp.dot(left_mat, right_mat, preferred_element_type=F32)


def outer_sum(left_mat, right_mat):
    return lax.dot_general(
        left_mat, right_mat, (((0,), (0,)), ((), ())), preferred_element_type=F32
    )


def back_dot(gradient, weight):
    return lax.dot_general(
        gradient, weight, (((1,), (1,)), ((), ())), preferred_element_type=F32
    )


def turn(tensor, cosine, sine, back=False):
    half = tensor.shape[-1] // 2
    first, second = tensor[:, :half], tensor[:, half:]
    if back:
        return jnp.concatenate(
            [first * cosine + second * sine, second * cosine - first * sine], axis=-1
        )
    return jnp.concatenate(
        [first * cosine - second * sine, second * cosine + first * sine], axis=-1
    )


def head_norm(tensor):
    inverse = lax.rsqrt(jnp.mean(tensor * tensor, axis=-1, keepdims=True) + EPSILON)
    return tensor * inverse, inverse


def head_norm_back(normed, inverse, gradient):
    return inverse * (gradient - normed * jnp.mean(gradient * normed, axis=-1, keepdims=True))


def head_shares(queries, keys, device):
    rows, key_count = queries.shape[0], keys.shape[0]
    prompt_len = key_count - rows
    scores = back_dot(queries, keys)
    local = lax.broadcasted_iota(jnp.int32, scores.shape, 0)
    index = lax.broadcasted_iota(jnp.int32, scores.shape, 1)
    own = index - prompt_len
    in_prompt = device < PROMPT_DEVS
    last_seen = jnp.where(in_prompt, device * rows, prompt_len) + local
    allowed = index <= last_seen
    if rows > CONT_LEN:
        piece = jnp.logical_or(own < 0, own // CONT_LEN == local // CONT_LEN)
        allowed = jnp.logical_and(allowed, piece)
    scores = jnp.where(allowed, scores, NEG_FILL)
    grown = jnp.exp(scores - jnp.max(scores, axis=-1, keepdims=True))
    return grown / jnp.sum(grown, axis=-1, keepdims=True)


def head_specs(rows, key_count):
    head = pl.BlockSpec((rows, HD), lambda h: (0, h))
    half = pl.BlockSpec((rows, HD // 2), lambda h: (0, 0))
    gain = pl.BlockSpec((2, HD), lambda h: (0, 0))
    keys = pl.BlockSpec((key_count, HD), lambda h: (0, h // (H // KVH)))
    values = pl.BlockSpec((key_count, HD), lambda h: (0, KVH + h // (H // KVH)))
    return head, half, gain, keys, values


def attend(projected, cosine, sine, gains, kv_seen, device):
    rows, key_count = projected.shape[0], kv_seen.shape[0]
    head, half, gain, keys, values = head_specs(rows, key_count)

    def kernel(at_ref, x_ref, c_ref, s_ref, g_ref, k_ref, v_ref, q_ref, o_ref):
        normed, _ = head_norm(x_ref[...])
        queries = turn(normed * g_ref[0:1, :], c_ref[...], s_ref[...]).astype(BF)
        q_ref[...] = queries
        shares = head_shares(queries, k_ref[...], at_ref[0])
        o_ref[...] = dot(shares.astype(BF), v_ref[...]).astype(BF)

    return pl.pallas_call(
        kernel,
        grid=(H,),
        in_specs=[pl.BlockSpec(memory_space=pltpu.SMEM), head, half, half, gain, keys, values],
        out_specs=[head, head],
        out_shape=[jax.ShapeDtypeStruct((rows, H * HD), BF)] * 2,
        cost_estimate=pl.CostEstimate(
            flops=4 * rows * H * HD * key_count,
            bytes_accessed=rows * H * HD * 8 + key_count * KVH * HD * 4,
            transcendentals=rows * H * key_count,
        ),
        name="attend",
    )(device.reshape(1), projected, cosine, sine, gains, kv_seen, kv_seen)


def attend_back(projected, queries, cosine, sine, gains, kv_seen, gradient, device):
    rows, key_count = projected.shape[0], kv_seen.shape[0]
    groups = H // KVH
    head, half, gain, keys, values = head_specs(rows, key_count)

    def kernel(
        at_ref, x_ref, q_ref, c_ref, s_ref, g_ref, k_ref, v_ref, do_ref,
        dx_ref, dk_ref, dv_ref, dg_ref,
    ):
        queries, grad = q_ref[...], do_ref[...]
        shares = head_shares(queries, k_ref[...], at_ref[0])
        grad_shares = back_dot(grad, v_ref[...])
        inner = jnp.sum(shares * grad_shares, axis=-1, keepdims=True)
        grad_scores = (shares * (grad_shares - inner)).astype(BF)
        key_grad = outer_sum(grad_scores, queries)
        value_grad = outer_sum(shares.astype(BF), grad)
        first = lax.rem(pl.program_id(0), groups) == 0

        @pl.when(first)
        def _():
            dk_ref[...] = key_grad
            dv_ref[...] = value_grad

        @pl.when(jnp.logical_not(first))
        def _():
            dk_ref[...] += key_grad
            dv_ref[...] += value_grad

        turned = turn(dot(grad_scores, k_ref[...]), c_ref[...], s_ref[...], back=True)
        normed, inverse = head_norm(x_ref[...])
        dg_ref[...] = jnp.sum(turned * normed, axis=0, keepdims=True)[None]
        dx_ref[...] = head_norm_back(normed, inverse, turned * g_ref[0:1, :]).astype(BF)

    shared = pl.BlockSpec((key_count, HD), lambda h: (0, h // groups))
    return pl.pallas_call(
        kernel,
        grid=(H,),
        in_specs=[
            pl.BlockSpec(memory_space=pltpu.SMEM), head, head, half, half, gain, keys, values, head,
        ],
        out_specs=[head, shared, shared, pl.BlockSpec((1, 1, HD), lambda h: (h, 0, 0))],
        out_shape=[
            jax.ShapeDtypeStruct((rows, H * HD), BF),
            jax.ShapeDtypeStruct((key_count, KVH * HD), F32),
            jax.ShapeDtypeStruct((key_count, KVH * HD), F32),
            jax.ShapeDtypeStruct((H, 1, HD), F32),
        ],
        cost_estimate=pl.CostEstimate(
            flops=10 * rows * H * HD * key_count,
            bytes_accessed=rows * H * HD * 10 + key_count * KVH * HD * 12,
            transcendentals=rows * H * key_count,
        ),
        name="attend_back",
    )(
        device.reshape(1), projected, queries, cosine, sine, gains, kv_seen, kv_seen, gradient,
    )


def kv_prep(projected, cosine, sine, gains):
    rows = projected.shape[0]

    def kernel(x_ref, c_ref, s_ref, g_ref, out_ref):
        for head in range(2 * KVH):
            columns = slice(head * HD, (head + 1) * HD)
            normed, _ = head_norm(x_ref[:, columns])
            if head < KVH:
                normed = turn(normed * g_ref[1:2, :], c_ref[...], s_ref[...])
            out_ref[:, columns] = normed.astype(BF)

    return pl.pallas_call(
        kernel,
        out_shape=jax.ShapeDtypeStruct((rows, 2 * KVH * HD), BF),
        name="kv_prep",
    )(projected, cosine, sine, gains)


def kv_prep_back(projected, gradient, cosine, sine, gains):
    rows = projected.shape[0]

    def kernel(x_ref, d_ref, c_ref, s_ref, g_ref, dx_ref, dg_ref):
        gain_grad = jnp.zeros((1, HD), F32)
        for head in range(2 * KVH):
            columns = slice(head * HD, (head + 1) * HD)
            normed, inverse = head_norm(x_ref[:, columns])
            grad = d_ref[:, columns]
            if head < KVH:
                grad = turn(grad, c_ref[...], s_ref[...], back=True)
                gain_grad = gain_grad + jnp.sum(grad * normed, axis=0, keepdims=True)
                grad = grad * g_ref[1:2, :]
            dx_ref[:, columns] = head_norm_back(normed, inverse, grad).astype(BF)
        dg_ref[...] = gain_grad

    return pl.pallas_call(
        kernel,
        out_shape=[
            jax.ShapeDtypeStruct((rows, 2 * KVH * HD), BF),
            jax.ShapeDtypeStruct((1, HD), F32),
        ],
        name="kv_prep_back",
    )(projected, gradient, cosine, sine, gains)


class Place:
    def __init__(self):
        self.count = lax.axis_size("fsdp")
        self.copies = lax.axis_size("rep")
        self.device = lax.axis_index("fsdp")
        self.copy = lax.axis_index("rep")
        self.chips = self.count // 2
        self.chip = self.device // 2
        self.core = self.device % 2
        self.at_end = jnp.logical_or(self.chip == 0, self.chip == self.chips - 1)
        self.four = self.chips == 4

    def core_swap(self, array):
        return lax.ppermute(array, "fsdp", [(i, i ^ 1) for i in range(self.count)])

    def copy_swap(self, array, mask):
        return lax.ppermute(array, "rep", [(i, i ^ mask) for i in range(self.copies)])

    def chip_send(self, array, moves):
        pairs = [(2 * a + core, 2 * b + core) for a, b in moves for core in range(2)]
        return lax.ppermute(array, "fsdp", pairs)

    def by_core(self, mine, other):
        first = self.core == 0
        return jnp.where(first, mine, other), jnp.where(first, other, mine)

    def owner(self, j):
        return self.chip ^ j

    def chip_swap(self, array, mask):
        return self.chip_send(array, [(i, i ^ mask) for i in range(self.chips)])

    def spread_near(self, array):
        if not self.four:
            return [self.chip_swap(array, mask) for mask in range(1, self.chips)]
        return [self.chip_swap(array, 1), self.chip_swap(array, 2)]

    def spread_far(self, array, near):
        if not self.four:
            return []
        ends = self.chip_send(near[1], [(1, 0), (2, 3)])
        return [jnp.where(self.at_end, ends, self.chip_send(array, [(1, 2), (2, 1)]))]

    def spread(self, array):
        near = self.spread_near(array)
        return [array] + near + self.spread_far(array, near)

    def collect_near(self, parts):
        if not self.four:
            return [
                self.chip_swap(parts[mask].astype(BF), mask) for mask in range(1, self.chips)
            ]
        last = parts[3].astype(BF)
        return [
            self.chip_send(last, [(0, 1), (3, 2)]),
            self.chip_swap(parts[1].astype(BF), 1),
            self.chip_send(last, [(1, 2), (2, 1)]),
        ]

    def collect_far(self, parts, near):
        if not self.four:
            return near
        return near[1:] + [self.chip_swap((parts[2] + near[0].astype(F32)).astype(BF), 2)]

    def collect_sum(self, own, arrived):
        total = own
        for array in arrived:
            total = total + array.astype(F32)
        return total

    def in_order(self, pieces):
        block = jnp.concatenate(pieces, axis=0)
        rows, columns = block.shape
        bit = 1
        while bit < self.copies:
            split = block.reshape(self.copies // (2 * bit), 2, rows // self.copies * bit, columns)
            flipped = jnp.concatenate([split[:, 1:], split[:, :1]], axis=1)
            block = jnp.where((self.copy // bit) % 2 == 1, flipped, split).reshape(rows, columns)
            bit *= 2
        return block

    def swap_copies(self, array):
        if self.copies != 4:
            return [array] + [self.copy_swap(array, mask) for mask in range(1, self.copies)]
        half = array.shape[0] // 2
        first, second = self.copy_swap(array, 1), self.copy_swap(array, 2)
        last = [self.copy_swap(second[:half], 1), self.copy_swap(first[half:], 2)]
        return [array, first, second, jnp.concatenate(last, axis=0)]

    def lay_out(self, shard, shard_other, lane, lane_other, copies):
        rows, columns = shard.shape
        share = rows // copies
        chips, count = self.chips, self.count
        where = jnp.stack(
            [self.chip, self.core, self.copy if copies > 1 else 0]
            + [self.owner(j) for j in range(1, chips)]
        ).astype(jnp.int32)

        def kernel(at_ref, shard_ref, other_ref, lane_ref, lane_other_ref, whole_ref):
            core = at_ref[1]
            for side, (own, far) in enumerate(
                ((shard_ref, lane_ref), (other_ref, lane_other_ref))
            ):
                on = core if side == 0 else 1 - core
                base = pl.multiple_of((2 * at_ref[0] + on) * rows, rows)
                whole_ref[pl.ds(base, rows), :] = own[...]
                for j in range(1, chips):
                    base = (2 * at_ref[2 + j] + on) * rows
                    for mask in range(copies):
                        spot = pl.multiple_of(
                            base + jnp.bitwise_xor(at_ref[2], mask) * share, share
                        )
                        start = (mask * (chips - 1) + j - 1) * share
                        whole_ref[pl.ds(spot, share), :] = far[start : start + share, :]

        return pl.pallas_call(
            kernel,
            out_shape=jax.ShapeDtypeStruct((count * rows, columns), shard.dtype),
            in_specs=[pl.BlockSpec(memory_space=pltpu.SMEM)]
            + [pl.BlockSpec(memory_space=pltpu.VMEM)] * 4,
            out_specs=pl.BlockSpec(memory_space=pltpu.VMEM),
            name="lay_out",
        )(where, shard, shard_other, lane, lane_other)

    def own_share(self, shard):
        share = shard.shape[0] // self.copies
        return lax.dynamic_slice_in_dim(shard, self.copy * share, share, 0)

    def along_chain(self, own):
        return jnp.concatenate(self.spread(own)[1:], axis=0)

    def across_copies(self, slots):
        return jnp.concatenate(self.swap_copies(slots), axis=0)

    def lanes(self, whole):
        rows = whole.shape[0] // self.count
        split = whole.reshape(self.chips, 2, rows, whole.shape[1])
        return [
            lax.dynamic_index_in_dim(split, core, 1, keepdims=False).reshape(-1, whole.shape[1])
            for core in (self.core, 1 - self.core)
        ]

    def lane_outer(self, left, right, core):
        rows = left.shape[1] // self.count
        height, width = right.shape

        def kernel(at_ref, left_ref, right_ref, out_ref):
            out_ref[...] = outer_sum(left_ref[...], right_ref[...]).astype(BF)

        return pl.pallas_call(
            kernel,
            grid_spec=pltpu.PrefetchScalarGridSpec(
                num_scalar_prefetch=1,
                grid=(self.chips,),
                in_specs=[
                    pl.BlockSpec((height, rows), lambda i, at: (0, 2 * i + at[0])),
                    pl.BlockSpec((height, width), lambda i, at: (0, 0)),
                ],
                out_specs=pl.BlockSpec((rows, width), lambda i, at: (i, 0)),
            ),
            out_shape=jax.ShapeDtypeStruct((self.chips * rows, width), BF),
            cost_estimate=pl.CostEstimate(
                flops=2 * height * self.chips * rows * width,
                bytes_accessed=2 * (height + self.chips * rows) * width,
                transcendentals=0,
            ),
            name="lane_outer",
        )(core.reshape(1), left, right)

    def lane_parts(self, mine, arrived):
        rows = arrived[0].shape[0] // self.chips

        def part(chip):
            sums = [
                lax.dynamic_slice_in_dim(own, chip * rows, rows, 0).astype(F32)
                + lax.dynamic_slice_in_dim(other, chip * rows, rows, 0).astype(F32)
                for own, other in zip(mine, arrived)
            ]
            return jnp.concatenate(sums, axis=-1)

        return [part(self.owner(j)) for j in range(self.chips)]

    def copies_sum(self, array):
        share = array.shape[0] // self.copies
        array = array.astype(BF)

        def take(mask):
            return lax.dynamic_slice_in_dim(array, (self.copy ^ mask) * share, share, 0)

        total = take(0).astype(F32)
        for mask in range(1, self.copies):
            total = total + self.copy_swap(take(mask), mask).astype(F32)
        return total.astype(BF)

    def copies_all(self, total):
        return self.in_order(
            [total] + [self.copy_swap(total, mask) for mask in range(1, self.copies)]
        )


def half_specs(units, width, tile):
    tiles = units // tile
    return [
        pl.BlockSpec((tile, width), lambda i: (jnp.minimum(i, tiles - 1), 0)),
        pl.BlockSpec((tile, width), lambda i: (jnp.maximum(i - tiles, 0), 0)),
    ]


def gelu_parts(value):
    inner = GELU_SCALE * (value + GELU_CUBIC * value * value * value)
    bent = jnp.tanh(inner)
    slope = GELU_SCALE * (1.0 + 3.0 * GELU_CUBIC * value * value)
    return 0.5 * value * (1.0 + bent), 0.5 * (1.0 + bent) + 0.5 * value * (1.0 - bent * bent) * slope


def stack_rows(refs):
    values = [ref[...] for ref in refs]
    return values[0] if len(values) == 1 else jnp.concatenate(values, axis=0)


def ffn_block(blocks, gates, ups, downs, sum_type):
    (piece, width), count = blocks[0].shape, len(blocks)
    rows = piece * count
    units = gates[0].shape[0]
    tile = min(units, 512)
    tiles = units // tile

    def kernel(*refs):
        x_refs, (g0, g1, u0, u1, d0, d1) = refs[:count], refs[count : count + 6]
        sum_refs = refs[count + 6 : 2 * count + 6]
        hid_ref, gate_ref, up_ref, total = refs[2 * count + 6 :]
        step = pl.program_id(0)

        def work(g_ref, u_ref, d_ref):
            x = stack_rows(x_refs)
            gate, up = back_dot(x, g_ref[...]), back_dot(x, u_ref[...])
            bent = jnp.tanh(GELU_SCALE * (gate + GELU_CUBIC * gate * gate * gate))
            hidden = (0.5 * gate * (1.0 + bent) * up).astype(BF)
            hid_ref[...] = hidden
            gate_ref[...] = gate.astype(BF)
            up_ref[...] = up.astype(BF)
            return dot(hidden, d_ref[...])

        @pl.when(step == 0)
        def _():
            total[...] = work(g0, u0, d0)

        @pl.when(jnp.logical_and(step > 0, step < tiles))
        def _():
            total[...] += work(g0, u0, d0)

        @pl.when(step >= tiles)
        def _():
            total[...] += work(g1, u1, d1)

        @pl.when(step == 2 * tiles - 1)
        def _():
            for i, sum_ref in enumerate(sum_refs):
                sum_ref[...] = total[i * piece : (i + 1) * piece, :].astype(sum_type)

    whole = pl.BlockSpec((piece, width), lambda i: (0, 0))
    part = pl.BlockSpec((rows, tile), lambda i: (0, i))
    *sums, hidden, gate, up = pl.pallas_call(
        kernel,
        grid=(2 * tiles,),
        in_specs=[whole] * count + half_specs(units, width, tile) * 3,
        out_specs=[whole] * count + [part] * 3,
        out_shape=[jax.ShapeDtypeStruct((piece, width), sum_type)] * count
        + [jax.ShapeDtypeStruct((rows, 2 * units), BF)] * 3,
        scratch_shapes=[pltpu.VMEM((rows, width), F32)],
        cost_estimate=pl.CostEstimate(
            flops=12 * rows * width * units,
            bytes_accessed=12 * units * width + 12 * rows * units + 6 * rows * width,
            transcendentals=2 * rows * units,
        ),
        name="ffn_block",
    )(*blocks, *gates, *ups, *downs)
    return sums, hidden, gate, up


def ffn_block_back(grads, gate, up, gates, ups, downs, sum_type):
    (piece, width), count = grads[0].shape, len(grads)
    rows = piece * count
    units = gates[0].shape[0]
    tile = min(units, 512)
    tiles = units // tile

    def kernel(*refs):
        x_refs, (gate_ref, up_ref) = refs[:count], refs[count : count + 2]
        g0, g1, u0, u1, d0, d1 = refs[count + 2 : count + 8]
        sum_refs = refs[count + 8 : 2 * count + 8]
        dg_ref, du_ref, total = refs[2 * count + 8 :]
        step = pl.program_id(0)

        def work(g_ref, u_ref, d_ref):
            value, slope = gelu_parts(gate_ref[...].astype(F32))
            hidden = back_dot(stack_rows(x_refs), d_ref[...])
            grad_gate = (hidden * up_ref[...].astype(F32) * slope).astype(BF)
            grad_up = (hidden * value).astype(BF)
            dg_ref[...] = grad_gate
            du_ref[...] = grad_up
            return dot(grad_gate, g_ref[...]) + dot(grad_up, u_ref[...])

        @pl.when(step == 0)
        def _():
            total[...] = work(g0, u0, d0)

        @pl.when(jnp.logical_and(step > 0, step < tiles))
        def _():
            total[...] += work(g0, u0, d0)

        @pl.when(step >= tiles)
        def _():
            total[...] += work(g1, u1, d1)

        @pl.when(step == 2 * tiles - 1)
        def _():
            for i, sum_ref in enumerate(sum_refs):
                sum_ref[...] = total[i * piece : (i + 1) * piece, :].astype(sum_type)

    whole = pl.BlockSpec((piece, width), lambda i: (0, 0))
    part = pl.BlockSpec((rows, tile), lambda i: (0, i))
    *sums, grad_gate, grad_up = pl.pallas_call(
        kernel,
        grid=(2 * tiles,),
        in_specs=[whole] * count + [part, part] + half_specs(units, width, tile) * 3,
        out_specs=[whole] * count + [part] * 2,
        out_shape=[jax.ShapeDtypeStruct((piece, width), sum_type)] * count
        + [jax.ShapeDtypeStruct((rows, 2 * units), BF)] * 2,
        scratch_shapes=[pltpu.VMEM((rows, width), F32)],
        cost_estimate=pl.CostEstimate(
            flops=12 * rows * width * units,
            bytes_accessed=12 * units * width + 16 * rows * units + 6 * rows * width,
            transcendentals=2 * rows * units,
        ),
        name="ffn_block_back",
    )(*grads, gate, up, *gates, *ups, *downs)
    return sums, grad_gate, grad_up


def outer_blocks(lefts, rights, start, columns, added=None, whole=None, place=0, places=1):
    width = rights[0].shape[1]
    tile = min(columns, 256)
    n_left, tiles = len(lefts), columns // tile
    n_both = n_left + len(rights)

    def kernel(*refs):
        out_ref = refs[-1]
        total = outer_sum(stack_rows(refs[:n_left]), stack_rows(refs[n_left:n_both]))
        if added is not None:
            total = total + refs[n_both][...].astype(F32)
        out_ref[...] = total.astype(BF)

    rows = sum(left.shape[0] for left in lefts)
    operands = [*lefts, *rights]
    specs = [pl.BlockSpec((left.shape[0], tile), lambda i: (0, i + start // tile)) for left in lefts]
    specs += [pl.BlockSpec(right.shape, lambda i: (0, 0)) for right in rights]
    if added is not None:
        operands.append(added)
        specs.append(pl.BlockSpec((tile, width), lambda i: (i, 0)))
    aliases = {}
    if whole is not None:
        aliases = {len(operands): 0}
        operands.append(whole)
        specs.append(pl.BlockSpec(memory_space=pl.ANY))
    return pl.pallas_call(
        kernel,
        grid=(tiles,),
        in_specs=specs,
        out_specs=pl.BlockSpec((tile, width), lambda i: (i + place * tiles, 0)),
        out_shape=jax.ShapeDtypeStruct((places * columns, width), BF),
        input_output_aliases=aliases,
        cost_estimate=pl.CostEstimate(
            flops=2 * rows * columns * width,
            bytes_accessed=2 * rows * (columns + width) + 4 * columns * width,
            transcendentals=0,
        ),
        name="outer_blocks",
    )(*operands)


def split_pair(pair):
    units, _, width = pair.shape
    rows = min(units, 128)

    def kernel(pair_ref, first_ref, second_ref):
        first_ref[...] = pair_ref[:, 0, :].astype(BF)
        second_ref[...] = pair_ref[:, 1, :].astype(BF)

    flat = pl.BlockSpec((rows, width), lambda i: (i, 0))
    return pl.pallas_call(
        kernel,
        grid=(units // rows,),
        in_specs=[pl.BlockSpec((rows, 2, width), lambda i: (i, 0, 0))],
        out_specs=[flat, flat],
        out_shape=[jax.ShapeDtypeStruct((units, width), BF)] * 2,
        cost_estimate=pl.CostEstimate(
            flops=0, bytes_accessed=units * width * 12, transcendentals=0
        ),
        name="split_pair",
    )(pair)


def join_pair(stacked, units):
    width = stacked.shape[1]
    rows = min(units, 128)
    tiles = units // rows

    def kernel(first_ref, second_ref, pair_ref):
        pair_ref[:, 0, :] = first_ref[...].astype(F32)
        pair_ref[:, 1, :] = second_ref[...].astype(F32)

    return pl.pallas_call(
        kernel,
        grid=(tiles,),
        in_specs=[
            pl.BlockSpec((rows, width), lambda i: (i + tiles, 0)),
            pl.BlockSpec((rows, width), lambda i: (i + 2 * tiles, 0)),
        ],
        out_specs=pl.BlockSpec((rows, 2, width), lambda i: (i, 0, 0)),
        out_shape=jax.ShapeDtypeStruct((units, 2, width), F32),
        cost_estimate=pl.CostEstimate(
            flops=0, bytes_accessed=units * width * 12, transcendentals=0
        ),
        name="join_pair",
    )(stacked, stacked)


def tie(*values):
    return lax.optimization_barrier(values)


def body(
    tokens,
    layer_input,
    cotangent,
    norm_gains,
    qk_gains,
    w_qkv,
    w_out,
    laurel_left,
    laurel_right,
    w_gate_up,
    w_down,
    pli_gate,
    pli_proj,
):
    at = Place()
    device = at.device
    rows_dev, width = tokens.shape
    shard = w_qkv.shape[0]
    prompt_len = PROMPT_DEVS * rows_dev
    q_cols = H * HD
    lr, pd = laurel_left.shape[1], pli_gate.shape[1]
    n_gain, n_qk = norm_gains.size, qk_gains.size

    def pack_gains(norm_part, qk_part):
        flat = jnp.concatenate([norm_part.reshape(-1), qk_part.reshape(-1)]).astype(BF)
        flat = jnp.pad(flat, (0, shard * 128 - flat.size))
        return flat.reshape(shard, 128)

    kv_pack = jnp.concatenate(
        [w_qkv[:, q_cols:].astype(BF), pack_gains(norm_gains, qk_gains)], axis=1
    )
    def gather_all(array):
        return lax.all_gather(at.own_share(array), ("fsdp", "rep"), axis=0, tiled=True)

    main_all = gather_all(
        jnp.concatenate(
            [
                w_qkv[:, :q_cols].astype(BF),
                w_out.astype(BF),
                laurel_left.astype(BF),
                laurel_right.astype(BF).reshape(shard, lr),
            ],
            axis=1,
        )
    )
    q_all = main_all[:, :q_cols]
    out_all = main_all[:, q_cols : q_cols + width]
    left_all = main_all[:, q_cols + width : q_cols + width + lr]
    right_all = main_all[:, q_cols + width + lr :].reshape(lr, width)
    pli_pack_all = gather_all(
        jnp.concatenate([pli_gate.astype(BF), pli_proj.astype(BF).reshape(shard, pd)], axis=1)
    )
    w_gate, w_up = split_pair(w_gate_up)
    w_down_bf = w_down.astype(BF)
    own_wide = (w_gate, w_up, w_down_bf)
    kv_twin = at.core_swap(kv_pack)
    kv_near = at.spread_near(kv_pack)
    kv_near, kv_twin, own_wide = tie(kv_near, kv_twin, own_wide)
    kv_far = at.spread_far(kv_pack, kv_near)
    their_wide = [at.core_swap(own) for own in own_wide]
    kv_lane = jnp.concatenate(kv_near + kv_far, axis=0)
    kv_all = at.lay_out(kv_pack, kv_twin, kv_lane, at.core_swap(kv_lane), 1)
    kv_weight = kv_all[:, : 2 * KVH * HD]
    gain_rows_all = kv_all[:, 2 * KVH * HD :].reshape(at.count, -1)[:, : n_gain + n_qk]
    gains = jnp.moveaxis(
        gain_rows_all[:, :n_gain].reshape(at.count, norm_gains.shape[0], -1), 0, 1
    ).reshape(norm_gains.shape[0], -1).astype(F32)
    qk_gain = jnp.moveaxis(
        gain_rows_all[:, n_gain:].reshape(at.count, qk_gains.shape[0], -1), 0, 1
    ).reshape(qk_gains.shape[0], -1).astype(F32)
    inputs = tokens.astype(F32)
    extra_input = layer_input.astype(F32)

    def input_norm(tensor, gain_rows):
        return rms_norm(tensor) * gain_rows[0]

    normed, input_pull = jax.vjp(input_norm, inputs, gains)
    normed_bf = normed.astype(BF)
    local_rows = jnp.arange(rows_dev, dtype=jnp.int32)
    places = jnp.where(
        device < PROMPT_DEVS, device * rows_dev + local_rows, prompt_len + local_rows % CONT_LEN
    )

    half = HD // 2
    frequency = THETA_BASE ** (-(jnp.arange(half, dtype=F32) * 2.0 / HD))
    angles = places.astype(F32)[:, None] * frequency
    cosine, sine = jnp.cos(angles), jnp.sin(angles)
    kv_proj = dot(normed_bf, kv_weight)
    kv_own = kv_prep(kv_proj, cosine, sine, qk_gain)

    prompt_chips = PROMPT_DEVS // 2
    if at.four:
        arrived = at.chip_send(kv_own, [(0, 2), (1, 3)])
        even = jnp.where(at.chip < prompt_chips, kv_own, arrived)
        odd = at.chip_swap(even, 1)
        kv_lane = [jnp.where(at.chip % 2 == i, even, odd) for i in range(2)]
    else:
        blocks = [kv_own] + [
            at.chip_send(kv_own, [(i, (i - j) % at.chips) for i in range(prompt_chips)])
            for j in range(1, at.chips)
        ]
        kv_lane = []
        for block in range(prompt_chips):
            seen = kv_own
            for j in range(1, at.chips):
                seen = jnp.where((at.chip + j) % at.chips == block, blocks[j], seen)
            kv_lane.append(seen)
    q_proj = dot(normed_bf, q_all)
    laurel_mid = dot(normed_bf, left_all).astype(BF)
    laurel_out = dot(laurel_mid, right_all)
    kv_lane, own_wide, their_wide, q_proj, laurel_out = tie(
        jnp.stack(kv_lane), own_wide, their_wide, q_proj, laurel_out
    )
    halves = list(zip(own_wide, their_wide))
    (gate_halves, up_halves, down_halves) = halves

    kv_other = at.core_swap(kv_lane)
    kv_pairs = [row for i in range(prompt_chips) for row in at.by_core(kv_lane[i], kv_other[i])]
    kv_seen = jnp.concatenate(kv_pairs + [kv_own], axis=0)
    queries_bf, attended_bf = attend(q_proj, cosine, sine, qk_gain, kv_seen, device)
    pgate_all = pli_pack_all[:, :pd]
    pproj_all = pli_pack_all[:, pd:].reshape(pd, width)
    attn_proj = dot(attended_bf, out_all)

    def middle(inputs, normed, attn_proj, laurel_out, gain_rows):
        first_sum = inputs + rms_norm(attn_proj) * gain_rows[1]
        laurel_sum = normed + rms_norm(laurel_out) * gain_rows[2]
        stream = (first_sum + laurel_sum) * HALF_ROOT
        return (stream, rms_norm(stream) * gain_rows[3])

    (stream, ffn_in), middle_pull = jax.vjp(middle, inputs, normed, attn_proj, laurel_out, gains)

    piece = rows_dev // CHUNKS
    units = w_down.shape[0]

    def staged(rows, work):
        near = at.spread_near(rows)
        first = work(0, [rows], F32)
        near, first = tie(near, first)
        far = at.spread_far(rows, near)
        pairs = [near[i : i + 2] for i in range(0, len(near), 2)]
        second = [work(j + 1, blocks, BF) for j, blocks in enumerate(pairs)]
        far, second = tie(far, second)
        parts = [part for sums, *_ in second for part in sums]
        back = [at.chip_swap(part, j + 1) for j, part in enumerate(parts)]
        done = [first, *second]
        last = None
        if far:
            third = work(len(done), far, BF)
            first_back, third = tie(back[0], third)
            back[0] = first_back
            done.append(third)
            last = third[0][0]
        return first[0][0], back, last, [kept for _, kept in done]

    def ffn_forward(rows):
        def work(j, blocks, sum_type):
            sums, *kept = ffn_block(blocks, gate_halves, up_halves, down_halves, sum_type)
            return sums, (blocks, *kept)

        own, back, last, kept = staged(rows, work)
        if last is not None:
            back = back + [at.chip_swap(last, at.chips - 1)]
        return at.collect_sum(own, back), kept

    def ffn_backward(rows, kept):
        def work(j, grads, sum_type):
            blocks, hidden, gate, up = kept[j]
            sums, grad_gate, grad_up = ffn_block_back(
                grads, gate, up, gate_halves, up_halves, down_halves, sum_type
            )
            return sums, (blocks, hidden, grads, grad_gate, grad_up)

        return staged(rows, work)

    def tail_norm(stream, ffn_out, gain_rows):
        return stream + rms_norm(ffn_out) * gain_rows[4]

    def pli_mix(pli_pre, extra_input):
        return jax.nn.gelu(pli_pre, approximate=True) * extra_input

    def final_norm(after_ffn, pli_out, gain_rows):
        return after_ffn + rms_norm(pli_out) * gain_rows[5]

    cuts = [slice(i * piece, (i + 1) * piece) for i in range(CHUNKS)]
    forwards = [ffn_forward(ffn_in[cut].astype(BF)) for cut in cuts]
    gain_total = 0.0
    results, extras, streams, ins, all_grads = [], [], [], [], []
    pli_rows = []
    for cut, (ffn_out, kept) in zip(cuts, forwards):
        after_ffn, tail_pull = jax.vjp(tail_norm, stream[cut], ffn_out, gains)
        after_bf = after_ffn.astype(BF)
        pli_mid, pli_pull = jax.vjp(pli_mix, dot(after_bf, pgate_all), extra_input[cut])
        pli_mid_bf = pli_mid.astype(BF)
        result, final_pull = jax.vjp(final_norm, after_ffn, dot(pli_mid_bf, pproj_all), gains)
        grad_after, grad_pli_out, gain_final = final_pull(cotangent[cut].astype(F32))
        grad_pli_out_bf = grad_pli_out.astype(BF)
        grad_pli_pre, grad_extra = pli_pull(back_dot(grad_pli_out_bf, pproj_all))
        grad_pli_pre_bf = grad_pli_pre.astype(BF)
        grad_after = grad_after + back_dot(grad_pli_pre_bf, pgate_all)
        grad_stream, grad_ffn_out, gain_tail = tail_pull(grad_after)
        own, back, last, grads = ffn_backward(grad_ffn_out.astype(BF), kept)
        gain_total = gain_total + gain_final + gain_tail
        results.append(result.astype(BF))
        extras.append(grad_extra)
        streams.append(grad_stream)
        ins.append((own, back, last))
        all_grads.append(grads)
        pli_rows.append((pli_mid_bf, grad_pli_out_bf, after_bf, grad_pli_pre_bf))

    kept = [[group[i] for grads in all_grads for group in grads] for i in range(5)]
    hiddens, gates, ups = kept[1], kept[3], kept[4]
    ins_blocks, outs_grad = [[block for blocks in kept[i] for block in blocks] for i in (0, 2)]
    pairs = [(hiddens, outs_grad), (gates, ins_blocks), (ups, ins_blocks)]
    theirs = [
        outer_blocks(lefts, rights, units, units) for lefts, rights in pairs
    ]
    mids, pli_outs, afters, pres = [jnp.concatenate(rows, axis=0) for rows in zip(*pli_rows)]
    grad_pproj = outer_sum(mids, pli_outs).astype(BF).reshape(-1, pd)
    grad_pgate = outer_sum(afters, pres).astype(BF)
    half_rows = piece // 2
    lasts = [last for _, _, last in ins if last is not None]
    upper = [at.chip_swap(last[:half_rows], at.chips - 1) for last in lasts]
    upper, theirs, grad_pproj, grad_pgate = tie(upper, theirs, grad_pproj, grad_pgate)
    under = [at.chip_swap(last[half_rows:], at.chips - 1) for last in lasts]
    wide_w = None
    for place, ((lefts, rights), their) in enumerate(zip(pairs, theirs)):
        wide_w = outer_blocks(
            lefts, rights, 0, units, at.core_swap(their), wide_w, place, 3
        )
    backs, under, wide_w = tie([back for _, back, _ in ins], under, wide_w)
    wide_part = lax.psum_scatter(wide_w, "rep", scatter_dimension=0, tiled=True)
    ends = [[jnp.concatenate(pair, axis=0)] for pair in zip(upper, under)] or [[]] * len(ins)
    ins = [
        at.collect_sum(own, back + end) for (own, _, _), back, end in zip(ins, backs, ends)
    ]

    grad_inputs, grad_normed, grad_attn_proj, grad_laurel_out, gain_middle = middle_pull(
        (jnp.concatenate(streams, axis=0), jnp.concatenate(ins, axis=0))
    )
    grad_attn_bf = grad_attn_proj.astype(BF)
    core, other_core = at.core, 1 - at.core
    out_leaving = at.core_swap(at.lane_outer(attended_bf, grad_attn_bf, other_core))
    out_mine = at.lane_outer(attended_bf, grad_attn_bf, core)
    grad_laurel_bf = grad_laurel_out.astype(BF)
    grad_right_w = outer_sum(laurel_mid, grad_laurel_bf).astype(BF).reshape(-1, lr)
    grad_mid_bf = back_dot(grad_laurel_bf, right_all).astype(BF)
    grad_left_w = outer_sum(normed_bf, grad_mid_bf).astype(BF)
    small_mine, small_leaving = at.lanes(
        jnp.concatenate([grad_left_w, grad_right_w, grad_pgate, grad_pproj], axis=1)
    )
    small_leaving = at.core_swap(small_leaving)
    out_leaving, small_leaving, out_mine, small_mine, grad_attn_bf = tie(
        out_leaving, small_leaving, out_mine, small_mine, grad_attn_bf
    )
    grad_attended = back_dot(grad_attn_bf, out_all).astype(BF)
    out_parts = at.lane_parts([out_mine, small_mine], [out_leaving, small_leaving])
    out_near = at.collect_near(out_parts)
    grad_q_bf, key_grad, value_grad, q_gain_rows = attend_back(
        q_proj, queries_bf, cosine, sine, qk_gain, kv_seen, grad_attended, device
    )
    out_near, grad_q_bf, key_grad, value_grad = tie(out_near, grad_q_bf, key_grad, value_grad)

    def kv_rows(first, core):
        begin = (2 * first + core) * rows_dev
        return jnp.concatenate(
            [
                lax.dynamic_slice_in_dim(grad, begin, rows_dev, 0).astype(BF)
                for grad in (key_grad, value_grad)
            ],
            axis=1,
        )

    kv_other = at.core_swap(
        jnp.stack([kv_rows(chip, other_core) for chip in range(prompt_chips)])
    )

    def kv_part(chip):
        index = jnp.clip(chip, 0, prompt_chips - 1)
        theirs = lax.dynamic_index_in_dim(kv_other, index, 0, keepdims=False)
        return kv_rows(index, core).astype(F32) + theirs.astype(F32)

    offsets = [0, 1] if at.four else range(at.chips)
    kv_parts = [
        kv_part((at.chip + j) % 2 if at.four else (at.chip + j) % at.chips) for j in offsets
    ]
    q_other_w = at.lane_outer(normed_bf, grad_q_bf, other_core)
    kv_parts, q_other_w, wide_part = tie(kv_parts, q_other_w, wide_part)
    wide_sum = lax.all_gather(wide_part, "rep", axis=0, tiled=True)
    if at.four:
        pair_sum = kv_parts[0] + at.chip_swap(kv_parts[1].astype(BF), 1).astype(F32)
        q_mine = at.lane_outer(normed_bf, grad_q_bf, core)
        pair_sum, q_mine = tie(pair_sum, q_mine)
        prompt_parts = [at.chip_send(pair_sum.astype(BF), [(2, 0), (3, 1)])]
    else:
        pair_sum = kv_parts[0]
        q_mine = at.lane_outer(normed_bf, grad_q_bf, core)
        prompt_parts = [
            at.chip_send(
                kv_parts[j].astype(BF), [((i - j) % at.chips, i) for i in range(prompt_chips)]
            )
            for j in range(1, at.chips)
        ]
    q_leaving = at.core_swap(q_other_w)
    grad_normed = grad_normed + back_dot(grad_mid_bf, left_all)
    grad_normed = grad_normed + back_dot(grad_q_bf, q_all)
    q_parts = at.lane_parts([q_mine], [q_leaving])
    prompt_parts, pair_sum, q_parts, grad_normed = tie(
        prompt_parts, pair_sum, q_parts, grad_normed
    )

    out_far = at.collect_far(out_parts, out_near)
    q_near = at.collect_near(q_parts)
    prompt_sum = pair_sum
    for sent in prompt_parts:
        prompt_sum = prompt_sum + sent.astype(F32)
    kv_sum = jnp.where(
        device < PROMPT_DEVS,
        prompt_sum,
        jnp.concatenate([key_grad[prompt_len:], value_grad[prompt_len:]], axis=1),
    )
    grad_kv_bf, k_gain_row = kv_prep_back(kv_proj, kv_sum, cosine, sine, qk_gain)
    kv_other_w = at.lane_outer(normed_bf, grad_kv_bf, other_core)
    kv_mine = at.lane_outer(normed_bf, grad_kv_bf, core)
    grad_normed = grad_normed + back_dot(grad_kv_bf, kv_weight)
    grad_first, gain_input = input_pull(grad_normed)
    grad_tokens = grad_inputs + grad_first
    gain_total = gain_total + gain_middle + gain_input
    qk_total = jnp.concatenate([jnp.sum(q_gain_rows, axis=0), k_gain_row], axis=0)

    def by_owner(array):
        return jnp.moveaxis(array.reshape(array.shape[0], at.count, -1), 1, 0).reshape(at.count, -1)

    gain_pack = jnp.concatenate([by_owner(gain_total), by_owner(qk_total)], axis=1).astype(BF)
    gain_pack = jnp.pad(gain_pack, ((0, 0), (0, shard * 128 - gain_pack.shape[1])))
    gain_mine, gain_leaving = at.lanes(gain_pack.reshape(-1, 128))
    out_far, q_near, kv_other_w, kv_mine, gain_mine, gain_leaving, grad_tokens = tie(
        out_far, q_near, kv_other_w, kv_mine, gain_mine, gain_leaving, grad_tokens
    )
    out_ready = at.collect_sum(out_parts[0], out_far).astype(BF)
    kv_leaving, gain_leaving, wide_sum, out_ready = tie(
        at.core_swap(kv_other_w), at.core_swap(gain_leaving), wide_sum, out_ready
    )
    q_far = at.collect_far(q_parts, q_near)
    kv_w_parts = at.lane_parts([kv_mine, gain_mine], [kv_leaving, gain_leaving])
    kv_near = at.collect_near(kv_w_parts)
    grad_gate_up, grad_down = join_pair(wide_sum, units), wide_sum[:units].astype(F32)
    q_far, kv_near, grad_gate_up, grad_down = tie(q_far, kv_near, grad_gate_up, grad_down)
    out_total = at.copies_sum(out_ready)
    kv_far = at.collect_far(kv_w_parts, kv_near)
    q_total = at.copies_sum(at.collect_sum(q_parts[0], q_far))
    kv_far, q_total, out_total = tie(kv_far, q_total, out_total)
    kv_total = at.copies_sum(at.collect_sum(kv_w_parts[0], kv_far))
    q_sum = at.copies_all(q_total)
    out_sum = at.copies_all(out_total)
    kv_total, q_sum, out_sum = tie(kv_total, q_sum, out_sum)
    kv_sum_w = at.copies_all(kv_total)
    gain_out = kv_sum_w[:, 2 * KVH * HD :].reshape(-1)
    return (
        jnp.concatenate(results, axis=0),
        grad_tokens,
        jnp.concatenate(extras, axis=0),
        gain_out[:n_gain].reshape(norm_gains.shape).astype(F32),
        gain_out[n_gain : n_gain + n_qk].reshape(qk_gains.shape).astype(F32),
        jnp.concatenate([q_sum, kv_sum_w[:, : 2 * KVH * HD]], axis=1).astype(F32),
        out_sum[:, :width].astype(F32),
        out_sum[:, width : width + lr].astype(F32),
        out_sum[:, width + lr : width + 2 * lr].reshape(laurel_right.shape).astype(F32),
        grad_gate_up,
        grad_down,
        out_sum[:, width + 2 * lr : width + 2 * lr + pd].astype(F32),
        out_sum[:, width + 2 * lr + pd :].reshape(pli_proj.shape).astype(F32),
    )


def solution(mesh):
    placed = (
        P(("rep", "fsdp"), None),
        P(("rep", "fsdp"), None),
        P(("rep", "fsdp"), None),
        P(None, "fsdp"),
        P(None, "fsdp"),
        P("fsdp", None),
        P("fsdp", None),
        P("fsdp", None),
        P("fsdp", None),
        P("fsdp", None, None),
        P("fsdp", None),
        P("fsdp", None),
        P("fsdp", None),
    )
    return jax.shard_map(
        body,
        mesh=mesh,
        in_specs=placed,
        out_specs=(
            P(("rep", "fsdp"), None),
            P(("rep", "fsdp"), None),
            P(("rep", "fsdp"), None),
            P(None, "fsdp"),
            P(None, "fsdp"),
            P("fsdp", None),
            P("fsdp", None),
            P("fsdp", None),
            P("fsdp", None),
            P("fsdp", None, None),
            P("fsdp", None),
            P("fsdp", None),
            P("fsdp", None),
        ),
        check_vma=False,
    )
```

```python
import jax
import jax.numpy as jnp
from jax import lax
from jax.experimental import pallas as pl
from jax.experimental.pallas import tpu as pltpu
from jax.sharding import PartitionSpec as P

H = 8
KVH = 2
HD = 256
CONT_LEN = 256
PROMPT_DEVS = 4
CHUNKS = 1

EPSILON = 1e-06
THETA_BASE = 1000000.0
HALF_ROOT = 0.7071067811865476
NEG_FILL = -1e30
GELU_SCALE = 0.7978845608028654
GELU_CUBIC = 0.044715
BF = jnp.bfloat16
F32 = jnp.float32


def rms_norm(tensor):
    return tensor * lax.rsqrt(jnp.mean(tensor * tensor, axis=-1, keepdims=True) + EPSILON)


def dot(left_mat, right_mat):
    return jnp.dot(left_mat, right_mat, preferred_element_type=F32)


def outer_sum(left_mat, right_mat):
    return lax.dot_general(
        left_mat, right_mat, (((0,), (0,)), ((), ())), preferred_element_type=F32
    )


def back_dot(gradient, weight):
    return lax.dot_general(
        gradient, weight, (((1,), (1,)), ((), ())), preferred_element_type=F32
    )


def turn(tensor, cosine, sine, back=False):
    half = tensor.shape[-1] // 2
    first, second = tensor[:, :half], tensor[:, half:]
    if back:
        return jnp.concatenate(
            [first * cosine + second * sine, second * cosine - first * sine], axis=-1
        )
    return jnp.concatenate(
        [first * cosine - second * sine, second * cosine + first * sine], axis=-1
    )


def head_norm(tensor):
    inverse = lax.rsqrt(jnp.mean(tensor * tensor, axis=-1, keepdims=True) + EPSILON)
    return tensor * inverse, inverse


def head_norm_back(normed, inverse, gradient):
    return inverse * (gradient - normed * jnp.mean(gradient * normed, axis=-1, keepdims=True))


def head_shares(queries, keys, device):
    rows, key_count = queries.shape[0], keys.shape[0]
    prompt_len = key_count - rows
    scores = back_dot(queries, keys)
    local = lax.broadcasted_iota(jnp.int32, scores.shape, 0)
    index = lax.broadcasted_iota(jnp.int32, scores.shape, 1)
    own = index - prompt_len
    in_prompt = device < PROMPT_DEVS
    last_seen = jnp.where(in_prompt, device * rows, prompt_len) + local
    allowed = index <= last_seen
    if rows > CONT_LEN:
        piece = jnp.logical_or(own < 0, own // CONT_LEN == local // CONT_LEN)
        allowed = jnp.logical_and(allowed, piece)
    scores = jnp.where(allowed, scores, NEG_FILL)
    grown = jnp.exp(scores - jnp.max(scores, axis=-1, keepdims=True))
    return grown / jnp.sum(grown, axis=-1, keepdims=True)


def head_specs(rows, key_count):
    head = pl.BlockSpec((rows, HD), lambda h: (0, h))
    half = pl.BlockSpec((rows, HD // 2), lambda h: (0, 0))
    gain = pl.BlockSpec((2, HD), lambda h: (0, 0))
    keys = pl.BlockSpec((key_count, HD), lambda h: (0, h // (H // KVH)))
    values = pl.BlockSpec((key_count, HD), lambda h: (0, KVH + h // (H // KVH)))
    return head, half, gain, keys, values


def attend(projected, cosine, sine, gains, kv_seen, device):
    rows, key_count = projected.shape[0], kv_seen.shape[0]
    head, half, gain, keys, values = head_specs(rows, key_count)

    def kernel(at_ref, x_ref, c_ref, s_ref, g_ref, k_ref, v_ref, q_ref, o_ref):
        normed, _ = head_norm(x_ref[...])
        queries = turn(normed * g_ref[0:1, :], c_ref[...], s_ref[...]).astype(BF)
        q_ref[...] = queries
        shares = head_shares(queries, k_ref[...], at_ref[0])
        o_ref[...] = dot(shares.astype(BF), v_ref[...]).astype(BF)

    return pl.pallas_call(
        kernel,
        grid=(H,),
        in_specs=[pl.BlockSpec(memory_space=pltpu.SMEM), head, half, half, gain, keys, values],
        out_specs=[head, head],
        out_shape=[jax.ShapeDtypeStruct((rows, H * HD), BF)] * 2,
        cost_estimate=pl.CostEstimate(
            flops=4 * rows * H * HD * key_count,
            bytes_accessed=rows * H * HD * 8 + key_count * KVH * HD * 4,
            transcendentals=rows * H * key_count,
        ),
        name="attend",
    )(device.reshape(1), projected, cosine, sine, gains, kv_seen, kv_seen)


def attend_back(projected, queries, cosine, sine, gains, kv_seen, gradient, weights, device):
    rows, key_count = projected.shape[0], kv_seen.shape[0]
    groups = H // KVH
    width = gradient.shape[1]
    head, half, gain, keys, values = head_specs(rows, key_count)

    def kernel(
        at_ref, x_ref, q_ref, c_ref, s_ref, g_ref, k_ref, v_ref, do_ref, w_ref,
        dx_ref, dk_ref, dv_ref, dg_ref,
    ):
        queries = q_ref[...]
        grad = back_dot(do_ref[...], w_ref[...]).astype(BF)
        shares = head_shares(queries, k_ref[...], at_ref[0])
        grad_shares = back_dot(grad, v_ref[...])
        inner = jnp.sum(shares * grad_shares, axis=-1, keepdims=True)
        grad_scores = (shares * (grad_shares - inner)).astype(BF)
        key_grad = outer_sum(grad_scores, queries)
        value_grad = outer_sum(shares.astype(BF), grad)
        first = lax.rem(pl.program_id(0), groups) == 0

        @pl.when(first)
        def _():
            dk_ref[...] = key_grad
            dv_ref[...] = value_grad

        @pl.when(jnp.logical_not(first))
        def _():
            dk_ref[...] += key_grad
            dv_ref[...] += value_grad

        turned = turn(dot(grad_scores, k_ref[...]), c_ref[...], s_ref[...], back=True)
        normed, inverse = head_norm(x_ref[...])
        dg_ref[...] = jnp.sum(turned * normed, axis=0, keepdims=True)[None]
        dx_ref[...] = head_norm_back(normed, inverse, turned * g_ref[0:1, :]).astype(BF)

    shared = pl.BlockSpec((key_count, HD), lambda h: (0, h // groups))
    return pl.pallas_call(
        kernel,
        grid=(H,),
        in_specs=[
            pl.BlockSpec(memory_space=pltpu.SMEM), head, head, half, half, gain, keys, values,
            pl.BlockSpec((rows, width), lambda h: (0, 0)),
            pl.BlockSpec((HD, width), lambda h: (h, H * HD // width)),
        ],
        out_specs=[head, shared, shared, pl.BlockSpec((1, 1, HD), lambda h: (h, 0, 0))],
        out_shape=[
            jax.ShapeDtypeStruct((rows, H * HD), BF),
            jax.ShapeDtypeStruct((key_count, KVH * HD), F32),
            jax.ShapeDtypeStruct((key_count, KVH * HD), F32),
            jax.ShapeDtypeStruct((H, 1, HD), F32),
        ],
        cost_estimate=pl.CostEstimate(
            flops=10 * rows * H * HD * key_count,
            bytes_accessed=rows * H * HD * 10 + key_count * KVH * HD * 12,
            transcendentals=rows * H * key_count,
        ),
        name="attend_back",
    )(
        device.reshape(1), projected, queries, cosine, sine, gains, kv_seen, kv_seen, gradient, weights,
    )


def kv_prep(projected, cosine, sine, gains):
    rows = projected.shape[0]

    def kernel(x_ref, c_ref, s_ref, g_ref, out_ref):
        for head in range(2 * KVH):
            columns = slice(head * HD, (head + 1) * HD)
            normed, _ = head_norm(x_ref[:, columns])
            if head < KVH:
                normed = turn(normed * g_ref[1:2, :], c_ref[...], s_ref[...])
            out_ref[:, columns] = normed.astype(BF)

    return pl.pallas_call(
        kernel,
        out_shape=jax.ShapeDtypeStruct((rows, 2 * KVH * HD), BF),
        name="kv_prep",
    )(projected, cosine, sine, gains)


def kv_prep_back(projected, gradient, cosine, sine, gains):
    rows = projected.shape[0]

    def kernel(x_ref, d_ref, c_ref, s_ref, g_ref, dx_ref, dg_ref):
        gain_grad = jnp.zeros((1, HD), F32)
        for head in range(2 * KVH):
            columns = slice(head * HD, (head + 1) * HD)
            normed, inverse = head_norm(x_ref[:, columns])
            grad = d_ref[:, columns]
            if head < KVH:
                grad = turn(grad, c_ref[...], s_ref[...], back=True)
                gain_grad = gain_grad + jnp.sum(grad * normed, axis=0, keepdims=True)
                grad = grad * g_ref[1:2, :]
            dx_ref[:, columns] = head_norm_back(normed, inverse, grad).astype(BF)
        dg_ref[...] = gain_grad

    return pl.pallas_call(
        kernel,
        out_shape=[
            jax.ShapeDtypeStruct((rows, 2 * KVH * HD), BF),
            jax.ShapeDtypeStruct((1, HD), F32),
        ],
        name="kv_prep_back",
    )(projected, gradient, cosine, sine, gains)


class Place:
    def __init__(self):
        self.count = lax.axis_size("fsdp")
        self.copies = lax.axis_size("rep")
        self.device = lax.axis_index("fsdp")
        self.copy = lax.axis_index("rep")
        self.chips = self.count // 2
        self.chip = self.device // 2
        self.core = self.device % 2
        self.at_end = jnp.logical_or(self.chip == 0, self.chip == self.chips - 1)
        self.four = self.chips == 4

    def core_swap(self, array):
        return lax.ppermute(array, "fsdp", [(i, i ^ 1) for i in range(self.count)])

    def copy_swap(self, array, mask):
        return lax.ppermute(array, "rep", [(i, i ^ mask) for i in range(self.copies)])

    def chip_send(self, array, moves):
        pairs = [(2 * a + core, 2 * b + core) for a, b in moves for core in range(2)]
        return lax.ppermute(array, "fsdp", pairs)

    def by_core(self, mine, other):
        first = self.core == 0
        return jnp.where(first, mine, other), jnp.where(first, other, mine)

    def owner(self, j):
        return self.chip ^ j

    def chip_swap(self, array, mask):
        return self.chip_send(array, [(i, i ^ mask) for i in range(self.chips)])

    def spread_near(self, array):
        if not self.four:
            return [self.chip_swap(array, mask) for mask in range(1, self.chips)]
        return [self.chip_swap(array, 1), self.chip_swap(array, 2)]

    def spread_far(self, array, near):
        if not self.four:
            return []
        ends = self.chip_send(near[1], [(1, 0), (2, 3)])
        return [jnp.where(self.at_end, ends, self.chip_send(array, [(1, 2), (2, 1)]))]

    def spread(self, array):
        near = self.spread_near(array)
        return [array] + near + self.spread_far(array, near)

    def collect_near(self, parts):
        if not self.four:
            return [
                self.chip_swap(parts[mask].astype(BF), mask) for mask in range(1, self.chips)
            ]
        return self.collect_ends(parts) + self.collect_beside(parts)

    def collect_ends(self, parts):
        return [self.chip_send(parts[3].astype(BF), [(0, 1), (3, 2)])] if self.four else []

    def collect_beside(self, parts):
        if not self.four:
            return self.collect_near(parts)
        return [
            self.chip_swap(parts[1].astype(BF), 1),
            self.chip_send(parts[3].astype(BF), [(1, 2), (2, 1)]),
        ]

    def collect_far(self, parts, near):
        if not self.four:
            return near
        passed = parts[2].astype(F32) + near[0].astype(F32)
        return near[1:] + [self.chip_swap(passed.astype(BF), 2)]

    def collect_sum(self, own, arrived):
        total = own.astype(F32)
        for array in arrived:
            total = total + array.astype(F32)
        return total

    def in_order(self, pieces):
        block = jnp.concatenate(pieces, axis=0)
        rows, columns = block.shape
        bit = 1
        while bit < self.copies:
            split = block.reshape(self.copies // (2 * bit), 2, rows // self.copies * bit, columns)
            flipped = jnp.concatenate([split[:, 1:], split[:, :1]], axis=1)
            block = jnp.where((self.copy // bit) % 2 == 1, flipped, split).reshape(rows, columns)
            bit *= 2
        return block

    def swap_copies(self, array):
        if self.copies != 4:
            return [array] + [self.copy_swap(array, mask) for mask in range(1, self.copies)]
        half = array.shape[0] // 2
        first, second = self.copy_swap(array, 1), self.copy_swap(array, 2)
        last = [self.copy_swap(second[:half], 1), self.copy_swap(first[half:], 2)]
        return [array, first, second, jnp.concatenate(last, axis=0)]

    def lay_out(self, shard, shard_other, lane, lane_other, copies):
        rows, columns = shard.shape
        share = rows // copies
        chips, count = self.chips, self.count
        where = jnp.stack(
            [self.chip, self.core, self.copy if copies > 1 else 0]
            + [self.owner(j) for j in range(1, chips)]
        ).astype(jnp.int32)

        def kernel(at_ref, shard_ref, other_ref, lane_ref, lane_other_ref, whole_ref):
            core = at_ref[1]
            for side, (own, far) in enumerate(
                ((shard_ref, lane_ref), (other_ref, lane_other_ref))
            ):
                on = core if side == 0 else 1 - core
                base = pl.multiple_of((2 * at_ref[0] + on) * rows, rows)
                whole_ref[pl.ds(base, rows), :] = own[...]
                for j in range(1, chips):
                    base = (2 * at_ref[2 + j] + on) * rows
                    for mask in range(copies):
                        spot = pl.multiple_of(
                            base + jnp.bitwise_xor(at_ref[2], mask) * share, share
                        )
                        start = (mask * (chips - 1) + j - 1) * share
                        whole_ref[pl.ds(spot, share), :] = far[start : start + share, :]

        return pl.pallas_call(
            kernel,
            out_shape=jax.ShapeDtypeStruct((count * rows, columns), shard.dtype),
            in_specs=[pl.BlockSpec(memory_space=pltpu.SMEM)]
            + [pl.BlockSpec(memory_space=pltpu.VMEM)] * 4,
            out_specs=pl.BlockSpec(memory_space=pltpu.VMEM),
            name="lay_out",
        )(where, shard, shard_other, lane, lane_other)

    def own_share(self, shard):
        share = shard.shape[0] // self.copies
        return lax.dynamic_slice_in_dim(shard, self.copy * share, share, 0)

    def along_chain(self, own):
        return jnp.concatenate(self.spread(own)[1:], axis=0)

    def across_copies(self, slots):
        return jnp.concatenate(self.swap_copies(slots), axis=0)

    def lanes(self, whole):
        rows = whole.shape[0] // self.count
        split = whole.reshape(self.chips, 2, rows, whole.shape[1])
        return [
            lax.dynamic_index_in_dim(split, core, 1, keepdims=False).reshape(-1, whole.shape[1])
            for core in (self.core, 1 - self.core)
        ]

    def lane_columns(self, whole, core):
        columns = whole.shape[1] // self.count
        return jnp.concatenate(
            [
                lax.dynamic_slice_in_dim(whole, (2 * chip + core) * columns, columns, 1)
                for chip in range(self.chips)
            ],
            axis=1,
        )

    def lane_parts(self, mine, arrived):
        rows = arrived[0].shape[0] // self.chips

        def part(chip):
            sums = [
                lax.dynamic_slice_in_dim(own, chip * rows, rows, 0).astype(F32)
                + lax.dynamic_slice_in_dim(other, chip * rows, rows, 0).astype(F32)
                for own, other in zip(mine, arrived)
            ]
            return jnp.concatenate(sums, axis=-1).astype(BF)

        return [part(self.owner(j)) for j in range(self.chips)]

    def copies_sum(self, array):
        share = array.shape[0] // self.copies
        array = array.astype(BF)

        def take(mask):
            return lax.dynamic_slice_in_dim(array, (self.copy ^ mask) * share, share, 0)

        total = take(0).astype(F32)
        for mask in range(1, self.copies):
            total = total + self.copy_swap(take(mask), mask).astype(F32)
        return total.astype(BF)

    def copies_all(self, total):
        return self.in_order(
            [total] + [self.copy_swap(total, mask) for mask in range(1, self.copies)]
        )


def half_specs(units, width, tile):
    tiles = units // tile
    return [
        pl.BlockSpec((tile, width), lambda i: (jnp.minimum(i, tiles - 1), 0)),
        pl.BlockSpec((tile, width), lambda i: (jnp.maximum(i - tiles, 0), 0)),
    ]


def gelu_parts(value):
    inner = GELU_SCALE * (value + GELU_CUBIC * value * value * value)
    bent = jnp.tanh(inner)
    slope = GELU_SCALE * (1.0 + 3.0 * GELU_CUBIC * value * value)
    return 0.5 * value * (1.0 + bent), 0.5 * (1.0 + bent) + 0.5 * value * (1.0 - bent * bent) * slope


def stack_rows(refs):
    values = [ref[...] for ref in refs]
    return values[0] if len(values) == 1 else jnp.concatenate(values, axis=0)


def ffn_block(blocks, gates, ups, downs, sum_type):
    (piece, width), count = blocks[0].shape, len(blocks)
    rows = piece * count
    units = gates[0].shape[0]
    tile = min(units, 512)
    tiles = units // tile

    def kernel(*refs):
        x_refs, (g0, g1, u0, u1, d0, d1) = refs[:count], refs[count : count + 6]
        sum_refs = refs[count + 6 : 2 * count + 6]
        hid_ref, gate_ref, up_ref, total = refs[2 * count + 6 :]
        step = pl.program_id(0)

        def work(g_ref, u_ref, d_ref):
            x = stack_rows(x_refs)
            gate, up = back_dot(x, g_ref[...]), back_dot(x, u_ref[...])
            bent = jnp.tanh(GELU_SCALE * (gate + GELU_CUBIC * gate * gate * gate))
            hidden = (0.5 * gate * (1.0 + bent) * up).astype(BF)
            hid_ref[...] = hidden
            gate_ref[...] = gate.astype(BF)
            up_ref[...] = up.astype(BF)
            return dot(hidden, d_ref[...])

        @pl.when(step == 0)
        def _():
            total[...] = work(g0, u0, d0)

        @pl.when(jnp.logical_and(step > 0, step < tiles))
        def _():
            total[...] += work(g0, u0, d0)

        @pl.when(step >= tiles)
        def _():
            total[...] += work(g1, u1, d1)

        @pl.when(step == 2 * tiles - 1)
        def _():
            for i, sum_ref in enumerate(sum_refs):
                sum_ref[...] = total[i * piece : (i + 1) * piece, :].astype(sum_type)

    whole = pl.BlockSpec((piece, width), lambda i: (0, 0))
    part = pl.BlockSpec((rows, tile), lambda i: (0, i))
    *sums, hidden, gate, up = pl.pallas_call(
        kernel,
        grid=(2 * tiles,),
        in_specs=[whole] * count + half_specs(units, width, tile) * 3,
        out_specs=[whole] * count + [part] * 3,
        out_shape=[jax.ShapeDtypeStruct((piece, width), sum_type)] * count
        + [jax.ShapeDtypeStruct((rows, 2 * units), BF)] * 3,
        scratch_shapes=[pltpu.VMEM((rows, width), F32)],
        cost_estimate=pl.CostEstimate(
            flops=12 * rows * width * units,
            bytes_accessed=12 * units * width + 12 * rows * units + 6 * rows * width,
            transcendentals=2 * rows * units,
        ),
        name="ffn_block",
    )(*blocks, *gates, *ups, *downs)
    return sums, hidden, gate, up


def ffn_block_back(grads, gate, up, gates, ups, downs, sum_type):
    (piece, width), count = grads[0].shape, len(grads)
    rows = piece * count
    units = gates[0].shape[0]
    tile = min(units, 512)
    tiles = units // tile

    def kernel(*refs):
        x_refs, (gate_ref, up_ref) = refs[:count], refs[count : count + 2]
        g0, g1, u0, u1, d0, d1 = refs[count + 2 : count + 8]
        sum_refs = refs[count + 8 : 2 * count + 8]
        dg_ref, du_ref, total = refs[2 * count + 8 :]
        step = pl.program_id(0)

        def work(g_ref, u_ref, d_ref):
            value, slope = gelu_parts(gate_ref[...].astype(F32))
            hidden = back_dot(stack_rows(x_refs), d_ref[...])
            grad_gate = (hidden * up_ref[...].astype(F32) * slope).astype(BF)
            grad_up = (hidden * value).astype(BF)
            dg_ref[...] = grad_gate
            du_ref[...] = grad_up
            return dot(grad_gate, g_ref[...]) + dot(grad_up, u_ref[...])

        @pl.when(step == 0)
        def _():
            total[...] = work(g0, u0, d0)

        @pl.when(jnp.logical_and(step > 0, step < tiles))
        def _():
            total[...] += work(g0, u0, d0)

        @pl.when(step >= tiles)
        def _():
            total[...] += work(g1, u1, d1)

        @pl.when(step == 2 * tiles - 1)
        def _():
            for i, sum_ref in enumerate(sum_refs):
                sum_ref[...] = total[i * piece : (i + 1) * piece, :].astype(sum_type)

    whole = pl.BlockSpec((piece, width), lambda i: (0, 0))
    part = pl.BlockSpec((rows, tile), lambda i: (0, i))
    *sums, grad_gate, grad_up = pl.pallas_call(
        kernel,
        grid=(2 * tiles,),
        in_specs=[whole] * count + [part, part] + half_specs(units, width, tile) * 3,
        out_specs=[whole] * count + [part] * 2,
        out_shape=[jax.ShapeDtypeStruct((piece, width), sum_type)] * count
        + [jax.ShapeDtypeStruct((rows, 2 * units), BF)] * 2,
        scratch_shapes=[pltpu.VMEM((rows, width), F32)],
        cost_estimate=pl.CostEstimate(
            flops=12 * rows * width * units,
            bytes_accessed=12 * units * width + 16 * rows * units + 6 * rows * width,
            transcendentals=2 * rows * units,
        ),
        name="ffn_block_back",
    )(*grads, gate, up, *gates, *ups, *downs)
    return sums, grad_gate, grad_up


def outer_blocks(lefts, rights, start, columns, added=None, whole=None, place=0, places=1):
    width = rights[0].shape[1]
    tile = min(columns, 256)
    n_left, tiles = len(lefts), columns // tile
    n_both = n_left + len(rights)

    def kernel(*refs):
        out_ref = refs[-1]
        total = outer_sum(stack_rows(refs[:n_left]), stack_rows(refs[n_left:n_both]))
        if added is not None:
            total = total + refs[n_both][...].astype(F32)
        out_ref[...] = total.astype(BF)

    rows = sum(left.shape[0] for left in lefts)
    operands = [*lefts, *rights]
    specs = [pl.BlockSpec((left.shape[0], tile), lambda i: (0, i + start // tile)) for left in lefts]
    specs += [pl.BlockSpec(right.shape, lambda i: (0, 0)) for right in rights]
    if added is not None:
        operands.append(added)
        specs.append(pl.BlockSpec((tile, width), lambda i: (i, 0)))
    aliases = {}
    if whole is not None:
        aliases = {len(operands): 0}
        operands.append(whole)
        specs.append(pl.BlockSpec(memory_space=pl.ANY))
    return pl.pallas_call(
        kernel,
        grid=(tiles,),
        in_specs=specs,
        out_specs=pl.BlockSpec((tile, width), lambda i: (i + place * tiles, 0)),
        out_shape=jax.ShapeDtypeStruct((places * columns, width), BF),
        input_output_aliases=aliases,
        cost_estimate=pl.CostEstimate(
            flops=2 * rows * columns * width,
            bytes_accessed=2 * rows * (columns + width) + 4 * columns * width,
            transcendentals=0,
        ),
        name="outer_blocks",
    )(*operands)


def split_pair(pair):
    units, _, width = pair.shape
    rows = min(units, 128)

    def kernel(pair_ref, first_ref, second_ref):
        first_ref[...] = pair_ref[:, 0, :].astype(BF)
        second_ref[...] = pair_ref[:, 1, :].astype(BF)

    flat = pl.BlockSpec((rows, width), lambda i: (i, 0))
    return pl.pallas_call(
        kernel,
        grid=(units // rows,),
        in_specs=[pl.BlockSpec((rows, 2, width), lambda i: (i, 0, 0))],
        out_specs=[flat, flat],
        out_shape=[jax.ShapeDtypeStruct((units, width), BF)] * 2,
        cost_estimate=pl.CostEstimate(
            flops=0, bytes_accessed=units * width * 12, transcendentals=0
        ),
        name="split_pair",
    )(pair)


def join_pair(stacked, units):
    width = stacked.shape[1]
    rows = min(units, 128)
    tiles = units // rows

    def kernel(first_ref, second_ref, pair_ref):
        pair_ref[:, 0, :] = first_ref[...].astype(F32)
        pair_ref[:, 1, :] = second_ref[...].astype(F32)

    return pl.pallas_call(
        kernel,
        grid=(tiles,),
        in_specs=[
            pl.BlockSpec((rows, width), lambda i: (i, 0)),
            pl.BlockSpec((rows, width), lambda i: (i + tiles, 0)),
        ],
        out_specs=pl.BlockSpec((rows, 2, width), lambda i: (i, 0, 0)),
        out_shape=jax.ShapeDtypeStruct((units, 2, width), F32),
        cost_estimate=pl.CostEstimate(
            flops=0, bytes_accessed=units * width * 12, transcendentals=0
        ),
        name="join_pair",
    )(stacked, stacked)


def tie(*values):
    return lax.optimization_barrier(values)


def body(
    tokens,
    layer_input,
    cotangent,
    norm_gains,
    qk_gains,
    w_qkv,
    w_out,
    laurel_left,
    laurel_right,
    w_gate_up,
    w_down,
    pli_gate,
    pli_proj,
):
    at = Place()
    device = at.device
    rows_dev, width = tokens.shape
    shard = w_qkv.shape[0]
    prompt_len = PROMPT_DEVS * rows_dev
    q_cols = H * HD
    lr, pd = laurel_left.shape[1], pli_gate.shape[1]
    n_gain, n_qk = norm_gains.size, qk_gains.size

    def pack_gains(norm_part, qk_part):
        flat = jnp.concatenate([norm_part.reshape(-1), qk_part.reshape(-1)]).astype(BF)
        flat = jnp.pad(flat, (0, shard * 128 - flat.size))
        return flat.reshape(shard, 128)

    kv_pack = jnp.concatenate(
        [w_qkv[:, q_cols:].astype(BF), pack_gains(norm_gains, qk_gains)], axis=1
    )
    def gather_all(array):
        return lax.all_gather(at.own_share(array), ("fsdp", "rep"), axis=0, tiled=True)

    main_all = gather_all(
        jnp.concatenate(
            [
                w_qkv[:, :q_cols].astype(BF),
                w_out.astype(BF),
                laurel_left.astype(BF),
                laurel_right.astype(BF).reshape(shard, lr),
            ],
            axis=1,
        )
    )
    q_all = main_all[:, :q_cols]
    out_all = main_all[:, q_cols : q_cols + width]
    left_all = main_all[:, q_cols + width : q_cols + width + lr]
    right_all = main_all[:, q_cols + width + lr :].reshape(lr, width)
    pli_pack_all = gather_all(
        jnp.concatenate([pli_gate.astype(BF), pli_proj.astype(BF).reshape(shard, pd)], axis=1)
    )
    w_gate, w_up = split_pair(w_gate_up)
    w_down_bf = w_down.astype(BF)
    own_wide = (w_gate, w_up, w_down_bf)
    kv_twin = at.core_swap(kv_pack)
    kv_near = at.spread_near(kv_pack)
    kv_near, kv_twin, own_wide = tie(kv_near, kv_twin, own_wide)
    kv_far = at.spread_far(kv_pack, kv_near)
    their_wide = [at.core_swap(own) for own in own_wide]
    kv_lane = jnp.concatenate(kv_near + kv_far, axis=0)
    kv_all = at.lay_out(kv_pack, kv_twin, kv_lane, at.core_swap(kv_lane), 1)
    kv_weight = kv_all[:, : 2 * KVH * HD]
    gain_rows_all = kv_all[:, 2 * KVH * HD :].reshape(at.count, -1)[:, : n_gain + n_qk]
    gains = jnp.moveaxis(
        gain_rows_all[:, :n_gain].reshape(at.count, norm_gains.shape[0], -1), 0, 1
    ).reshape(norm_gains.shape[0], -1).astype(F32)
    qk_gain = jnp.moveaxis(
        gain_rows_all[:, n_gain:].reshape(at.count, qk_gains.shape[0], -1), 0, 1
    ).reshape(qk_gains.shape[0], -1).astype(F32)
    inputs = tokens.astype(F32)
    extra_input = layer_input.astype(F32)

    def input_norm(tensor, gain_rows):
        return rms_norm(tensor) * gain_rows[0]

    normed, input_pull = jax.vjp(input_norm, inputs, gains)
    normed_bf = normed.astype(BF)
    local_rows = jnp.arange(rows_dev, dtype=jnp.int32)
    places = jnp.where(
        device < PROMPT_DEVS, device * rows_dev + local_rows, prompt_len + local_rows % CONT_LEN
    )

    half = HD // 2
    frequency = THETA_BASE ** (-(jnp.arange(half, dtype=F32) * 2.0 / HD))
    angles = places.astype(F32)[:, None] * frequency
    cosine, sine = jnp.cos(angles), jnp.sin(angles)
    kv_proj = dot(normed_bf, kv_weight)
    kv_own = kv_prep(kv_proj, cosine, sine, qk_gain)

    prompt_chips = PROMPT_DEVS // 2
    if at.four:
        arrived = at.chip_send(kv_own, [(0, 2), (1, 3)])
        even = jnp.where(at.chip < prompt_chips, kv_own, arrived)
        odd = at.chip_swap(even, 1)
        kv_lane = [jnp.where(at.chip % 2 == i, even, odd) for i in range(2)]
    else:
        blocks = [kv_own] + [
            at.chip_send(kv_own, [(i, (i - j) % at.chips) for i in range(prompt_chips)])
            for j in range(1, at.chips)
        ]
        kv_lane = []
        for block in range(prompt_chips):
            seen = kv_own
            for j in range(1, at.chips):
                seen = jnp.where((at.chip + j) % at.chips == block, blocks[j], seen)
            kv_lane.append(seen)
    q_proj = dot(normed_bf, q_all)
    laurel_mid = dot(normed_bf, left_all).astype(BF)
    laurel_out = dot(laurel_mid, right_all)
    kv_lane, own_wide, their_wide, q_proj, laurel_out = tie(
        jnp.stack(kv_lane), own_wide, their_wide, q_proj, laurel_out
    )
    halves = list(zip(own_wide, their_wide))
    (gate_halves, up_halves, down_halves) = halves

    kv_other = at.core_swap(kv_lane)
    kv_pairs = [row for i in range(prompt_chips) for row in at.by_core(kv_lane[i], kv_other[i])]
    kv_seen = jnp.concatenate(kv_pairs + [kv_own], axis=0)
    queries_bf, attended_bf = attend(q_proj, cosine, sine, qk_gain, kv_seen, device)
    pgate_all = pli_pack_all[:, :pd]
    pproj_all = pli_pack_all[:, pd:].reshape(pd, width)
    attn_proj = dot(attended_bf, out_all)

    def middle(inputs, normed, attn_proj, laurel_out, gain_rows):
        first_sum = inputs + rms_norm(attn_proj) * gain_rows[1]
        laurel_sum = normed + rms_norm(laurel_out) * gain_rows[2]
        stream = (first_sum + laurel_sum) * HALF_ROOT
        return (stream, rms_norm(stream) * gain_rows[3])

    (stream, ffn_in), middle_pull = jax.vjp(middle, inputs, normed, attn_proj, laurel_out, gains)

    piece = rows_dev // CHUNKS
    units = w_down.shape[0]

    def staged(rows, work, extra=()):
        near = at.spread_near(rows)
        first = work(0, [rows], F32)
        near, first, extra = tie(near, first, extra)
        far = at.spread_far(rows, near)
        pairs = [near[i : i + 2] for i in range(0, len(near), 2)]
        second = [work(j + 1, blocks, BF) for j, blocks in enumerate(pairs)]
        far, second = tie(far, second)
        parts = [part for sums, *_ in second for part in sums]
        back = [at.chip_swap(part, j + 1) for j, part in enumerate(parts)]
        done = [first, *second]
        last = None
        if far:
            third = work(len(done), far, BF)
            first_back, third = tie(back[0], third)
            back[0] = first_back
            done.append(third)
            last = third[0][0]
        return first[0][0], back, last, [kept for _, kept in done], extra

    def ffn_forward(rows, extra):
        def work(j, blocks, sum_type):
            sums, *kept = ffn_block(blocks, gate_halves, up_halves, down_halves, sum_type)
            return sums, (blocks, *kept)

        own, back, last, kept, extra = staged(rows, work, extra)
        if last is not None:
            back = back + [at.chip_swap(last, at.chips - 1)]
        return at.collect_sum(own, back), kept, extra

    def ffn_backward(rows, kept):
        def work(j, grads, sum_type):
            blocks, hidden, gate, up = kept[j]
            sums, grad_gate, grad_up = ffn_block_back(
                grads, gate, up, gate_halves, up_halves, down_halves, sum_type
            )
            return sums, (blocks, hidden, grads, grad_gate, grad_up)

        return staged(rows, work)

    def tail_norm(stream, ffn_out, gain_rows):
        return stream + rms_norm(ffn_out) * gain_rows[4]

    def pli_mix(pli_pre, extra_input):
        return jax.nn.gelu(pli_pre, approximate=True) * extra_input

    def final_norm(after_ffn, pli_out, gain_rows):
        return after_ffn + rms_norm(pli_out) * gain_rows[5]

    cuts = [slice(i * piece, (i + 1) * piece) for i in range(CHUNKS)]
    core, other_core = at.core, 1 - at.core
    lanes = [
        at.lane_columns(rows, side) for rows in (attended_bf, normed_bf) for side in (core, other_core)
    ]
    forwards = []
    for cut in cuts:
        ffn_out, kept, lanes = ffn_forward(ffn_in[cut].astype(BF), lanes)
        forwards.append((ffn_out, kept))
    attended_mine, attended_other, normed_mine, normed_other = lanes
    gain_total = 0.0
    results, extras, streams, ins, all_grads = [], [], [], [], []
    pli_rows = []
    for cut, (ffn_out, kept) in zip(cuts, forwards):
        after_ffn, tail_pull = jax.vjp(tail_norm, stream[cut], ffn_out, gains)
        after_bf = after_ffn.astype(BF)
        pli_mid, pli_pull = jax.vjp(pli_mix, dot(after_bf, pgate_all), extra_input[cut])
        pli_mid_bf = pli_mid.astype(BF)
        result, final_pull = jax.vjp(final_norm, after_ffn, dot(pli_mid_bf, pproj_all), gains)
        grad_after, grad_pli_out, gain_final = final_pull(cotangent[cut].astype(F32))
        grad_pli_out_bf = grad_pli_out.astype(BF)
        grad_pli_pre, grad_extra = pli_pull(back_dot(grad_pli_out_bf, pproj_all))
        grad_pli_pre_bf = grad_pli_pre.astype(BF)
        grad_after = grad_after + back_dot(grad_pli_pre_bf, pgate_all)
        grad_stream, grad_ffn_out, gain_tail = tail_pull(grad_after)
        own, back, last, grads, _ = ffn_backward(grad_ffn_out.astype(BF), kept)
        gain_total = gain_total + gain_final + gain_tail
        results.append(result.astype(BF))
        extras.append(grad_extra)
        streams.append(grad_stream)
        ins.append((own, back, last))
        all_grads.append(grads)
        pli_rows.append((pli_mid_bf, grad_pli_out_bf, after_bf, grad_pli_pre_bf))

    kept = [[group[i] for grads in all_grads for group in grads] for i in range(5)]
    hiddens, gates, ups = kept[1], kept[3], kept[4]
    ins_blocks, outs_grad = [[block for blocks in kept[i] for block in blocks] for i in (0, 2)]
    lasts = [last for _, _, last in ins if last is not None]
    lasts, pli_rows, hiddens, gates, ups = tie(lasts, pli_rows, hiddens, gates, ups)
    pairs = [(hiddens, outs_grad), (gates, ins_blocks), (ups, ins_blocks)]
    theirs = [
        outer_blocks(lefts, rights, units, units) for lefts, rights in pairs
    ]
    mids, pli_outs, afters, pres = [jnp.concatenate(rows, axis=0) for rows in zip(*pli_rows)]
    grad_pproj = outer_blocks([mids], [pli_outs], 0, pd)
    grad_pgate = outer_blocks([afters], [pres], 0, width)
    lasts = [at.chip_swap(last, at.chips - 1) for last in lasts]
    backs = [back for _, back, _ in ins]
    backs, lasts, theirs, grad_pproj, grad_pgate = tie(
        backs, lasts, theirs, grad_pproj, grad_pgate
    )
    grad_pproj = grad_pproj.reshape(-1, pd)
    ends = [[last] for last in lasts] or [[]] * len(ins)
    ins = [at.collect_sum(own, back + end) for (own, _, _), back, end in zip(ins, backs, ends)]

    grad_inputs, grad_normed, grad_attn_proj, grad_laurel_out, gain_middle = middle_pull(
        (jnp.concatenate(streams, axis=0), jnp.concatenate(ins, axis=0))
    )
    grad_attn_bf = grad_attn_proj.astype(BF)
    out_leaving = at.core_swap(outer_sum(attended_other, grad_attn_bf).astype(BF))
    out_mine = outer_sum(attended_mine, grad_attn_bf).astype(BF)
    grad_laurel_bf = grad_laurel_out.astype(BF)
    grad_right_w = outer_sum(laurel_mid, grad_laurel_bf).astype(BF).reshape(-1, lr)
    grad_mid_bf = back_dot(grad_laurel_bf, right_all).astype(BF)
    grad_left_w = outer_sum(normed_bf, grad_mid_bf).astype(BF)
    small_mine, small_leaving = at.lanes(
        jnp.concatenate([grad_left_w, grad_right_w, grad_pgate, grad_pproj], axis=1)
    )
    small_leaving = at.core_swap(small_leaving)
    their_down = at.core_swap(theirs[0])
    out_leaving, small_leaving, out_mine, small_mine, theirs, their_down, grad_attn_bf = tie(
        out_leaving, small_leaving, out_mine, small_mine, theirs, their_down, grad_attn_bf
    )
    out_parts = at.lane_parts([out_mine, small_mine], [out_leaving, small_leaving])
    out_ends = at.collect_ends(out_parts)
    theirs = [at.core_swap(their) for their in theirs[1:]]
    grad_q_bf, key_grad, value_grad, q_gain_rows = attend_back(
        q_proj, queries_bf, cosine, sine, qk_gain, kv_seen, grad_attn_bf, main_all, device
    )
    down_w = outer_blocks(*pairs[0], 0, units, their_down)
    out_ends, theirs, out_parts, grad_q_bf, key_grad, value_grad, down_w = tie(
        out_ends, theirs, out_parts, grad_q_bf, key_grad, value_grad, down_w
    )
    down_part = lax.psum_scatter(down_w, "rep", scatter_dimension=0, tiled=True)
    out_beside = at.collect_beside(out_parts)
    out_near = out_ends + out_beside
    wide_w = None
    for place, ((lefts, rights), their) in enumerate(zip(pairs[1:], theirs)):
        wide_w = outer_blocks(lefts, rights, 0, units, their, wide_w, place, 2)

    def kv_rows(first, core):
        begin = (2 * first + core) * rows_dev
        return jnp.concatenate(
            [
                lax.dynamic_slice_in_dim(grad, begin, rows_dev, 0).astype(BF)
                for grad in (key_grad, value_grad)
            ],
            axis=1,
        )

    kv_other = at.core_swap(
        jnp.stack([kv_rows(chip, other_core) for chip in range(prompt_chips)])
    )

    def kv_part(chip):
        index = jnp.clip(chip, 0, prompt_chips - 1)
        theirs = lax.dynamic_index_in_dim(kv_other, index, 0, keepdims=False)
        return kv_rows(index, core).astype(F32) + theirs.astype(F32)

    offsets = [0, 1] if at.four else range(at.chips)
    kv_parts = [
        kv_part((at.chip + j) % 2 if at.four else (at.chip + j) % at.chips) for j in offsets
    ]
    q_other_w = outer_blocks([normed_other], [grad_q_bf], 0, width // 2)
    q_mine = outer_blocks([normed_mine], [grad_q_bf], 0, width // 2)
    kv_parts, out_near, wide_w, q_other_w, q_mine = tie(
        kv_parts, out_near, wide_w, q_other_w, q_mine
    )
    wide_part = lax.psum_scatter(wide_w, "rep", scatter_dimension=0, tiled=True)
    if at.four:
        pair_sum = kv_parts[0] + at.chip_swap(kv_parts[1].astype(BF), 1).astype(F32)
        pair_sum, out_near, down_part = tie(pair_sum, out_near, down_part)
        prompt_parts = [at.chip_send(pair_sum.astype(BF), [(2, 0), (3, 1)])]
    else:
        pair_sum = kv_parts[0]
        prompt_parts = [
            at.chip_send(
                kv_parts[j].astype(BF), [((i - j) % at.chips, i) for i in range(prompt_chips)]
            )
            for j in range(1, at.chips)
        ]
    q_leaving = at.core_swap(q_other_w)
    out_far = at.collect_far(out_parts, out_near)
    down_sum = lax.all_gather(down_part, "rep", axis=0, tiled=True)
    prompt_parts, pair_sum, q_leaving = tie(prompt_parts, pair_sum, q_leaving)
    q_parts = at.lane_parts([q_mine], [q_leaving])
    q_near = at.collect_near(q_parts)
    prompt_sum = pair_sum
    for sent in prompt_parts:
        prompt_sum = prompt_sum + sent.astype(F32)
    kv_sum = jnp.where(
        device < PROMPT_DEVS,
        prompt_sum,
        jnp.concatenate([key_grad[prompt_len:], value_grad[prompt_len:]], axis=1),
    )
    grad_kv_bf, k_gain_row = kv_prep_back(kv_proj, kv_sum, cosine, sine, qk_gain)
    kv_other_w = outer_sum(normed_other, grad_kv_bf).astype(BF)
    kv_mine = outer_sum(normed_mine, grad_kv_bf).astype(BF)
    grad_normed = grad_normed + back_dot(grad_mid_bf, left_all)
    grad_normed = grad_normed + back_dot(grad_q_bf, q_all) + back_dot(grad_kv_bf, kv_weight)
    grad_first, gain_input = input_pull(grad_normed)
    grad_tokens = grad_inputs + grad_first
    gain_total = gain_total + gain_middle + gain_input
    qk_total = jnp.concatenate([jnp.sum(q_gain_rows, axis=0), k_gain_row], axis=0)

    def by_owner(array):
        return jnp.moveaxis(array.reshape(array.shape[0], at.count, -1), 1, 0).reshape(at.count, -1)

    gain_pack = jnp.concatenate([by_owner(gain_total), by_owner(qk_total)], axis=1).astype(BF)
    gain_pack = jnp.pad(gain_pack, ((0, 0), (0, shard * 128 - gain_pack.shape[1])))
    gain_mine, gain_leaving = at.lanes(gain_pack.reshape(-1, 128))
    out_far, q_near, kv_other_w, kv_mine, gain_mine, gain_leaving, grad_tokens, wide_part = tie(
        out_far, q_near, kv_other_w, kv_mine, gain_mine, gain_leaving, grad_tokens, wide_part
    )
    wide_sum = lax.all_gather(wide_part, "rep", axis=0, tiled=True)
    out_ready = at.collect_sum(out_parts[0], out_far).astype(BF)
    q_far = at.collect_far(q_parts, q_near)
    kv_leaving, gain_leaving, out_ready = tie(
        at.core_swap(kv_other_w), at.core_swap(gain_leaving), out_ready
    )
    kv_w_parts = at.lane_parts([kv_mine, gain_mine], [kv_leaving, gain_leaving])
    kv_near = at.collect_near(kv_w_parts)
    out_total = at.copies_sum(out_ready)
    q_far, kv_near, out_total, down_sum = tie(q_far, kv_near, out_total, down_sum)
    kv_far = at.collect_far(kv_w_parts, kv_near)
    q_total = at.copies_sum(at.collect_sum(q_parts[0], q_far))
    out_sum = at.copies_all(out_total)
    grad_down = down_sum.astype(F32)
    kv_far, q_total, out_sum, grad_down = tie(kv_far, q_total, out_sum, grad_down)
    kv_total = at.copies_sum(at.collect_sum(kv_w_parts[0], kv_far))
    q_sum = at.copies_all(q_total)
    kv_total, q_sum = tie(kv_total, q_sum)
    grad_gate_up = join_pair(wide_sum, units)
    kv_sum_w = at.copies_all(kv_total)
    gain_out = kv_sum_w[:, 2 * KVH * HD :].reshape(-1)
    return (
        jnp.concatenate(results, axis=0),
        grad_tokens,
        jnp.concatenate(extras, axis=0),
        gain_out[:n_gain].reshape(norm_gains.shape).astype(F32),
        gain_out[n_gain : n_gain + n_qk].reshape(qk_gains.shape).astype(F32),
        jnp.concatenate([q_sum, kv_sum_w[:, : 2 * KVH * HD]], axis=1).astype(F32),
        out_sum[:, :width].astype(F32),
        out_sum[:, width : width + lr].astype(F32),
        out_sum[:, width + lr : width + 2 * lr].reshape(laurel_right.shape).astype(F32),
        grad_gate_up,
        grad_down,
        out_sum[:, width + 2 * lr : width + 2 * lr + pd].astype(F32),
        out_sum[:, width + 2 * lr + pd :].reshape(pli_proj.shape).astype(F32),
    )


def solution(mesh):
    placed = (
        P(("rep", "fsdp"), None),
        P(("rep", "fsdp"), None),
        P(("rep", "fsdp"), None),
        P(None, "fsdp"),
        P(None, "fsdp"),
        P("fsdp", None),
        P("fsdp", None),
        P("fsdp", None),
        P("fsdp", None),
        P("fsdp", None, None),
        P("fsdp", None),
        P("fsdp", None),
        P("fsdp", None),
    )
    return jax.shard_map(
        body,
        mesh=mesh,
        in_specs=placed,
        out_specs=(
            P(("rep", "fsdp"), None),
            P(("rep", "fsdp"), None),
            P(("rep", "fsdp"), None),
            P(None, "fsdp"),
            P(None, "fsdp"),
            P("fsdp", None),
            P("fsdp", None),
            P("fsdp", None),
            P("fsdp", None),
            P("fsdp", None, None),
            P("fsdp", None),
            P("fsdp", None),
            P("fsdp", None),
        ),
        check_vma=False,
    )
```

```python
import jax
import jax.numpy as jnp
from jax import lax
from jax.experimental import pallas as pl
from jax.experimental.pallas import tpu as pltpu
from jax.sharding import PartitionSpec as P

H = 8
KVH = 2
HD = 256
CONT_LEN = 256
PROMPT_DEVS = 4
CHUNKS = 1

EPSILON = 1e-06
THETA_BASE = 1000000.0
HALF_ROOT = 0.7071067811865476
NEG_FILL = -1e30
GELU_SCALE = 0.7978845608028654
GELU_CUBIC = 0.044715
BF = jnp.bfloat16
F32 = jnp.float32


def rms_norm(tensor):
    return tensor * lax.rsqrt(jnp.mean(tensor * tensor, axis=-1, keepdims=True) + EPSILON)


def dot(left_mat, right_mat):
    return jnp.dot(left_mat, right_mat, preferred_element_type=F32)


def outer_sum(left_mat, right_mat):
    return lax.dot_general(
        left_mat, right_mat, (((0,), (0,)), ((), ())), preferred_element_type=F32
    )


def back_dot(gradient, weight):
    return lax.dot_general(
        gradient, weight, (((1,), (1,)), ((), ())), preferred_element_type=F32
    )


def turn(tensor, cosine, sine, back=False):
    half = tensor.shape[-1] // 2
    first, second = tensor[:, :half], tensor[:, half:]
    if back:
        return jnp.concatenate(
            [first * cosine + second * sine, second * cosine - first * sine], axis=-1
        )
    return jnp.concatenate(
        [first * cosine - second * sine, second * cosine + first * sine], axis=-1
    )


def head_norm(tensor):
    inverse = lax.rsqrt(jnp.mean(tensor * tensor, axis=-1, keepdims=True) + EPSILON)
    return tensor * inverse, inverse


def head_norm_back(normed, inverse, gradient):
    return inverse * (gradient - normed * jnp.mean(gradient * normed, axis=-1, keepdims=True))


def head_shares(queries, keys, device):
    rows, key_count = queries.shape[0], keys.shape[0]
    prompt_len = key_count - rows
    scores = back_dot(queries, keys)
    local = lax.broadcasted_iota(jnp.int32, scores.shape, 0)
    index = lax.broadcasted_iota(jnp.int32, scores.shape, 1)
    own = index - prompt_len
    in_prompt = device < PROMPT_DEVS
    last_seen = jnp.where(in_prompt, device * rows, prompt_len) + local
    allowed = index <= last_seen
    if rows > CONT_LEN:
        piece = jnp.logical_or(own < 0, own // CONT_LEN == local // CONT_LEN)
        allowed = jnp.logical_and(allowed, piece)
    scores = jnp.where(allowed, scores, NEG_FILL)
    grown = jnp.exp(scores - jnp.max(scores, axis=-1, keepdims=True))
    return grown / jnp.sum(grown, axis=-1, keepdims=True)


def head_specs(rows, key_count):
    head = pl.BlockSpec((rows, HD), lambda h: (0, h))
    half = pl.BlockSpec((rows, HD // 2), lambda h: (0, 0))
    gain = pl.BlockSpec((2, HD), lambda h: (0, 0))
    keys = pl.BlockSpec((key_count, HD), lambda h: (0, h // (H // KVH)))
    values = pl.BlockSpec((key_count, HD), lambda h: (0, KVH + h // (H // KVH)))
    return head, half, gain, keys, values


def attend(projected, cosine, sine, gains, kv_seen, device):
    rows, key_count = projected.shape[0], kv_seen.shape[0]
    head, half, gain, keys, values = head_specs(rows, key_count)

    def kernel(at_ref, x_ref, c_ref, s_ref, g_ref, k_ref, v_ref, q_ref, o_ref):
        normed, _ = head_norm(x_ref[...])
        queries = turn(normed * g_ref[0:1, :], c_ref[...], s_ref[...]).astype(BF)
        q_ref[...] = queries
        shares = head_shares(queries, k_ref[...], at_ref[0])
        o_ref[...] = dot(shares.astype(BF), v_ref[...]).astype(BF)

    return pl.pallas_call(
        kernel,
        grid=(H,),
        in_specs=[pl.BlockSpec(memory_space=pltpu.SMEM), head, half, half, gain, keys, values],
        out_specs=[head, head],
        out_shape=[jax.ShapeDtypeStruct((rows, H * HD), BF)] * 2,
        cost_estimate=pl.CostEstimate(
            flops=4 * rows * H * HD * key_count,
            bytes_accessed=rows * H * HD * 8 + key_count * KVH * HD * 4,
            transcendentals=rows * H * key_count,
        ),
        name="attend",
    )(device.reshape(1), projected, cosine, sine, gains, kv_seen, kv_seen)


def attend_back(projected, queries, cosine, sine, gains, kv_seen, gradient, weights, device):
    rows, key_count = projected.shape[0], kv_seen.shape[0]
    groups = H // KVH
    width = gradient.shape[1]
    head, half, gain, keys, values = head_specs(rows, key_count)

    def kernel(
        at_ref, x_ref, q_ref, c_ref, s_ref, g_ref, k_ref, v_ref, do_ref, w_ref,
        dx_ref, dk_ref, dv_ref, dg_ref,
    ):
        queries = q_ref[...]
        grad = back_dot(do_ref[...], w_ref[...]).astype(BF)
        shares = head_shares(queries, k_ref[...], at_ref[0])
        grad_shares = back_dot(grad, v_ref[...])
        inner = jnp.sum(shares * grad_shares, axis=-1, keepdims=True)
        grad_scores = (shares * (grad_shares - inner)).astype(BF)
        key_grad = outer_sum(grad_scores, queries)
        value_grad = outer_sum(shares.astype(BF), grad)
        first = lax.rem(pl.program_id(0), groups) == 0

        @pl.when(first)
        def _():
            dk_ref[...] = key_grad
            dv_ref[...] = value_grad

        @pl.when(jnp.logical_not(first))
        def _():
            dk_ref[...] += key_grad
            dv_ref[...] += value_grad

        turned = turn(dot(grad_scores, k_ref[...]), c_ref[...], s_ref[...], back=True)
        normed, inverse = head_norm(x_ref[...])
        dg_ref[...] = jnp.sum(turned * normed, axis=0, keepdims=True)[None]
        dx_ref[...] = head_norm_back(normed, inverse, turned * g_ref[0:1, :]).astype(BF)

    shared = pl.BlockSpec((key_count, HD), lambda h: (0, h // groups))
    return pl.pallas_call(
        kernel,
        grid=(H,),
        in_specs=[
            pl.BlockSpec(memory_space=pltpu.SMEM), head, head, half, half, gain, keys, values,
            pl.BlockSpec((rows, width), lambda h: (0, 0)),
            pl.BlockSpec((HD, width), lambda h: (h, H * HD // width)),
        ],
        out_specs=[head, shared, shared, pl.BlockSpec((1, 1, HD), lambda h: (h, 0, 0))],
        out_shape=[
            jax.ShapeDtypeStruct((rows, H * HD), BF),
            jax.ShapeDtypeStruct((key_count, KVH * HD), F32),
            jax.ShapeDtypeStruct((key_count, KVH * HD), F32),
            jax.ShapeDtypeStruct((H, 1, HD), F32),
        ],
        cost_estimate=pl.CostEstimate(
            flops=10 * rows * H * HD * key_count,
            bytes_accessed=rows * H * HD * 10 + key_count * KVH * HD * 12,
            transcendentals=rows * H * key_count,
        ),
        name="attend_back",
    )(
        device.reshape(1), projected, queries, cosine, sine, gains, kv_seen, kv_seen, gradient, weights,
    )


def kv_prep(projected, cosine, sine, gains):
    rows = projected.shape[0]

    def kernel(x_ref, c_ref, s_ref, g_ref, out_ref):
        for head in range(2 * KVH):
            columns = slice(head * HD, (head + 1) * HD)
            normed, _ = head_norm(x_ref[:, columns])
            if head < KVH:
                normed = turn(normed * g_ref[1:2, :], c_ref[...], s_ref[...])
            out_ref[:, columns] = normed.astype(BF)

    return pl.pallas_call(
        kernel,
        out_shape=jax.ShapeDtypeStruct((rows, 2 * KVH * HD), BF),
        name="kv_prep",
    )(projected, cosine, sine, gains)


def kv_prep_back(projected, gradient, cosine, sine, gains):
    rows = projected.shape[0]

    def kernel(x_ref, d_ref, c_ref, s_ref, g_ref, dx_ref, dg_ref):
        gain_grad = jnp.zeros((1, HD), F32)
        for head in range(2 * KVH):
            columns = slice(head * HD, (head + 1) * HD)
            normed, inverse = head_norm(x_ref[:, columns])
            grad = d_ref[:, columns]
            if head < KVH:
                grad = turn(grad, c_ref[...], s_ref[...], back=True)
                gain_grad = gain_grad + jnp.sum(grad * normed, axis=0, keepdims=True)
                grad = grad * g_ref[1:2, :]
            dx_ref[:, columns] = head_norm_back(normed, inverse, grad).astype(BF)
        dg_ref[...] = gain_grad

    return pl.pallas_call(
        kernel,
        out_shape=[
            jax.ShapeDtypeStruct((rows, 2 * KVH * HD), BF),
            jax.ShapeDtypeStruct((1, HD), F32),
        ],
        name="kv_prep_back",
    )(projected, gradient, cosine, sine, gains)


class Place:
    def __init__(self):
        self.count = lax.axis_size("fsdp")
        self.copies = lax.axis_size("rep")
        self.device = lax.axis_index("fsdp")
        self.copy = lax.axis_index("rep")
        self.chips = self.count // 2
        self.chip = self.device // 2
        self.core = self.device % 2
        self.at_end = jnp.logical_or(self.chip == 0, self.chip == self.chips - 1)
        self.four = self.chips == 4

    def core_swap(self, array):
        return lax.ppermute(array, "fsdp", [(i, i ^ 1) for i in range(self.count)])

    def copy_swap(self, array, mask):
        return lax.ppermute(array, "rep", [(i, i ^ mask) for i in range(self.copies)])

    def chip_send(self, array, moves):
        pairs = [(2 * a + core, 2 * b + core) for a, b in moves for core in range(2)]
        return lax.ppermute(array, "fsdp", pairs)

    def by_core(self, mine, other):
        first = self.core == 0
        return jnp.where(first, mine, other), jnp.where(first, other, mine)

    def owner(self, j):
        return self.chip ^ j

    def chip_swap(self, array, mask):
        return self.chip_send(array, [(i, i ^ mask) for i in range(self.chips)])

    def spread_near(self, array):
        if not self.four:
            return [self.chip_swap(array, mask) for mask in range(1, self.chips)]
        return [self.chip_swap(array, 1), self.chip_swap(array, 2)]

    def spread_far(self, array, near):
        if not self.four:
            return []
        ends = self.chip_send(near[1], [(1, 0), (2, 3)])
        return [jnp.where(self.at_end, ends, self.chip_send(array, [(1, 2), (2, 1)]))]

    def spread(self, array):
        near = self.spread_near(array)
        return [array] + near + self.spread_far(array, near)

    def collect_near(self, parts):
        if not self.four:
            return [
                self.chip_swap(parts[mask].astype(BF), mask) for mask in range(1, self.chips)
            ]
        return self.collect_ends(parts) + self.collect_beside(parts)

    def collect_ends(self, parts):
        return [self.chip_send(parts[3].astype(BF), [(0, 1), (3, 2)])] if self.four else []

    def collect_beside(self, parts):
        if not self.four:
            return self.collect_near(parts)
        return [
            self.chip_swap(parts[1].astype(BF), 1),
            self.chip_send(parts[3].astype(BF), [(1, 2), (2, 1)]),
        ]

    def collect_far(self, parts, near):
        if not self.four:
            return near
        passed = parts[2].astype(F32) + near[0].astype(F32)
        return near[1:] + [self.chip_swap(passed.astype(BF), 2)]

    def collect_sum(self, own, arrived):
        total = own.astype(F32)
        for array in arrived:
            total = total + array.astype(F32)
        return total

    def in_order(self, pieces):
        block = jnp.concatenate(pieces, axis=0)
        rows, columns = block.shape
        bit = 1
        while bit < self.copies:
            split = block.reshape(self.copies // (2 * bit), 2, rows // self.copies * bit, columns)
            flipped = jnp.concatenate([split[:, 1:], split[:, :1]], axis=1)
            block = jnp.where((self.copy // bit) % 2 == 1, flipped, split).reshape(rows, columns)
            bit *= 2
        return block

    def swap_copies(self, array):
        if self.copies != 4:
            return [array] + [self.copy_swap(array, mask) for mask in range(1, self.copies)]
        half = array.shape[0] // 2
        first, second = self.copy_swap(array, 1), self.copy_swap(array, 2)
        last = [self.copy_swap(second[:half], 1), self.copy_swap(first[half:], 2)]
        return [array, first, second, jnp.concatenate(last, axis=0)]

    def lay_out(self, shard, shard_other, lane, lane_other, copies):
        rows, columns = shard.shape
        share = rows // copies
        chips, count = self.chips, self.count
        where = jnp.stack(
            [self.chip, self.core, self.copy if copies > 1 else 0]
            + [self.owner(j) for j in range(1, chips)]
        ).astype(jnp.int32)

        def kernel(at_ref, shard_ref, other_ref, lane_ref, lane_other_ref, whole_ref):
            core = at_ref[1]
            for side, (own, far) in enumerate(
                ((shard_ref, lane_ref), (other_ref, lane_other_ref))
            ):
                on = core if side == 0 else 1 - core
                base = pl.multiple_of((2 * at_ref[0] + on) * rows, rows)
                whole_ref[pl.ds(base, rows), :] = own[...]
                for j in range(1, chips):
                    base = (2 * at_ref[2 + j] + on) * rows
                    for mask in range(copies):
                        spot = pl.multiple_of(
                            base + jnp.bitwise_xor(at_ref[2], mask) * share, share
                        )
                        start = (mask * (chips - 1) + j - 1) * share
                        whole_ref[pl.ds(spot, share), :] = far[start : start + share, :]

        return pl.pallas_call(
            kernel,
            out_shape=jax.ShapeDtypeStruct((count * rows, columns), shard.dtype),
            in_specs=[pl.BlockSpec(memory_space=pltpu.SMEM)]
            + [pl.BlockSpec(memory_space=pltpu.VMEM)] * 4,
            out_specs=pl.BlockSpec(memory_space=pltpu.VMEM),
            name="lay_out",
        )(where, shard, shard_other, lane, lane_other)

    def own_share(self, shard):
        share = shard.shape[0] // self.copies
        return lax.dynamic_slice_in_dim(shard, self.copy * share, share, 0)

    def along_chain(self, own):
        return jnp.concatenate(self.spread(own)[1:], axis=0)

    def across_copies(self, slots):
        return jnp.concatenate(self.swap_copies(slots), axis=0)

    def lanes(self, whole):
        rows = whole.shape[0] // self.count
        split = whole.reshape(self.chips, 2, rows, whole.shape[1])
        return [
            lax.dynamic_index_in_dim(split, core, 1, keepdims=False).reshape(-1, whole.shape[1])
            for core in (self.core, 1 - self.core)
        ]

    def lane_columns(self, whole, core):
        columns = whole.shape[1] // self.count
        return jnp.concatenate(
            [
                lax.dynamic_slice_in_dim(whole, (2 * chip + core) * columns, columns, 1)
                for chip in range(self.chips)
            ],
            axis=1,
        )

    def lane_parts(self, mine, arrived):
        rows = arrived[0].shape[0] // self.chips

        def part(chip):
            sums = [
                lax.dynamic_slice_in_dim(own, chip * rows, rows, 0).astype(F32)
                + lax.dynamic_slice_in_dim(other, chip * rows, rows, 0).astype(F32)
                for own, other in zip(mine, arrived)
            ]
            return jnp.concatenate(sums, axis=-1).astype(BF)

        return [part(self.owner(j)) for j in range(self.chips)]

    def copies_sum(self, array):
        share = array.shape[0] // self.copies
        array = array.astype(BF)

        def take(mask):
            return lax.dynamic_slice_in_dim(array, (self.copy ^ mask) * share, share, 0)

        total = take(0).astype(F32)
        for mask in range(1, self.copies):
            total = total + self.copy_swap(take(mask), mask).astype(F32)
        return total.astype(BF)

    def copies_all(self, total):
        return self.in_order(
            [total] + [self.copy_swap(total, mask) for mask in range(1, self.copies)]
        )


def half_specs(units, width, tile):
    tiles = units // tile
    return [
        pl.BlockSpec((tile, width), lambda i: (jnp.minimum(i, tiles - 1), 0)),
        pl.BlockSpec((tile, width), lambda i: (jnp.maximum(i - tiles, 0), 0)),
    ]


def gelu_parts(value):
    inner = GELU_SCALE * (value + GELU_CUBIC * value * value * value)
    bent = jnp.tanh(inner)
    slope = GELU_SCALE * (1.0 + 3.0 * GELU_CUBIC * value * value)
    return 0.5 * value * (1.0 + bent), 0.5 * (1.0 + bent) + 0.5 * value * (1.0 - bent * bent) * slope


def stack_rows(refs):
    values = [ref[...] for ref in refs]
    return values[0] if len(values) == 1 else jnp.concatenate(values, axis=0)


def ffn_block(blocks, gates, ups, downs, sum_type):
    (piece, width), count = blocks[0].shape, len(blocks)
    rows = piece * count
    units = gates[0].shape[0]
    tile = min(units, 512)
    tiles = units // tile

    def kernel(*refs):
        x_refs, (g0, g1, u0, u1, d0, d1) = refs[:count], refs[count : count + 6]
        sum_refs = refs[count + 6 : 2 * count + 6]
        hid_ref, gate_ref, up_ref, total = refs[2 * count + 6 :]
        step = pl.program_id(0)

        def work(g_ref, u_ref, d_ref):
            x = stack_rows(x_refs)
            gate, up = back_dot(x, g_ref[...]), back_dot(x, u_ref[...])
            bent = jnp.tanh(GELU_SCALE * (gate + GELU_CUBIC * gate * gate * gate))
            hidden = (0.5 * gate * (1.0 + bent) * up).astype(BF)
            hid_ref[...] = hidden
            gate_ref[...] = gate.astype(BF)
            up_ref[...] = up.astype(BF)
            return dot(hidden, d_ref[...])

        @pl.when(step == 0)
        def _():
            total[...] = work(g0, u0, d0)

        @pl.when(jnp.logical_and(step > 0, step < tiles))
        def _():
            total[...] += work(g0, u0, d0)

        @pl.when(step >= tiles)
        def _():
            total[...] += work(g1, u1, d1)

        @pl.when(step == 2 * tiles - 1)
        def _():
            for i, sum_ref in enumerate(sum_refs):
                sum_ref[...] = total[i * piece : (i + 1) * piece, :].astype(sum_type)

    whole = pl.BlockSpec((piece, width), lambda i: (0, 0))
    part = pl.BlockSpec((rows, tile), lambda i: (0, i))
    *sums, hidden, gate, up = pl.pallas_call(
        kernel,
        grid=(2 * tiles,),
        in_specs=[whole] * count + half_specs(units, width, tile) * 3,
        out_specs=[whole] * count + [part] * 3,
        out_shape=[jax.ShapeDtypeStruct((piece, width), sum_type)] * count
        + [jax.ShapeDtypeStruct((rows, 2 * units), BF)] * 3,
        scratch_shapes=[pltpu.VMEM((rows, width), F32)],
        cost_estimate=pl.CostEstimate(
            flops=12 * rows * width * units,
            bytes_accessed=12 * units * width + 12 * rows * units + 6 * rows * width,
            transcendentals=2 * rows * units,
        ),
        name="ffn_block",
    )(*blocks, *gates, *ups, *downs)
    return sums, hidden, gate, up


def ffn_block_back(grads, gate, up, gates, ups, downs, sum_type):
    (piece, width), count = grads[0].shape, len(grads)
    rows = piece * count
    units = gates[0].shape[0]
    tile = min(units, 512)
    tiles = units // tile

    def kernel(*refs):
        x_refs, (gate_ref, up_ref) = refs[:count], refs[count : count + 2]
        g0, g1, u0, u1, d0, d1 = refs[count + 2 : count + 8]
        sum_refs = refs[count + 8 : 2 * count + 8]
        dg_ref, du_ref, total = refs[2 * count + 8 :]
        step = pl.program_id(0)

        def work(g_ref, u_ref, d_ref):
            value, slope = gelu_parts(gate_ref[...].astype(F32))
            hidden = back_dot(stack_rows(x_refs), d_ref[...])
            grad_gate = (hidden * up_ref[...].astype(F32) * slope).astype(BF)
            grad_up = (hidden * value).astype(BF)
            dg_ref[...] = grad_gate
            du_ref[...] = grad_up
            return dot(grad_gate, g_ref[...]) + dot(grad_up, u_ref[...])

        @pl.when(step == 0)
        def _():
            total[...] = work(g0, u0, d0)

        @pl.when(jnp.logical_and(step > 0, step < tiles))
        def _():
            total[...] += work(g0, u0, d0)

        @pl.when(step >= tiles)
        def _():
            total[...] += work(g1, u1, d1)

        @pl.when(step == 2 * tiles - 1)
        def _():
            for i, sum_ref in enumerate(sum_refs):
                sum_ref[...] = total[i * piece : (i + 1) * piece, :].astype(sum_type)

    whole = pl.BlockSpec((piece, width), lambda i: (0, 0))
    part = pl.BlockSpec((rows, tile), lambda i: (0, i))
    *sums, grad_gate, grad_up = pl.pallas_call(
        kernel,
        grid=(2 * tiles,),
        in_specs=[whole] * count + [part, part] + half_specs(units, width, tile) * 3,
        out_specs=[whole] * count + [part] * 2,
        out_shape=[jax.ShapeDtypeStruct((piece, width), sum_type)] * count
        + [jax.ShapeDtypeStruct((rows, 2 * units), BF)] * 2,
        scratch_shapes=[pltpu.VMEM((rows, width), F32)],
        cost_estimate=pl.CostEstimate(
            flops=12 * rows * width * units,
            bytes_accessed=12 * units * width + 16 * rows * units + 6 * rows * width,
            transcendentals=2 * rows * units,
        ),
        name="ffn_block_back",
    )(*grads, gate, up, *gates, *ups, *downs)
    return sums, grad_gate, grad_up


def outer_blocks(lefts, rights, start, columns, added=None, whole=None, place=0, places=1):
    width = rights[0].shape[1]
    tile = min(columns, 256)
    n_left, tiles = len(lefts), columns // tile
    n_both = n_left + len(rights)

    def kernel(*refs):
        out_ref = refs[-1]
        total = outer_sum(stack_rows(refs[:n_left]), stack_rows(refs[n_left:n_both]))
        if added is not None:
            total = total + refs[n_both][...].astype(F32)
        out_ref[...] = total.astype(BF)

    rows = sum(left.shape[0] for left in lefts)
    operands = [*lefts, *rights]
    specs = [pl.BlockSpec((left.shape[0], tile), lambda i: (0, i + start // tile)) for left in lefts]
    specs += [pl.BlockSpec(right.shape, lambda i: (0, 0)) for right in rights]
    if added is not None:
        operands.append(added)
        specs.append(pl.BlockSpec((tile, width), lambda i: (i, 0)))
    aliases = {}
    if whole is not None:
        aliases = {len(operands): 0}
        operands.append(whole)
        specs.append(pl.BlockSpec(memory_space=pl.ANY))
    return pl.pallas_call(
        kernel,
        grid=(tiles,),
        in_specs=specs,
        out_specs=pl.BlockSpec((tile, width), lambda i: (i + place * tiles, 0)),
        out_shape=jax.ShapeDtypeStruct((places * columns, width), BF),
        input_output_aliases=aliases,
        cost_estimate=pl.CostEstimate(
            flops=2 * rows * columns * width,
            bytes_accessed=2 * rows * (columns + width) + 4 * columns * width,
            transcendentals=0,
        ),
        name="outer_blocks",
    )(*operands)


def split_pair(pair):
    units, _, width = pair.shape
    rows = min(units, 128)

    def kernel(pair_ref, first_ref, second_ref):
        first_ref[...] = pair_ref[:, 0, :].astype(BF)
        second_ref[...] = pair_ref[:, 1, :].astype(BF)

    flat = pl.BlockSpec((rows, width), lambda i: (i, 0))
    return pl.pallas_call(
        kernel,
        grid=(units // rows,),
        in_specs=[pl.BlockSpec((rows, 2, width), lambda i: (i, 0, 0))],
        out_specs=[flat, flat],
        out_shape=[jax.ShapeDtypeStruct((units, width), BF)] * 2,
        cost_estimate=pl.CostEstimate(
            flops=0, bytes_accessed=units * width * 12, transcendentals=0
        ),
        name="split_pair",
    )(pair)


def join_pair(stacked, units):
    width = stacked.shape[1]
    rows = min(units, 128)
    tiles = units // rows

    def kernel(first_ref, second_ref, pair_ref):
        pair_ref[:, 0, :] = first_ref[...].astype(F32)
        pair_ref[:, 1, :] = second_ref[...].astype(F32)

    return pl.pallas_call(
        kernel,
        grid=(tiles,),
        in_specs=[
            pl.BlockSpec((rows, width), lambda i: (i, 0)),
            pl.BlockSpec((rows, width), lambda i: (i + tiles, 0)),
        ],
        out_specs=pl.BlockSpec((rows, 2, width), lambda i: (i, 0, 0)),
        out_shape=jax.ShapeDtypeStruct((units, 2, width), F32),
        cost_estimate=pl.CostEstimate(
            flops=0, bytes_accessed=units * width * 12, transcendentals=0
        ),
        name="join_pair",
    )(stacked, stacked)


def tie(*values):
    return lax.optimization_barrier(values)


def body(
    tokens,
    layer_input,
    cotangent,
    norm_gains,
    qk_gains,
    w_qkv,
    w_out,
    laurel_left,
    laurel_right,
    w_gate_up,
    w_down,
    pli_gate,
    pli_proj,
):
    at = Place()
    device = at.device
    rows_dev, width = tokens.shape
    shard = w_qkv.shape[0]
    prompt_len = PROMPT_DEVS * rows_dev
    q_cols = H * HD
    lr, pd = laurel_left.shape[1], pli_gate.shape[1]
    n_gain, n_qk = norm_gains.size, qk_gains.size

    def pack_gains(norm_part, qk_part):
        flat = jnp.concatenate([norm_part.reshape(-1), qk_part.reshape(-1)]).astype(BF)
        flat = jnp.pad(flat, (0, shard * 128 - flat.size))
        return flat.reshape(shard, 128)

    kv_pack = jnp.concatenate(
        [w_qkv[:, q_cols:].astype(BF), pack_gains(norm_gains, qk_gains)], axis=1
    )
    def gather_all(array):
        return lax.all_gather(at.own_share(array), ("fsdp", "rep"), axis=0, tiled=True)

    main_all = gather_all(
        jnp.concatenate(
            [
                w_qkv[:, :q_cols].astype(BF),
                w_out.astype(BF),
                laurel_left.astype(BF),
                laurel_right.astype(BF).reshape(shard, lr),
            ],
            axis=1,
        )
    )
    q_all = main_all[:, :q_cols]
    out_all = main_all[:, q_cols : q_cols + width]
    left_all = main_all[:, q_cols + width : q_cols + width + lr]
    right_all = main_all[:, q_cols + width + lr :].reshape(lr, width)
    pli_pack_all = gather_all(
        jnp.concatenate([pli_gate.astype(BF), pli_proj.astype(BF).reshape(shard, pd)], axis=1)
    )
    w_gate, w_up = split_pair(w_gate_up)
    w_down_bf = w_down.astype(BF)
    own_wide = (w_gate, w_up, w_down_bf)
    kv_twin = at.core_swap(kv_pack)
    kv_near = at.spread_near(kv_pack)
    kv_near, kv_twin, own_wide = tie(kv_near, kv_twin, own_wide)
    kv_far = at.spread_far(kv_pack, kv_near)
    their_wide = [at.core_swap(own) for own in own_wide]
    kv_lane = jnp.concatenate(kv_near + kv_far, axis=0)
    kv_all = at.lay_out(kv_pack, kv_twin, kv_lane, at.core_swap(kv_lane), 1)
    kv_weight = kv_all[:, : 2 * KVH * HD]
    gain_rows_all = kv_all[:, 2 * KVH * HD :].reshape(at.count, -1)[:, : n_gain + n_qk]
    gains = jnp.moveaxis(
        gain_rows_all[:, :n_gain].reshape(at.count, norm_gains.shape[0], -1), 0, 1
    ).reshape(norm_gains.shape[0], -1).astype(F32)
    qk_gain = jnp.moveaxis(
        gain_rows_all[:, n_gain:].reshape(at.count, qk_gains.shape[0], -1), 0, 1
    ).reshape(qk_gains.shape[0], -1).astype(F32)
    inputs = tokens.astype(F32)
    extra_input = layer_input.astype(F32)

    def input_norm(tensor, gain_rows):
        return rms_norm(tensor) * gain_rows[0]

    normed, input_pull = jax.vjp(input_norm, inputs, gains)
    normed_bf = normed.astype(BF)
    local_rows = jnp.arange(rows_dev, dtype=jnp.int32)
    places = jnp.where(
        device < PROMPT_DEVS, device * rows_dev + local_rows, prompt_len + local_rows % CONT_LEN
    )

    half = HD // 2
    frequency = THETA_BASE ** (-(jnp.arange(half, dtype=F32) * 2.0 / HD))
    angles = places.astype(F32)[:, None] * frequency
    cosine, sine = jnp.cos(angles), jnp.sin(angles)
    kv_proj = dot(normed_bf, kv_weight)
    kv_own = kv_prep(kv_proj, cosine, sine, qk_gain)

    prompt_chips = PROMPT_DEVS // 2
    if at.four:
        arrived = at.chip_send(kv_own, [(0, 2), (1, 3)])
        even = jnp.where(at.chip < prompt_chips, kv_own, arrived)
        odd = at.chip_swap(even, 1)
        kv_lane = [jnp.where(at.chip % 2 == i, even, odd) for i in range(2)]
    else:
        blocks = [kv_own] + [
            at.chip_send(kv_own, [(i, (i - j) % at.chips) for i in range(prompt_chips)])
            for j in range(1, at.chips)
        ]
        kv_lane = []
        for block in range(prompt_chips):
            seen = kv_own
            for j in range(1, at.chips):
                seen = jnp.where((at.chip + j) % at.chips == block, blocks[j], seen)
            kv_lane.append(seen)
    q_proj = dot(normed_bf, q_all)
    laurel_mid = dot(normed_bf, left_all).astype(BF)
    laurel_out = dot(laurel_mid, right_all)
    kv_lane, own_wide, their_wide, q_proj, laurel_out = tie(
        jnp.stack(kv_lane), own_wide, their_wide, q_proj, laurel_out
    )
    halves = list(zip(own_wide, their_wide))
    (gate_halves, up_halves, down_halves) = halves

    kv_other = at.core_swap(kv_lane)
    kv_pairs = [row for i in range(prompt_chips) for row in at.by_core(kv_lane[i], kv_other[i])]
    kv_seen = jnp.concatenate(kv_pairs + [kv_own], axis=0)
    queries_bf, attended_bf = attend(q_proj, cosine, sine, qk_gain, kv_seen, device)
    pgate_all = pli_pack_all[:, :pd]
    pproj_all = pli_pack_all[:, pd:].reshape(pd, width)
    attn_proj = dot(attended_bf, out_all)

    def middle(inputs, normed, attn_proj, laurel_out, gain_rows):
        first_sum = inputs + rms_norm(attn_proj) * gain_rows[1]
        laurel_sum = normed + rms_norm(laurel_out) * gain_rows[2]
        stream = (first_sum + laurel_sum) * HALF_ROOT
        return (stream, rms_norm(stream) * gain_rows[3])

    (stream, ffn_in), middle_pull = jax.vjp(middle, inputs, normed, attn_proj, laurel_out, gains)

    piece = rows_dev // CHUNKS
    units = w_down.shape[0]

    def staged(rows, work, extra=()):
        near = at.spread_near(rows)
        first = work(0, [rows], F32)
        near, first, extra = tie(near, first, extra)
        far = at.spread_far(rows, near)
        pairs = [near[i : i + 2] for i in range(0, len(near), 2)]
        second = [work(j + 1, blocks, BF) for j, blocks in enumerate(pairs)]
        far, second = tie(far, second)
        parts = [part for sums, *_ in second for part in sums]
        back = [at.chip_swap(part, j + 1) for j, part in enumerate(parts)]
        done = [first, *second]
        last = None
        if far:
            third = work(len(done), far, BF)
            first_back, third = tie(back[0], third)
            back[0] = first_back
            done.append(third)
            last = third[0][0]
        return first[0][0], back, last, [kept for _, kept in done], extra

    def ffn_forward(rows, extra):
        def work(j, blocks, sum_type):
            sums, *kept = ffn_block(blocks, gate_halves, up_halves, down_halves, sum_type)
            return sums, (blocks, *kept)

        own, back, last, kept, extra = staged(rows, work, extra)
        if last is not None:
            back = back + [at.chip_swap(last, at.chips - 1)]
        return at.collect_sum(own, back), kept, extra

    def ffn_backward(rows, kept):
        def work(j, grads, sum_type):
            blocks, hidden, gate, up = kept[j]
            sums, grad_gate, grad_up = ffn_block_back(
                grads, gate, up, gate_halves, up_halves, down_halves, sum_type
            )
            return sums, (blocks, hidden, grads, grad_gate, grad_up)

        return staged(rows, work)

    def tail_norm(stream, ffn_out, gain_rows):
        return stream + rms_norm(ffn_out) * gain_rows[4]

    def pli_mix(pli_pre, extra_input):
        return jax.nn.gelu(pli_pre, approximate=True) * extra_input

    def final_norm(after_ffn, pli_out, gain_rows):
        return after_ffn + rms_norm(pli_out) * gain_rows[5]

    cuts = [slice(i * piece, (i + 1) * piece) for i in range(CHUNKS)]
    core, other_core = at.core, 1 - at.core
    lanes = [
        at.lane_columns(rows, side) for rows in (attended_bf, normed_bf) for side in (core, other_core)
    ]
    forwards = []
    for cut in cuts:
        ffn_out, kept, lanes = ffn_forward(ffn_in[cut].astype(BF), lanes)
        forwards.append((ffn_out, kept))
    attended_mine, attended_other, normed_mine, normed_other = lanes
    gain_total = 0.0
    results, extras, streams, ins, all_grads = [], [], [], [], []
    pli_rows = []
    for cut, (ffn_out, kept) in zip(cuts, forwards):
        after_ffn, tail_pull = jax.vjp(tail_norm, stream[cut], ffn_out, gains)
        after_bf = after_ffn.astype(BF)
        pli_mid, pli_pull = jax.vjp(pli_mix, dot(after_bf, pgate_all), extra_input[cut])
        pli_mid_bf = pli_mid.astype(BF)
        result, final_pull = jax.vjp(final_norm, after_ffn, dot(pli_mid_bf, pproj_all), gains)
        grad_after, grad_pli_out, gain_final = final_pull(cotangent[cut].astype(F32))
        grad_pli_out_bf = grad_pli_out.astype(BF)
        grad_pli_pre, grad_extra = pli_pull(back_dot(grad_pli_out_bf, pproj_all))
        grad_pli_pre_bf = grad_pli_pre.astype(BF)
        grad_after = grad_after + back_dot(grad_pli_pre_bf, pgate_all)
        grad_stream, grad_ffn_out, gain_tail = tail_pull(grad_after)
        own, back, last, grads, _ = ffn_backward(grad_ffn_out.astype(BF), kept)
        gain_total = gain_total + gain_final + gain_tail
        results.append(result.astype(BF))
        extras.append(grad_extra)
        streams.append(grad_stream)
        ins.append((own, back, last))
        all_grads.append(grads)
        pli_rows.append((pli_mid_bf, grad_pli_out_bf, after_bf, grad_pli_pre_bf))

    kept = [[group[i] for grads in all_grads for group in grads] for i in range(5)]
    hiddens, gates, ups = kept[1], kept[3], kept[4]
    ins_blocks, outs_grad = [[block for blocks in kept[i] for block in blocks] for i in (0, 2)]
    lasts = [last for _, _, last in ins if last is not None]
    lasts, pli_rows, hiddens, gates, ups = tie(lasts, pli_rows, hiddens, gates, ups)
    pairs = [(hiddens, outs_grad), (gates, ins_blocks), (ups, ins_blocks)]
    theirs = [
        outer_blocks(lefts, rights, units, units) for lefts, rights in pairs
    ]
    mids, pli_outs, afters, pres = [jnp.concatenate(rows, axis=0) for rows in zip(*pli_rows)]
    grad_pproj = outer_blocks([mids], [pli_outs], 0, pd)
    grad_pgate = outer_blocks([afters], [pres], 0, width)
    lasts = [at.chip_swap(last, at.chips - 1) for last in lasts]
    backs = [back for _, back, _ in ins]
    backs, lasts, theirs, grad_pproj, grad_pgate = tie(
        backs, lasts, theirs, grad_pproj, grad_pgate
    )
    grad_pproj = grad_pproj.reshape(-1, pd)
    ends = [[last] for last in lasts] or [[]] * len(ins)
    ins = [at.collect_sum(own, back + end) for (own, _, _), back, end in zip(ins, backs, ends)]

    grad_inputs, grad_normed, grad_attn_proj, grad_laurel_out, gain_middle = middle_pull(
        (jnp.concatenate(streams, axis=0), jnp.concatenate(ins, axis=0))
    )
    grad_attn_bf = grad_attn_proj.astype(BF)
    out_leaving = at.core_swap(outer_sum(attended_other, grad_attn_bf).astype(BF))
    out_mine = outer_sum(attended_mine, grad_attn_bf).astype(BF)
    grad_laurel_bf = grad_laurel_out.astype(BF)
    grad_right_w = outer_sum(laurel_mid, grad_laurel_bf).astype(BF).reshape(-1, lr)
    grad_mid_bf = back_dot(grad_laurel_bf, right_all).astype(BF)
    grad_left_w = outer_sum(normed_bf, grad_mid_bf).astype(BF)
    small_mine, small_leaving = at.lanes(
        jnp.concatenate([grad_left_w, grad_right_w, grad_pgate, grad_pproj], axis=1)
    )
    small_leaving = at.core_swap(small_leaving)
    their_down = at.core_swap(theirs[0])
    out_leaving, small_leaving, out_mine, small_mine, theirs, their_down, grad_attn_bf = tie(
        out_leaving, small_leaving, out_mine, small_mine, theirs, their_down, grad_attn_bf
    )
    out_parts = at.lane_parts([out_mine, small_mine], [out_leaving, small_leaving])
    out_ends = at.collect_ends(out_parts)
    theirs = [at.core_swap(their) for their in theirs[1:]]
    grad_q_bf, key_grad, value_grad, q_gain_rows = attend_back(
        q_proj, queries_bf, cosine, sine, qk_gain, kv_seen, grad_attn_bf, main_all, device
    )
    down_w = outer_blocks(*pairs[0], 0, units, their_down)
    out_ends, theirs, out_parts, grad_q_bf, key_grad, value_grad, down_w = tie(
        out_ends, theirs, out_parts, grad_q_bf, key_grad, value_grad, down_w
    )
    down_part = lax.psum_scatter(down_w, "rep", scatter_dimension=0, tiled=True)
    out_beside = at.collect_beside(out_parts)
    out_near = out_ends + out_beside
    wide_w = None
    for place, ((lefts, rights), their) in enumerate(zip(pairs[1:], theirs)):
        wide_w = outer_blocks(lefts, rights, 0, units, their, wide_w, place, 2)

    def kv_rows(first, core):
        begin = (2 * first + core) * rows_dev
        return jnp.concatenate(
            [
                lax.dynamic_slice_in_dim(grad, begin, rows_dev, 0).astype(BF)
                for grad in (key_grad, value_grad)
            ],
            axis=1,
        )

    kv_other = at.core_swap(
        jnp.stack([kv_rows(chip, other_core) for chip in range(prompt_chips)])
    )

    def kv_part(chip):
        index = jnp.clip(chip, 0, prompt_chips - 1)
        theirs = lax.dynamic_index_in_dim(kv_other, index, 0, keepdims=False)
        return kv_rows(index, core).astype(F32) + theirs.astype(F32)

    offsets = [0, 1] if at.four else range(at.chips)
    kv_parts = [
        kv_part((at.chip + j) % 2 if at.four else (at.chip + j) % at.chips) for j in offsets
    ]
    q_other_w = outer_blocks([normed_other], [grad_q_bf], 0, width // 2)
    q_mine = outer_blocks([normed_mine], [grad_q_bf], 0, width // 2)
    kv_parts, out_near, wide_w, q_other_w, q_mine = tie(
        kv_parts, out_near, wide_w, q_other_w, q_mine
    )
    wide_part = lax.psum_scatter(wide_w, "rep", scatter_dimension=0, tiled=True)
    if at.four:
        pair_sum = kv_parts[0] + at.chip_swap(kv_parts[1].astype(BF), 1).astype(F32)
        pair_sum, out_near, down_part = tie(pair_sum, out_near, down_part)
        prompt_parts = [at.chip_send(pair_sum.astype(BF), [(2, 0), (3, 1)])]
    else:
        pair_sum = kv_parts[0]
        prompt_parts = [
            at.chip_send(
                kv_parts[j].astype(BF), [((i - j) % at.chips, i) for i in range(prompt_chips)]
            )
            for j in range(1, at.chips)
        ]
    q_leaving = at.core_swap(q_other_w)
    out_far = at.collect_far(out_parts, out_near)
    down_sum = lax.all_gather(down_part, "rep", axis=0, tiled=True)
    prompt_parts, pair_sum, q_leaving = tie(prompt_parts, pair_sum, q_leaving)
    q_parts = at.lane_parts([q_mine], [q_leaving])
    q_near = at.collect_near(q_parts)
    prompt_sum = pair_sum
    for sent in prompt_parts:
        prompt_sum = prompt_sum + sent.astype(F32)
    kv_sum = jnp.where(
        device < PROMPT_DEVS,
        prompt_sum,
        jnp.concatenate([key_grad[prompt_len:], value_grad[prompt_len:]], axis=1),
    )
    grad_kv_bf, k_gain_row = kv_prep_back(kv_proj, kv_sum, cosine, sine, qk_gain)
    kv_other_w = outer_sum(normed_other, grad_kv_bf).astype(BF)
    kv_mine = outer_sum(normed_mine, grad_kv_bf).astype(BF)
    grad_normed = grad_normed + back_dot(grad_mid_bf, left_all)
    grad_normed = grad_normed + back_dot(grad_q_bf, q_all) + back_dot(grad_kv_bf, kv_weight)
    grad_first, gain_input = input_pull(grad_normed)
    grad_tokens = grad_inputs + grad_first
    gain_total = gain_total + gain_middle + gain_input
    qk_total = jnp.concatenate([jnp.sum(q_gain_rows, axis=0), k_gain_row], axis=0)

    def by_owner(array):
        return jnp.moveaxis(array.reshape(array.shape[0], at.count, -1), 1, 0).reshape(at.count, -1)

    gain_pack = jnp.concatenate([by_owner(gain_total), by_owner(qk_total)], axis=1).astype(BF)
    gain_pack = jnp.pad(gain_pack, ((0, 0), (0, shard * 128 - gain_pack.shape[1])))
    gain_mine, gain_leaving = at.lanes(gain_pack.reshape(-1, 128))
    out_far, q_near, kv_other_w, kv_mine, gain_mine, gain_leaving, grad_tokens, wide_part = tie(
        out_far, q_near, kv_other_w, kv_mine, gain_mine, gain_leaving, grad_tokens, wide_part
    )
    wide_sum = lax.all_gather(wide_part, "rep", axis=0, tiled=True)
    out_ready = at.collect_sum(out_parts[0], out_far).astype(BF)
    q_far = at.collect_far(q_parts, q_near)
    kv_leaving, gain_leaving, out_ready = tie(
        at.core_swap(kv_other_w), at.core_swap(gain_leaving), out_ready
    )
    kv_w_parts = at.lane_parts([kv_mine, gain_mine], [kv_leaving, gain_leaving])
    kv_near = at.collect_near(kv_w_parts)
    out_total = at.copies_sum(out_ready)
    q_far, kv_near, out_total, down_sum = tie(q_far, kv_near, out_total, down_sum)
    kv_far = at.collect_far(kv_w_parts, kv_near)
    q_total = at.copies_sum(at.collect_sum(q_parts[0], q_far))
    out_sum = at.copies_all(out_total)
    kv_far, q_total, out_sum, down_sum = tie(kv_far, q_total, out_sum, down_sum)
    kv_total = at.copies_sum(at.collect_sum(kv_w_parts[0], kv_far))
    q_sum = at.copies_all(q_total)
    kv_total, q_sum, down_sum = tie(kv_total, q_sum, down_sum)
    grad_gate_up, grad_down = join_pair(wide_sum, units), down_sum.astype(F32)
    kv_sum_w = at.copies_all(kv_total)
    gain_out = kv_sum_w[:, 2 * KVH * HD :].reshape(-1)
    return (
        jnp.concatenate(results, axis=0),
        grad_tokens,
        jnp.concatenate(extras, axis=0),
        gain_out[:n_gain].reshape(norm_gains.shape).astype(F32),
        gain_out[n_gain : n_gain + n_qk].reshape(qk_gains.shape).astype(F32),
        jnp.concatenate([q_sum, kv_sum_w[:, : 2 * KVH * HD]], axis=1).astype(F32),
        out_sum[:, :width].astype(F32),
        out_sum[:, width : width + lr].astype(F32),
        out_sum[:, width + lr : width + 2 * lr].reshape(laurel_right.shape).astype(F32),
        grad_gate_up,
        grad_down,
        out_sum[:, width + 2 * lr : width + 2 * lr + pd].astype(F32),
        out_sum[:, width + 2 * lr + pd :].reshape(pli_proj.shape).astype(F32),
    )


def solution(mesh):
    placed = (
        P(("rep", "fsdp"), None),
        P(("rep", "fsdp"), None),
        P(("rep", "fsdp"), None),
        P(None, "fsdp"),
        P(None, "fsdp"),
        P("fsdp", None),
        P("fsdp", None),
        P("fsdp", None),
        P("fsdp", None),
        P("fsdp", None, None),
        P("fsdp", None),
        P("fsdp", None),
        P("fsdp", None),
    )
    return jax.shard_map(
        body,
        mesh=mesh,
        in_specs=placed,
        out_specs=(
            P(("rep", "fsdp"), None),
            P(("rep", "fsdp"), None),
            P(("rep", "fsdp"), None),
            P(None, "fsdp"),
            P(None, "fsdp"),
            P("fsdp", None),
            P("fsdp", None),
            P("fsdp", None),
            P("fsdp", None),
            P("fsdp", None, None),
            P("fsdp", None),
            P("fsdp", None),
            P("fsdp", None),
        ),
        check_vma=False,
    )
```

```python
import jax
import jax.numpy as jnp
from jax import lax
from jax.experimental import pallas as pl
from jax.experimental.pallas import tpu as pltpu
from jax.sharding import PartitionSpec as P

H = 8
KVH = 2
HD = 256
CONT_LEN = 256
PROMPT_DEVS = 4
CHUNKS = 1

EPSILON = 1e-06
THETA_BASE = 1000000.0
HALF_ROOT = 0.7071067811865476
NEG_FILL = -1e30
GELU_SCALE = 0.7978845608028654
GELU_CUBIC = 0.044715
BF = jnp.bfloat16
F32 = jnp.float32


def rms_norm(tensor):
    return tensor * lax.rsqrt(jnp.mean(tensor * tensor, axis=-1, keepdims=True) + EPSILON)


def dot(left_mat, right_mat):
    return jnp.dot(left_mat, right_mat, preferred_element_type=F32)


def outer_sum(left_mat, right_mat):
    return lax.dot_general(
        left_mat, right_mat, (((0,), (0,)), ((), ())), preferred_element_type=F32
    )


def back_dot(gradient, weight):
    return lax.dot_general(
        gradient, weight, (((1,), (1,)), ((), ())), preferred_element_type=F32
    )


def turn(tensor, cosine, sine, back=False):
    half = tensor.shape[-1] // 2
    first, second = tensor[:, :half], tensor[:, half:]
    if back:
        return jnp.concatenate(
            [first * cosine + second * sine, second * cosine - first * sine], axis=-1
        )
    return jnp.concatenate(
        [first * cosine - second * sine, second * cosine + first * sine], axis=-1
    )


def head_norm(tensor):
    inverse = lax.rsqrt(jnp.mean(tensor * tensor, axis=-1, keepdims=True) + EPSILON)
    return tensor * inverse, inverse


def head_norm_back(normed, inverse, gradient):
    return inverse * (gradient - normed * jnp.mean(gradient * normed, axis=-1, keepdims=True))


def head_shares(queries, keys, device):
    rows, key_count = queries.shape[0], keys.shape[0]
    prompt_len = key_count - rows
    scores = back_dot(queries, keys)
    local = lax.broadcasted_iota(jnp.int32, scores.shape, 0)
    index = lax.broadcasted_iota(jnp.int32, scores.shape, 1)
    own = index - prompt_len
    in_prompt = device < PROMPT_DEVS
    last_seen = jnp.where(in_prompt, device * rows, prompt_len) + local
    allowed = index <= last_seen
    if rows > CONT_LEN:
        piece = jnp.logical_or(own < 0, own // CONT_LEN == local // CONT_LEN)
        allowed = jnp.logical_and(allowed, piece)
    scores = jnp.where(allowed, scores, NEG_FILL)
    grown = jnp.exp(scores - jnp.max(scores, axis=-1, keepdims=True))
    return grown / jnp.sum(grown, axis=-1, keepdims=True)


def head_specs(rows, key_count):
    head = pl.BlockSpec((rows, HD), lambda h: (0, h))
    half = pl.BlockSpec((rows, HD // 2), lambda h: (0, 0))
    gain = pl.BlockSpec((2, HD), lambda h: (0, 0))
    keys = pl.BlockSpec((key_count, HD), lambda h: (0, h // (H // KVH)))
    values = pl.BlockSpec((key_count, HD), lambda h: (0, KVH + h // (H // KVH)))
    return head, half, gain, keys, values


def attend(projected, cosine, sine, gains, kv_seen, device):
    rows, key_count = projected.shape[0], kv_seen.shape[0]
    head, half, gain, keys, values = head_specs(rows, key_count)

    def kernel(at_ref, x_ref, c_ref, s_ref, g_ref, k_ref, v_ref, q_ref, o_ref):
        normed, _ = head_norm(x_ref[...])
        queries = turn(normed * g_ref[0:1, :], c_ref[...], s_ref[...]).astype(BF)
        q_ref[...] = queries
        shares = head_shares(queries, k_ref[...], at_ref[0])
        o_ref[...] = dot(shares.astype(BF), v_ref[...]).astype(BF)

    return pl.pallas_call(
        kernel,
        grid=(H,),
        in_specs=[pl.BlockSpec(memory_space=pltpu.SMEM), head, half, half, gain, keys, values],
        out_specs=[head, head],
        out_shape=[jax.ShapeDtypeStruct((rows, H * HD), BF)] * 2,
        cost_estimate=pl.CostEstimate(
            flops=4 * rows * H * HD * key_count,
            bytes_accessed=rows * H * HD * 8 + key_count * KVH * HD * 4,
            transcendentals=rows * H * key_count,
        ),
        name="attend",
    )(device.reshape(1), projected, cosine, sine, gains, kv_seen, kv_seen)


def attend_back(projected, queries, cosine, sine, gains, kv_seen, gradient, weights, device):
    rows, key_count = projected.shape[0], kv_seen.shape[0]
    groups = H // KVH
    width = gradient.shape[1]
    head, half, gain, keys, values = head_specs(rows, key_count)

    def kernel(
        at_ref, x_ref, q_ref, c_ref, s_ref, g_ref, k_ref, v_ref, do_ref, w_ref,
        dx_ref, dk_ref, dv_ref, dg_ref,
    ):
        queries = q_ref[...]
        grad = back_dot(do_ref[...], w_ref[...]).astype(BF)
        shares = head_shares(queries, k_ref[...], at_ref[0])
        grad_shares = back_dot(grad, v_ref[...])
        inner = jnp.sum(shares * grad_shares, axis=-1, keepdims=True)
        grad_scores = (shares * (grad_shares - inner)).astype(BF)
        key_grad = outer_sum(grad_scores, queries)
        value_grad = outer_sum(shares.astype(BF), grad)
        first = lax.rem(pl.program_id(0), groups) == 0

        @pl.when(first)
        def _():
            dk_ref[...] = key_grad
            dv_ref[...] = value_grad

        @pl.when(jnp.logical_not(first))
        def _():
            dk_ref[...] += key_grad
            dv_ref[...] += value_grad

        turned = turn(dot(grad_scores, k_ref[...]), c_ref[...], s_ref[...], back=True)
        normed, inverse = head_norm(x_ref[...])
        dg_ref[...] = jnp.sum(turned * normed, axis=0, keepdims=True)[None]
        dx_ref[...] = head_norm_back(normed, inverse, turned * g_ref[0:1, :]).astype(BF)

    shared = pl.BlockSpec((key_count, HD), lambda h: (0, h // groups))
    return pl.pallas_call(
        kernel,
        grid=(H,),
        in_specs=[
            pl.BlockSpec(memory_space=pltpu.SMEM), head, head, half, half, gain, keys, values,
            pl.BlockSpec((rows, width), lambda h: (0, 0)),
            pl.BlockSpec((HD, width), lambda h: (h, H * HD // width)),
        ],
        out_specs=[head, shared, shared, pl.BlockSpec((1, 1, HD), lambda h: (h, 0, 0))],
        out_shape=[
            jax.ShapeDtypeStruct((rows, H * HD), BF),
            jax.ShapeDtypeStruct((key_count, KVH * HD), F32),
            jax.ShapeDtypeStruct((key_count, KVH * HD), F32),
            jax.ShapeDtypeStruct((H, 1, HD), F32),
        ],
        cost_estimate=pl.CostEstimate(
            flops=10 * rows * H * HD * key_count,
            bytes_accessed=rows * H * HD * 10 + key_count * KVH * HD * 12,
            transcendentals=rows * H * key_count,
        ),
        name="attend_back",
    )(
        device.reshape(1), projected, queries, cosine, sine, gains, kv_seen, kv_seen, gradient, weights,
    )


def kv_prep(projected, cosine, sine, gains):
    rows = projected.shape[0]

    def kernel(x_ref, c_ref, s_ref, g_ref, out_ref):
        for head in range(2 * KVH):
            columns = slice(head * HD, (head + 1) * HD)
            normed, _ = head_norm(x_ref[:, columns])
            if head < KVH:
                normed = turn(normed * g_ref[1:2, :], c_ref[...], s_ref[...])
            out_ref[:, columns] = normed.astype(BF)

    return pl.pallas_call(
        kernel,
        out_shape=jax.ShapeDtypeStruct((rows, 2 * KVH * HD), BF),
        name="kv_prep",
    )(projected, cosine, sine, gains)


def kv_prep_back(projected, gradient, cosine, sine, gains):
    rows = projected.shape[0]

    def kernel(x_ref, d_ref, c_ref, s_ref, g_ref, dx_ref, dg_ref):
        gain_grad = jnp.zeros((1, HD), F32)
        for head in range(2 * KVH):
            columns = slice(head * HD, (head + 1) * HD)
            normed, inverse = head_norm(x_ref[:, columns])
            grad = d_ref[:, columns]
            if head < KVH:
                grad = turn(grad, c_ref[...], s_ref[...], back=True)
                gain_grad = gain_grad + jnp.sum(grad * normed, axis=0, keepdims=True)
                grad = grad * g_ref[1:2, :]
            dx_ref[:, columns] = head_norm_back(normed, inverse, grad).astype(BF)
        dg_ref[...] = gain_grad

    return pl.pallas_call(
        kernel,
        out_shape=[
            jax.ShapeDtypeStruct((rows, 2 * KVH * HD), BF),
            jax.ShapeDtypeStruct((1, HD), F32),
        ],
        name="kv_prep_back",
    )(projected, gradient, cosine, sine, gains)


class Place:
    def __init__(self):
        self.count = lax.axis_size("fsdp")
        self.copies = lax.axis_size("rep")
        self.device = lax.axis_index("fsdp")
        self.copy = lax.axis_index("rep")
        self.chips = self.count // 2
        self.chip = self.device // 2
        self.core = self.device % 2
        self.at_end = jnp.logical_or(self.chip == 0, self.chip == self.chips - 1)
        self.four = self.chips == 4

    def core_swap(self, array):
        return lax.ppermute(array, "fsdp", [(i, i ^ 1) for i in range(self.count)])

    def copy_swap(self, array, mask):
        return lax.ppermute(array, "rep", [(i, i ^ mask) for i in range(self.copies)])

    def chip_send(self, array, moves):
        pairs = [(2 * a + core, 2 * b + core) for a, b in moves for core in range(2)]
        return lax.ppermute(array, "fsdp", pairs)

    def by_core(self, mine, other):
        first = self.core == 0
        return jnp.where(first, mine, other), jnp.where(first, other, mine)

    def owner(self, j):
        return self.chip ^ j

    def chip_swap(self, array, mask):
        return self.chip_send(array, [(i, i ^ mask) for i in range(self.chips)])

    def spread_near(self, array):
        if not self.four:
            return [self.chip_swap(array, mask) for mask in range(1, self.chips)]
        return [self.chip_swap(array, 1), self.chip_swap(array, 2)]

    def spread_far(self, array, near):
        if not self.four:
            return []
        ends = self.chip_send(near[1], [(1, 0), (2, 3)])
        return [jnp.where(self.at_end, ends, self.chip_send(array, [(1, 2), (2, 1)]))]

    def spread(self, array):
        near = self.spread_near(array)
        return [array] + near + self.spread_far(array, near)

    def collect_near(self, parts):
        if not self.four:
            return [
                self.chip_swap(parts[mask].astype(BF), mask) for mask in range(1, self.chips)
            ]
        return self.collect_ends(parts) + self.collect_beside(parts)

    def collect_ends(self, parts):
        return [self.chip_send(parts[3].astype(BF), [(0, 1), (3, 2)])] if self.four else []

    def collect_beside(self, parts):
        if not self.four:
            return self.collect_near(parts)
        return [
            self.chip_swap(parts[1].astype(BF), 1),
            self.chip_send(parts[3].astype(BF), [(1, 2), (2, 1)]),
        ]

    def collect_far(self, parts, near):
        if not self.four:
            return near
        passed = parts[2].astype(F32) + near[0].astype(F32)
        return near[1:] + [self.chip_swap(passed.astype(BF), 2)]

    def collect_sum(self, own, arrived):
        total = own.astype(F32)
        for array in arrived:
            total = total + array.astype(F32)
        return total

    def in_order(self, pieces):
        block = jnp.concatenate(pieces, axis=0)
        rows, columns = block.shape
        bit = 1
        while bit < self.copies:
            split = block.reshape(self.copies // (2 * bit), 2, rows // self.copies * bit, columns)
            flipped = jnp.concatenate([split[:, 1:], split[:, :1]], axis=1)
            block = jnp.where((self.copy // bit) % 2 == 1, flipped, split).reshape(rows, columns)
            bit *= 2
        return block

    def swap_copies(self, array):
        if self.copies != 4:
            return [array] + [self.copy_swap(array, mask) for mask in range(1, self.copies)]
        half = array.shape[0] // 2
        first, second = self.copy_swap(array, 1), self.copy_swap(array, 2)
        last = [self.copy_swap(second[:half], 1), self.copy_swap(first[half:], 2)]
        return [array, first, second, jnp.concatenate(last, axis=0)]

    def lay_out(self, shard, shard_other, lane, lane_other, copies):
        rows, columns = shard.shape
        share = rows // copies
        chips, count = self.chips, self.count
        where = jnp.stack(
            [self.chip, self.core, self.copy if copies > 1 else 0]
            + [self.owner(j) for j in range(1, chips)]
        ).astype(jnp.int32)

        def kernel(at_ref, shard_ref, other_ref, lane_ref, lane_other_ref, whole_ref):
            core = at_ref[1]
            for side, (own, far) in enumerate(
                ((shard_ref, lane_ref), (other_ref, lane_other_ref))
            ):
                on = core if side == 0 else 1 - core
                base = pl.multiple_of((2 * at_ref[0] + on) * rows, rows)
                whole_ref[pl.ds(base, rows), :] = own[...]
                for j in range(1, chips):
                    base = (2 * at_ref[2 + j] + on) * rows
                    for mask in range(copies):
                        spot = pl.multiple_of(
                            base + jnp.bitwise_xor(at_ref[2], mask) * share, share
                        )
                        start = (mask * (chips - 1) + j - 1) * share
                        whole_ref[pl.ds(spot, share), :] = far[start : start + share, :]

        return pl.pallas_call(
            kernel,
            out_shape=jax.ShapeDtypeStruct((count * rows, columns), shard.dtype),
            in_specs=[pl.BlockSpec(memory_space=pltpu.SMEM)]
            + [pl.BlockSpec(memory_space=pltpu.VMEM)] * 4,
            out_specs=pl.BlockSpec(memory_space=pltpu.VMEM),
            name="lay_out",
        )(where, shard, shard_other, lane, lane_other)

    def own_share(self, shard):
        share = shard.shape[0] // self.copies
        return lax.dynamic_slice_in_dim(shard, self.copy * share, share, 0)

    def along_chain(self, own):
        return jnp.concatenate(self.spread(own)[1:], axis=0)

    def across_copies(self, slots):
        return jnp.concatenate(self.swap_copies(slots), axis=0)

    def lanes(self, whole):
        rows = whole.shape[0] // self.count
        split = whole.reshape(self.chips, 2, rows, whole.shape[1])
        return [
            lax.dynamic_index_in_dim(split, core, 1, keepdims=False).reshape(-1, whole.shape[1])
            for core in (self.core, 1 - self.core)
        ]

    def lane_columns(self, whole, core):
        columns = whole.shape[1] // self.count
        return jnp.concatenate(
            [
                lax.dynamic_slice_in_dim(whole, (2 * chip + core) * columns, columns, 1)
                for chip in range(self.chips)
            ],
            axis=1,
        )

    def lane_parts(self, mine, arrived):
        rows = arrived[0].shape[0] // self.chips

        def part(chip):
            sums = [
                lax.dynamic_slice_in_dim(own, chip * rows, rows, 0).astype(F32)
                + lax.dynamic_slice_in_dim(other, chip * rows, rows, 0).astype(F32)
                for own, other in zip(mine, arrived)
            ]
            return jnp.concatenate(sums, axis=-1).astype(BF)

        return [part(self.owner(j)) for j in range(self.chips)]

    def copies_sum(self, array):
        share = array.shape[0] // self.copies
        array = array.astype(BF)

        def take(mask):
            return lax.dynamic_slice_in_dim(array, (self.copy ^ mask) * share, share, 0)

        total = take(0).astype(F32)
        for mask in range(1, self.copies):
            total = total + self.copy_swap(take(mask), mask).astype(F32)
        return total.astype(BF)

    def copies_all(self, total):
        return self.in_order(
            [total] + [self.copy_swap(total, mask) for mask in range(1, self.copies)]
        )


def half_specs(units, width, tile):
    tiles = units // tile
    return [
        pl.BlockSpec((tile, width), lambda i: (jnp.minimum(i, tiles - 1), 0)),
        pl.BlockSpec((tile, width), lambda i: (jnp.maximum(i - tiles, 0), 0)),
    ]


def gelu_parts(value):
    inner = GELU_SCALE * (value + GELU_CUBIC * value * value * value)
    bent = jnp.tanh(inner)
    slope = GELU_SCALE * (1.0 + 3.0 * GELU_CUBIC * value * value)
    return 0.5 * value * (1.0 + bent), 0.5 * (1.0 + bent) + 0.5 * value * (1.0 - bent * bent) * slope


def stack_rows(refs):
    values = [ref[...] for ref in refs]
    return values[0] if len(values) == 1 else jnp.concatenate(values, axis=0)


def ffn_block(blocks, gates, ups, downs, sum_type):
    (piece, width), count = blocks[0].shape, len(blocks)
    rows = piece * count
    units = gates[0].shape[0]
    tile = min(units, 512)
    tiles = units // tile

    def kernel(*refs):
        x_refs, (g0, g1, u0, u1, d0, d1) = refs[:count], refs[count : count + 6]
        sum_refs = refs[count + 6 : 2 * count + 6]
        hid_ref, gate_ref, up_ref, total = refs[2 * count + 6 :]
        step = pl.program_id(0)

        def work(g_ref, u_ref, d_ref):
            x = stack_rows(x_refs)
            gate, up = back_dot(x, g_ref[...]), back_dot(x, u_ref[...])
            bent = jnp.tanh(GELU_SCALE * (gate + GELU_CUBIC * gate * gate * gate))
            hidden = (0.5 * gate * (1.0 + bent) * up).astype(BF)
            hid_ref[...] = hidden
            gate_ref[...] = gate.astype(BF)
            up_ref[...] = up.astype(BF)
            return dot(hidden, d_ref[...])

        @pl.when(step == 0)
        def _():
            total[...] = work(g0, u0, d0)

        @pl.when(jnp.logical_and(step > 0, step < tiles))
        def _():
            total[...] += work(g0, u0, d0)

        @pl.when(step >= tiles)
        def _():
            total[...] += work(g1, u1, d1)

        @pl.when(step == 2 * tiles - 1)
        def _():
            for i, sum_ref in enumerate(sum_refs):
                sum_ref[...] = total[i * piece : (i + 1) * piece, :].astype(sum_type)

    whole = pl.BlockSpec((piece, width), lambda i: (0, 0))
    part = pl.BlockSpec((rows, tile), lambda i: (0, i))
    *sums, hidden, gate, up = pl.pallas_call(
        kernel,
        grid=(2 * tiles,),
        in_specs=[whole] * count + half_specs(units, width, tile) * 3,
        out_specs=[whole] * count + [part] * 3,
        out_shape=[jax.ShapeDtypeStruct((piece, width), sum_type)] * count
        + [jax.ShapeDtypeStruct((rows, 2 * units), BF)] * 3,
        scratch_shapes=[pltpu.VMEM((rows, width), F32)],
        cost_estimate=pl.CostEstimate(
            flops=12 * rows * width * units,
            bytes_accessed=12 * units * width + 12 * rows * units + 6 * rows * width,
            transcendentals=2 * rows * units,
        ),
        name="ffn_block",
    )(*blocks, *gates, *ups, *downs)
    return sums, hidden, gate, up


def ffn_block_back(grads, gate, up, gates, ups, downs, sum_type):
    (piece, width), count = grads[0].shape, len(grads)
    rows = piece * count
    units = gates[0].shape[0]
    tile = min(units, 512)
    tiles = units // tile

    def kernel(*refs):
        x_refs, (gate_ref, up_ref) = refs[:count], refs[count : count + 2]
        g0, g1, u0, u1, d0, d1 = refs[count + 2 : count + 8]
        sum_refs = refs[count + 8 : 2 * count + 8]
        dg_ref, du_ref, total = refs[2 * count + 8 :]
        step = pl.program_id(0)

        def work(g_ref, u_ref, d_ref):
            value, slope = gelu_parts(gate_ref[...].astype(F32))
            hidden = back_dot(stack_rows(x_refs), d_ref[...])
            grad_gate = (hidden * up_ref[...].astype(F32) * slope).astype(BF)
            grad_up = (hidden * value).astype(BF)
            dg_ref[...] = grad_gate
            du_ref[...] = grad_up
            return dot(grad_gate, g_ref[...]) + dot(grad_up, u_ref[...])

        @pl.when(step == 0)
        def _():
            total[...] = work(g0, u0, d0)

        @pl.when(jnp.logical_and(step > 0, step < tiles))
        def _():
            total[...] += work(g0, u0, d0)

        @pl.when(step >= tiles)
        def _():
            total[...] += work(g1, u1, d1)

        @pl.when(step == 2 * tiles - 1)
        def _():
            for i, sum_ref in enumerate(sum_refs):
                sum_ref[...] = total[i * piece : (i + 1) * piece, :].astype(sum_type)

    whole = pl.BlockSpec((piece, width), lambda i: (0, 0))
    part = pl.BlockSpec((rows, tile), lambda i: (0, i))
    *sums, grad_gate, grad_up = pl.pallas_call(
        kernel,
        grid=(2 * tiles,),
        in_specs=[whole] * count + [part, part] + half_specs(units, width, tile) * 3,
        out_specs=[whole] * count + [part] * 2,
        out_shape=[jax.ShapeDtypeStruct((piece, width), sum_type)] * count
        + [jax.ShapeDtypeStruct((rows, 2 * units), BF)] * 2,
        scratch_shapes=[pltpu.VMEM((rows, width), F32)],
        cost_estimate=pl.CostEstimate(
            flops=12 * rows * width * units,
            bytes_accessed=12 * units * width + 16 * rows * units + 6 * rows * width,
            transcendentals=2 * rows * units,
        ),
        name="ffn_block_back",
    )(*grads, gate, up, *gates, *ups, *downs)
    return sums, grad_gate, grad_up


def outer_blocks(lefts, rights, start, columns, added=None, whole=None, place=0, places=1):
    width = rights[0].shape[1]
    tile = min(columns, 256)
    n_left, tiles = len(lefts), columns // tile
    n_both = n_left + len(rights)

    def kernel(*refs):
        out_ref = refs[-1]
        total = outer_sum(stack_rows(refs[:n_left]), stack_rows(refs[n_left:n_both]))
        if added is not None:
            total = total + refs[n_both][...].astype(F32)
        out_ref[...] = total.astype(BF)

    rows = sum(left.shape[0] for left in lefts)
    operands = [*lefts, *rights]
    specs = [pl.BlockSpec((left.shape[0], tile), lambda i: (0, i + start // tile)) for left in lefts]
    specs += [pl.BlockSpec(right.shape, lambda i: (0, 0)) for right in rights]
    if added is not None:
        operands.append(added)
        specs.append(pl.BlockSpec((tile, width), lambda i: (i, 0)))
    aliases = {}
    if whole is not None:
        aliases = {len(operands): 0}
        operands.append(whole)
        specs.append(pl.BlockSpec(memory_space=pl.ANY))
    return pl.pallas_call(
        kernel,
        grid=(tiles,),
        in_specs=specs,
        out_specs=pl.BlockSpec((tile, width), lambda i: (i + place * tiles, 0)),
        out_shape=jax.ShapeDtypeStruct((places * columns, width), BF),
        input_output_aliases=aliases,
        cost_estimate=pl.CostEstimate(
            flops=2 * rows * columns * width,
            bytes_accessed=2 * rows * (columns + width) + 4 * columns * width,
            transcendentals=0,
        ),
        name="outer_blocks",
    )(*operands)


def split_pair(pair):
    units, _, width = pair.shape
    rows = min(units, 128)

    def kernel(pair_ref, first_ref, second_ref):
        first_ref[...] = pair_ref[:, 0, :].astype(BF)
        second_ref[...] = pair_ref[:, 1, :].astype(BF)

    flat = pl.BlockSpec((rows, width), lambda i: (i, 0))
    return pl.pallas_call(
        kernel,
        grid=(units // rows,),
        in_specs=[pl.BlockSpec((rows, 2, width), lambda i: (i, 0, 0))],
        out_specs=[flat, flat],
        out_shape=[jax.ShapeDtypeStruct((units, width), BF)] * 2,
        cost_estimate=pl.CostEstimate(
            flops=0, bytes_accessed=units * width * 12, transcendentals=0
        ),
        name="split_pair",
    )(pair)


def join_pair(stacked, units):
    width = stacked.shape[1]
    rows = min(units, 128)
    tiles = units // rows

    def kernel(first_ref, second_ref, pair_ref):
        pair_ref[:, 0, :] = first_ref[...].astype(F32)
        pair_ref[:, 1, :] = second_ref[...].astype(F32)

    return pl.pallas_call(
        kernel,
        grid=(tiles,),
        in_specs=[
            pl.BlockSpec((rows, width), lambda i: (i, 0)),
            pl.BlockSpec((rows, width), lambda i: (i + tiles, 0)),
        ],
        out_specs=pl.BlockSpec((rows, 2, width), lambda i: (i, 0, 0)),
        out_shape=jax.ShapeDtypeStruct((units, 2, width), F32),
        cost_estimate=pl.CostEstimate(
            flops=0, bytes_accessed=units * width * 12, transcendentals=0
        ),
        name="join_pair",
    )(stacked, stacked)


def tie(*values):
    return lax.optimization_barrier(values)


def body(
    tokens,
    layer_input,
    cotangent,
    norm_gains,
    qk_gains,
    w_qkv,
    w_out,
    laurel_left,
    laurel_right,
    w_gate_up,
    w_down,
    pli_gate,
    pli_proj,
):
    at = Place()
    device = at.device
    rows_dev, width = tokens.shape
    shard = w_qkv.shape[0]
    prompt_len = PROMPT_DEVS * rows_dev
    q_cols = H * HD
    lr, pd = laurel_left.shape[1], pli_gate.shape[1]
    n_gain, n_qk = norm_gains.size, qk_gains.size

    def pack_gains(norm_part, qk_part):
        flat = jnp.concatenate([norm_part.reshape(-1), qk_part.reshape(-1)]).astype(BF)
        flat = jnp.pad(flat, (0, shard * 128 - flat.size))
        return flat.reshape(shard, 128)

    kv_pack = jnp.concatenate(
        [w_qkv[:, q_cols:].astype(BF), pack_gains(norm_gains, qk_gains)], axis=1
    )
    def gather_all(array):
        return lax.all_gather(at.own_share(array), ("fsdp", "rep"), axis=0, tiled=True)

    main_all = gather_all(
        jnp.concatenate(
            [
                w_qkv[:, :q_cols].astype(BF),
                w_out.astype(BF),
                laurel_left.astype(BF),
                laurel_right.astype(BF).reshape(shard, lr),
            ],
            axis=1,
        )
    )
    q_all = main_all[:, :q_cols]
    out_all = main_all[:, q_cols : q_cols + width]
    left_all = main_all[:, q_cols + width : q_cols + width + lr]
    right_all = main_all[:, q_cols + width + lr :].reshape(lr, width)
    pli_pack_all = gather_all(
        jnp.concatenate([pli_gate.astype(BF), pli_proj.astype(BF).reshape(shard, pd)], axis=1)
    )
    w_gate, w_up = split_pair(w_gate_up)
    w_down_bf = w_down.astype(BF)
    own_wide = (w_gate, w_up, w_down_bf)
    kv_twin = at.core_swap(kv_pack)
    kv_near = at.spread_near(kv_pack)
    kv_near, kv_twin, own_wide = tie(kv_near, kv_twin, own_wide)
    kv_far = at.spread_far(kv_pack, kv_near)
    their_wide = [at.core_swap(own) for own in own_wide]
    kv_lane = jnp.concatenate(kv_near + kv_far, axis=0)
    kv_all = at.lay_out(kv_pack, kv_twin, kv_lane, at.core_swap(kv_lane), 1)
    kv_weight = kv_all[:, : 2 * KVH * HD]
    gain_rows_all = kv_all[:, 2 * KVH * HD :].reshape(at.count, -1)[:, : n_gain + n_qk]
    gains = jnp.moveaxis(
        gain_rows_all[:, :n_gain].reshape(at.count, norm_gains.shape[0], -1), 0, 1
    ).reshape(norm_gains.shape[0], -1).astype(F32)
    qk_gain = jnp.moveaxis(
        gain_rows_all[:, n_gain:].reshape(at.count, qk_gains.shape[0], -1), 0, 1
    ).reshape(qk_gains.shape[0], -1).astype(F32)
    inputs = tokens.astype(F32)
    extra_input = layer_input.astype(F32)

    def input_norm(tensor, gain_rows):
        return rms_norm(tensor) * gain_rows[0]

    normed, input_pull = jax.vjp(input_norm, inputs, gains)
    normed_bf = normed.astype(BF)
    local_rows = jnp.arange(rows_dev, dtype=jnp.int32)
    places = jnp.where(
        device < PROMPT_DEVS, device * rows_dev + local_rows, prompt_len + local_rows % CONT_LEN
    )

    half = HD // 2
    frequency = THETA_BASE ** (-(jnp.arange(half, dtype=F32) * 2.0 / HD))
    angles = places.astype(F32)[:, None] * frequency
    cosine, sine = jnp.cos(angles), jnp.sin(angles)
    kv_proj = dot(normed_bf, kv_weight)
    kv_own = kv_prep(kv_proj, cosine, sine, qk_gain)

    prompt_chips = PROMPT_DEVS // 2
    if at.four:
        arrived = at.chip_send(kv_own, [(0, 2), (1, 3)])
        even = jnp.where(at.chip < prompt_chips, kv_own, arrived)
        odd = at.chip_swap(even, 1)
        kv_lane = [jnp.where(at.chip % 2 == i, even, odd) for i in range(2)]
    else:
        blocks = [kv_own] + [
            at.chip_send(kv_own, [(i, (i - j) % at.chips) for i in range(prompt_chips)])
            for j in range(1, at.chips)
        ]
        kv_lane = []
        for block in range(prompt_chips):
            seen = kv_own
            for j in range(1, at.chips):
                seen = jnp.where((at.chip + j) % at.chips == block, blocks[j], seen)
            kv_lane.append(seen)
    q_proj = dot(normed_bf, q_all)
    laurel_mid = dot(normed_bf, left_all).astype(BF)
    laurel_out = dot(laurel_mid, right_all)
    kv_lane, own_wide, their_wide, q_proj, laurel_out = tie(
        jnp.stack(kv_lane), own_wide, their_wide, q_proj, laurel_out
    )
    halves = list(zip(own_wide, their_wide))
    (gate_halves, up_halves, down_halves) = halves

    kv_other = at.core_swap(kv_lane)
    kv_pairs = [row for i in range(prompt_chips) for row in at.by_core(kv_lane[i], kv_other[i])]
    kv_seen = jnp.concatenate(kv_pairs + [kv_own], axis=0)
    queries_bf, attended_bf = attend(q_proj, cosine, sine, qk_gain, kv_seen, device)
    pgate_all = pli_pack_all[:, :pd]
    pproj_all = pli_pack_all[:, pd:].reshape(pd, width)
    attn_proj = dot(attended_bf, out_all)

    def middle(inputs, normed, attn_proj, laurel_out, gain_rows):
        first_sum = inputs + rms_norm(attn_proj) * gain_rows[1]
        laurel_sum = normed + rms_norm(laurel_out) * gain_rows[2]
        stream = (first_sum + laurel_sum) * HALF_ROOT
        return (stream, rms_norm(stream) * gain_rows[3])

    (stream, ffn_in), middle_pull = jax.vjp(middle, inputs, normed, attn_proj, laurel_out, gains)

    piece = rows_dev // CHUNKS
    units = w_down.shape[0]

    def staged(rows, work, extra=()):
        near = at.spread_near(rows)
        first = work(0, [rows], F32)
        near, first, extra = tie(near, first, extra)
        far = at.spread_far(rows, near)
        pairs = [near[i : i + 2] for i in range(0, len(near), 2)]
        second = [work(j + 1, blocks, BF) for j, blocks in enumerate(pairs)]
        far, second = tie(far, second)
        parts = [part for sums, *_ in second for part in sums]
        back = [at.chip_swap(part, j + 1) for j, part in enumerate(parts)]
        done = [first, *second]
        last = None
        if far:
            third = work(len(done), far, BF)
            first_back, third = tie(back[0], third)
            back[0] = first_back
            done.append(third)
            last = third[0][0]
        return first[0][0], back, last, [kept for _, kept in done], extra

    def ffn_forward(rows, extra):
        def work(j, blocks, sum_type):
            sums, *kept = ffn_block(blocks, gate_halves, up_halves, down_halves, sum_type)
            return sums, (blocks, *kept)

        own, back, last, kept, extra = staged(rows, work, extra)
        if last is not None:
            back = back + [at.chip_swap(last, at.chips - 1)]
        return at.collect_sum(own, back), kept, extra

    def ffn_backward(rows, kept):
        def work(j, grads, sum_type):
            blocks, hidden, gate, up = kept[j]
            sums, grad_gate, grad_up = ffn_block_back(
                grads, gate, up, gate_halves, up_halves, down_halves, sum_type
            )
            return sums, (blocks, hidden, grads, grad_gate, grad_up)

        return staged(rows, work)

    def tail_norm(stream, ffn_out, gain_rows):
        return stream + rms_norm(ffn_out) * gain_rows[4]

    def pli_mix(pli_pre, extra_input):
        return jax.nn.gelu(pli_pre, approximate=True) * extra_input

    def final_norm(after_ffn, pli_out, gain_rows):
        return after_ffn + rms_norm(pli_out) * gain_rows[5]

    cuts = [slice(i * piece, (i + 1) * piece) for i in range(CHUNKS)]
    core, other_core = at.core, 1 - at.core
    lanes = [
        at.lane_columns(rows, side) for rows in (attended_bf, normed_bf) for side in (core, other_core)
    ]
    forwards = []
    for cut in cuts:
        ffn_out, kept, lanes = ffn_forward(ffn_in[cut].astype(BF), lanes)
        forwards.append((ffn_out, kept))
    attended_mine, attended_other, normed_mine, normed_other = lanes
    gain_total = 0.0
    results, extras, streams, ins, all_grads = [], [], [], [], []
    pli_rows = []
    for cut, (ffn_out, kept) in zip(cuts, forwards):
        after_ffn, tail_pull = jax.vjp(tail_norm, stream[cut], ffn_out, gains)
        after_bf = after_ffn.astype(BF)
        pli_mid, pli_pull = jax.vjp(pli_mix, dot(after_bf, pgate_all), extra_input[cut])
        pli_mid_bf = pli_mid.astype(BF)
        result, final_pull = jax.vjp(final_norm, after_ffn, dot(pli_mid_bf, pproj_all), gains)
        grad_after, grad_pli_out, gain_final = final_pull(cotangent[cut].astype(F32))
        grad_pli_out_bf = grad_pli_out.astype(BF)
        grad_pli_pre, grad_extra = pli_pull(back_dot(grad_pli_out_bf, pproj_all))
        grad_pli_pre_bf = grad_pli_pre.astype(BF)
        grad_after = grad_after + back_dot(grad_pli_pre_bf, pgate_all)
        grad_stream, grad_ffn_out, gain_tail = tail_pull(grad_after)
        own, back, last, grads, _ = ffn_backward(grad_ffn_out.astype(BF), kept)
        gain_total = gain_total + gain_final + gain_tail
        results.append(result.astype(BF))
        extras.append(grad_extra)
        streams.append(grad_stream)
        ins.append((own, back, last))
        all_grads.append(grads)
        pli_rows.append((pli_mid_bf, grad_pli_out_bf, after_bf, grad_pli_pre_bf))

    kept = [[group[i] for grads in all_grads for group in grads] for i in range(5)]
    hiddens, gates, ups = kept[1], kept[3], kept[4]
    ins_blocks, outs_grad = [[block for blocks in kept[i] for block in blocks] for i in (0, 2)]
    lasts = [last for _, _, last in ins if last is not None]
    lasts, pli_rows, hiddens, gates, ups = tie(lasts, pli_rows, hiddens, gates, ups)
    pairs = [(hiddens, outs_grad), (gates, ins_blocks), (ups, ins_blocks)]
    theirs = [
        outer_blocks(lefts, rights, units, units) for lefts, rights in pairs
    ]
    mids, pli_outs, afters, pres = [jnp.concatenate(rows, axis=0) for rows in zip(*pli_rows)]
    grad_pproj = outer_blocks([mids], [pli_outs], 0, pd)
    grad_pgate = outer_blocks([afters], [pres], 0, width)
    lasts = [at.chip_swap(last, at.chips - 1) for last in lasts]
    backs = [back for _, back, _ in ins]
    backs, lasts, theirs, grad_pproj, grad_pgate = tie(
        backs, lasts, theirs, grad_pproj, grad_pgate
    )
    grad_pproj = grad_pproj.reshape(-1, pd)
    ends = [[last] for last in lasts] or [[]] * len(ins)
    ins = [at.collect_sum(own, back + end) for (own, _, _), back, end in zip(ins, backs, ends)]

    grad_inputs, grad_normed, grad_attn_proj, grad_laurel_out, gain_middle = middle_pull(
        (jnp.concatenate(streams, axis=0), jnp.concatenate(ins, axis=0))
    )
    grad_attn_bf = grad_attn_proj.astype(BF)
    out_leaving = at.core_swap(outer_sum(attended_other, grad_attn_bf).astype(BF))
    out_mine = outer_sum(attended_mine, grad_attn_bf).astype(BF)
    grad_laurel_bf = grad_laurel_out.astype(BF)
    grad_right_w = outer_sum(laurel_mid, grad_laurel_bf).astype(BF).reshape(-1, lr)
    grad_mid_bf = back_dot(grad_laurel_bf, right_all).astype(BF)
    grad_left_w = outer_sum(normed_bf, grad_mid_bf).astype(BF)
    small_mine, small_leaving = at.lanes(
        jnp.concatenate([grad_left_w, grad_right_w, grad_pgate, grad_pproj], axis=1)
    )
    small_leaving = at.core_swap(small_leaving)
    their_down = at.core_swap(theirs[0])
    out_leaving, small_leaving, out_mine, small_mine, theirs, their_down, grad_attn_bf = tie(
        out_leaving, small_leaving, out_mine, small_mine, theirs, their_down, grad_attn_bf
    )
    out_parts = at.lane_parts([out_mine, small_mine], [out_leaving, small_leaving])
    out_ends = at.collect_ends(out_parts)
    theirs = [at.core_swap(their) for their in theirs[1:]]
    grad_q_bf, key_grad, value_grad, q_gain_rows = attend_back(
        q_proj, queries_bf, cosine, sine, qk_gain, kv_seen, grad_attn_bf, main_all, device
    )
    down_w = outer_blocks(*pairs[0], 0, units, their_down)
    out_ends, theirs, out_parts, grad_q_bf, key_grad, value_grad, down_w = tie(
        out_ends, theirs, out_parts, grad_q_bf, key_grad, value_grad, down_w
    )
    down_part = lax.psum_scatter(down_w, "rep", scatter_dimension=0, tiled=True)
    out_beside = at.collect_beside(out_parts)
    out_near = out_ends + out_beside
    wide_w = None
    for place, ((lefts, rights), their) in enumerate(zip(pairs[1:], theirs)):
        wide_w = outer_blocks(lefts, rights, 0, units, their, wide_w, place, 2)

    def kv_rows(first, core):
        begin = (2 * first + core) * rows_dev
        return jnp.concatenate(
            [
                lax.dynamic_slice_in_dim(grad, begin, rows_dev, 0).astype(BF)
                for grad in (key_grad, value_grad)
            ],
            axis=1,
        )

    kv_other = at.core_swap(
        jnp.stack([kv_rows(chip, other_core) for chip in range(prompt_chips)])
    )

    def kv_part(chip):
        index = jnp.clip(chip, 0, prompt_chips - 1)
        theirs = lax.dynamic_index_in_dim(kv_other, index, 0, keepdims=False)
        return kv_rows(index, core).astype(F32) + theirs.astype(F32)

    offsets = [0, 1] if at.four else range(at.chips)
    kv_parts = [
        kv_part((at.chip + j) % 2 if at.four else (at.chip + j) % at.chips) for j in offsets
    ]
    q_other_w = outer_blocks([normed_other], [grad_q_bf], 0, width // 2)
    q_mine = outer_blocks([normed_mine], [grad_q_bf], 0, width // 2)
    kv_parts, out_near, wide_w, q_other_w, q_mine = tie(
        kv_parts, out_near, wide_w, q_other_w, q_mine
    )
    wide_part = lax.psum_scatter(wide_w, "rep", scatter_dimension=0, tiled=True)
    if at.four:
        pair_sum = kv_parts[0] + at.chip_swap(kv_parts[1].astype(BF), 1).astype(F32)
        pair_sum, out_near = tie(pair_sum, out_near)
        prompt_parts = [at.chip_send(pair_sum.astype(BF), [(2, 0), (3, 1)])]
    else:
        pair_sum = kv_parts[0]
        prompt_parts = [
            at.chip_send(
                kv_parts[j].astype(BF), [((i - j) % at.chips, i) for i in range(prompt_chips)]
            )
            for j in range(1, at.chips)
        ]
    q_leaving = at.core_swap(q_other_w)
    out_far = at.collect_far(out_parts, out_near)
    prompt_parts, pair_sum, q_leaving, wide_part = tie(
        prompt_parts, pair_sum, q_leaving, wide_part
    )
    wide_sum = lax.all_gather(wide_part, "rep", axis=0, tiled=True)
    q_parts = at.lane_parts([q_mine], [q_leaving])
    q_near = at.collect_near(q_parts)
    prompt_sum = pair_sum
    for sent in prompt_parts:
        prompt_sum = prompt_sum + sent.astype(F32)
    kv_sum = jnp.where(
        device < PROMPT_DEVS,
        prompt_sum,
        jnp.concatenate([key_grad[prompt_len:], value_grad[prompt_len:]], axis=1),
    )
    grad_kv_bf, k_gain_row = kv_prep_back(kv_proj, kv_sum, cosine, sine, qk_gain)
    kv_other_w = outer_sum(normed_other, grad_kv_bf).astype(BF)
    kv_mine = outer_sum(normed_mine, grad_kv_bf).astype(BF)
    grad_normed = grad_normed + back_dot(grad_mid_bf, left_all)
    grad_normed = grad_normed + back_dot(grad_q_bf, q_all) + back_dot(grad_kv_bf, kv_weight)
    grad_first, gain_input = input_pull(grad_normed)
    grad_tokens = grad_inputs + grad_first
    gain_total = gain_total + gain_middle + gain_input
    qk_total = jnp.concatenate([jnp.sum(q_gain_rows, axis=0), k_gain_row], axis=0)

    def by_owner(array):
        return jnp.moveaxis(array.reshape(array.shape[0], at.count, -1), 1, 0).reshape(at.count, -1)

    gain_pack = jnp.concatenate([by_owner(gain_total), by_owner(qk_total)], axis=1).astype(BF)
    gain_pack = jnp.pad(gain_pack, ((0, 0), (0, shard * 128 - gain_pack.shape[1])))
    gain_mine, gain_leaving = at.lanes(gain_pack.reshape(-1, 128))
    out_far, q_near, kv_other_w, kv_mine, gain_mine, gain_leaving, grad_tokens, down_part = tie(
        out_far, q_near, kv_other_w, kv_mine, gain_mine, gain_leaving, grad_tokens, down_part
    )
    down_sum = lax.all_gather(down_part, "rep", axis=0, tiled=True)
    out_ready = at.collect_sum(out_parts[0], out_far).astype(BF)
    q_far = at.collect_far(q_parts, q_near)
    kv_leaving, gain_leaving, out_ready = tie(
        at.core_swap(kv_other_w), at.core_swap(gain_leaving), out_ready
    )
    kv_w_parts = at.lane_parts([kv_mine, gain_mine], [kv_leaving, gain_leaving])
    kv_near = at.collect_near(kv_w_parts)
    out_total = at.copies_sum(out_ready)
    q_far, kv_near, out_total = tie(q_far, kv_near, out_total)
    kv_far = at.collect_far(kv_w_parts, kv_near)
    q_total = at.copies_sum(at.collect_sum(q_parts[0], q_far))
    out_sum = at.copies_all(out_total)
    kv_far, q_total, out_sum = tie(kv_far, q_total, out_sum)
    kv_total = at.copies_sum(at.collect_sum(kv_w_parts[0], kv_far))
    q_sum = at.copies_all(q_total)
    kv_total, q_sum = tie(kv_total, q_sum)
    grad_gate_up, grad_down = join_pair(wide_sum, units), down_sum.astype(F32)
    kv_sum_w = at.copies_all(kv_total)
    gain_out = kv_sum_w[:, 2 * KVH * HD :].reshape(-1)
    return (
        jnp.concatenate(results, axis=0),
        grad_tokens,
        jnp.concatenate(extras, axis=0),
        gain_out[:n_gain].reshape(norm_gains.shape).astype(F32),
        gain_out[n_gain : n_gain + n_qk].reshape(qk_gains.shape).astype(F32),
        jnp.concatenate([q_sum, kv_sum_w[:, : 2 * KVH * HD]], axis=1).astype(F32),
        out_sum[:, :width].astype(F32),
        out_sum[:, width : width + lr].astype(F32),
        out_sum[:, width + lr : width + 2 * lr].reshape(laurel_right.shape).astype(F32),
        grad_gate_up,
        grad_down,
        out_sum[:, width + 2 * lr : width + 2 * lr + pd].astype(F32),
        out_sum[:, width + 2 * lr + pd :].reshape(pli_proj.shape).astype(F32),
    )


def solution(mesh):
    placed = (
        P(("rep", "fsdp"), None),
        P(("rep", "fsdp"), None),
        P(("rep", "fsdp"), None),
        P(None, "fsdp"),
        P(None, "fsdp"),
        P("fsdp", None),
        P("fsdp", None),
        P("fsdp", None),
        P("fsdp", None),
        P("fsdp", None, None),
        P("fsdp", None),
        P("fsdp", None),
        P("fsdp", None),
    )
    return jax.shard_map(
        body,
        mesh=mesh,
        in_specs=placed,
        out_specs=(
            P(("rep", "fsdp"), None),
            P(("rep", "fsdp"), None),
            P(("rep", "fsdp"), None),
            P(None, "fsdp"),
            P(None, "fsdp"),
            P("fsdp", None),
            P("fsdp", None),
            P("fsdp", None),
            P("fsdp", None),
            P("fsdp", None, None),
            P("fsdp", None),
            P("fsdp", None),
            P("fsdp", None),
        ),
        check_vma=False,
    )
```
